32 devices in a mesh: tm: 32 (over z, y, x, core).
Axes of the slice: x: 2, y: 2, z: 4, core: 2. Of those that a mesh axis runs over, the one named last changes fastest.
Arguments:
- initial: float32 [2, 64, 64], replicated, may hold values from 0 to 0.6
- coarse_guess: float32 [32, 2, 64, 64], P('tm'), may hold values from 0 to 0.6
- feed_rate: float32 [64, 64], replicated, may hold values from 0.02 to 0.08
- kill_rate: float32 [64, 64], replicated, may hold values from 0.03 to 0.07
Outputs:
- trajectory: float32 [128, 2, 64, 64], P('tm')
- c_residual: float32 [32, 2, 64, 64], P('tm')
- group_coarse: float32 [32, 2, 64, 64], P('tm')
- level_defect: float32 [32, 2, 64, 64], P('tm')
The draws below stay inside these ranges and needn't reach their ends.
All inputs are finite; a program needn't handle non-finite values.
Results may differ from the reference program's by a relative error of at most 0.0004.
Values sent between devices are 32-bit elements; how exact they have to be, the bound alone decides.
A program may use at most 64 MiB of HBM per device.

```python
import math
import jax
import jax.numpy as jnp
from jax import lax

STEPS_DEV = 4
GX = 64
GY = 64
GROUP = 16
N_TM = 32


def steps_of(stream_key, dims, shards, smallest, top_value):
    def one(position, parts):
        heights = jax.random.uniform(jax.random.fold_in(jax.random.fold_in(stream_key, 6), position), (parts,), jnp.float32, smallest / len(shards), top_value / len(shards))
        return jnp.repeat(jnp.exp(heights), dims[position] // parts).reshape((-1,) + (1,) * (len(dims) - position - 1))

    level = one(*shards[0])
    for cut in shards[1:]:
        level = level * one(*cut)
    return level


def setup_inputs(seed: int = 0) -> dict:
    key_list = jax.random.split(jax.random.key(seed), 5)
    return {
        "initial": jnp.clip(jax.random.uniform(key_list[0], (2, GX, GY), jnp.float32, 0.0, 0.6), 0.0, 0.6),
        "coarse_guess": jnp.clip(0.6 * jax.random.uniform(key_list[1], (N_TM, 2, GX, GY), jnp.float32) ** steps_of(key_list[1], (N_TM, 2, GX, GY), ((0, 32),), -0.2, 0.2), 0.0, 0.6),
        "feed_rate": jnp.clip(jnp.exp(jax.random.uniform(key_list[2], (GX, GY), jnp.float32, math.log(0.02), math.log(0.08))), 0.02, 0.08),
        "kill_rate": jnp.clip(jnp.exp(jax.random.uniform(key_list[3], (GX, GY), jnp.float32, math.log(0.03), math.log(0.07))), 0.03, 0.07),
    }


diffusion = (0.2, 0.1)
interval_time = 0.03125
highest = lax.Precision.HIGHEST

def cosine_basis(length):
    positions = jnp.arange(length, dtype=jnp.float32)
    angles = jnp.pi * (positions[:, None] + 0.5) * positions[None, :] / length
    weight = jnp.where(positions == 0, jnp.sqrt(1.0 / length), jnp.sqrt(2.0 / length))
    return jnp.cos(angles) * weight[None, :]

def eigen_values(length):
    positions = jnp.arange(length, dtype=jnp.float32)
    return -4.0 * jnp.sin(jnp.pi * positions / (2.0 * length)) ** 2

def make_tables(rows_first, rows_second):
    spectrum = eigen_values(rows_first)[:, None] + eigen_values(rows_second)[None, :]
    return (cosine_basis(rows_first), cosine_basis(rows_second), spectrum)

def advance(fields, feed_rate, kill_rate, time_step, tables):
    basis_rows, basis_cols, spectrum = tables
    substrate = fields[..., 0, :, :]
    catalyst = fields[..., 1, :, :]
    uptake = substrate * catalyst * catalyst
    substrate_new = substrate + time_step * (feed_rate * (1.0 - substrate) - uptake)
    catalyst_new = catalyst + time_step * (uptake - (feed_rate + kill_rate) * catalyst)
    reacted = jnp.stack([substrate_new, catalyst_new], axis=-3)
    spectral = jnp.matmul(jnp.matmul(basis_rows.T, reacted, precision=highest), basis_cols, precision=highest)
    diff_rates = jnp.array(diffusion, dtype=jnp.float32)
    spectral = spectral / (1.0 - time_step * diff_rates[:, None, None] * spectrum)
    return jnp.matmul(jnp.matmul(basis_rows, spectral, precision=highest), basis_cols.T, precision=highest)

def march(start_state, feed_rate, kill_rate, time_step, tables, count_steps):

    def turn(fields, unused):
        fields = advance(fields, feed_rate, kill_rate, time_step, tables)
        return (fields, fields)
    finished, visited = lax.scan(turn, start_state, None, length=count_steps)
    return (finished, visited)

def reference(initial, coarse_guess, feed_rate, kill_rate):
    tables = make_tables(initial.shape[1], initial.shape[2])
    fine_step = interval_time / STEPS_DEV
    level_step = interval_time
    coarse_step = interval_time * GROUP
    groups = N_TM // GROUP
    shape = initial.shape

    def before(values):
        return jnp.concatenate([initial[None], values[:-1]], axis=0)

    def evolve(fields, time_step):
        return advance(fields, feed_rate, kill_rate, time_step, tables)
    relaxed, unused = march(before(coarse_guess), feed_rate, kill_rate, fine_step, tables, STEPS_DEV)
    shifted = before(relaxed)
    arrived, unused = march(shifted, feed_rate, kill_rate, fine_step, tables, STEPS_DEV)
    c_residual = arrived - relaxed
    level_rhs = arrived - evolve(shifted, level_step)
    grouped_terms = level_rhs.reshape((groups, GROUP) + shape)
    group_start = jnp.concatenate([initial[None], relaxed.reshape((groups, GROUP) + shape)[:, -1][:-1]], axis=0)

    def level_turn(fields, right_side):
        fields = evolve(fields, level_step) + right_side
        return (fields, fields)
    inner_terms = jnp.moveaxis(grouped_terms[:, :-1], 1, 0)
    last_point, unused = lax.scan(level_turn, group_start, inner_terms)
    closing = evolve(last_point, level_step) + grouped_terms[:, -1]
    coarse_rhs = closing - evolve(group_start, coarse_step)

    def coarse_turn(fields, right_side):
        fields = evolve(fields, coarse_step) + right_side
        return (fields, fields)
    unused, coarse_values = lax.scan(coarse_turn, initial, coarse_rhs)
    group_coarse = jnp.repeat(coarse_values, GROUP, axis=0)
    fresh_start = jnp.concatenate([initial[None], coarse_values[:-1]], axis=0)
    unused, interior = lax.scan(level_turn, fresh_start, inner_terms)
    finishing = evolve(interior[-1], level_step) + grouped_terms[:, -1]
    group_defect = finishing - coarse_values
    level_defect = jnp.concatenate([jnp.zeros((groups, GROUP - 1) + shape, jnp.float32), group_defect[:, None]], axis=1)
    level_defect = level_defect.reshape((N_TM,) + shape)
    corrected = jnp.concatenate([jnp.moveaxis(interior, 0, 1), coarse_values[:, None]], axis=1)
    corrected = corrected.reshape((N_TM,) + shape)
    unused, inside = march(before(corrected), feed_rate, kill_rate, fine_step, tables, STEPS_DEV - 1)
    trajectory = jnp.concatenate([jnp.moveaxis(inside, 0, 1), corrected[:, None]], axis=1)
    return (trajectory.reshape((N_TM * STEPS_DEV,) + shape), c_residual, group_coarse, level_defect)
```

```python
import functools

import jax
import jax.numpy as jnp
import ml_dtypes
import numpy as np
from jax import lax
from jax.experimental import pallas as pl
from jax.experimental.pallas import tpu as pltpu
from jax.sharding import PartitionSpec as P

STEPS_DEV = 4
GROUP = 16
INPUTS = 10
LEAD = 8
VMEM_GRANT = 64000000

diffusion = (0.2, 0.1)
interval_time = 0.03125
MESH = pl.DeviceIdType.MESH
single = np.float32


def cosine_basis(length):
    positions = np.arange(length, dtype=single)
    angles = single(np.pi) * (positions[:, None] + single(0.5)) * positions[None, :] / single(length)
    weight = np.where(positions == 0, np.sqrt(single(1.0 / length)), np.sqrt(single(2.0 / length)))
    return (np.cos(angles) * weight[None, :].astype(single)).astype(single)


def eigen_values(length):
    positions = np.arange(length, dtype=single)
    waves = np.sin(single(np.pi) * positions / single(2.0 * length))
    return (single(-4.0) * waves * waves).astype(single)


def halves(matrix):
    high = matrix.astype(ml_dtypes.bfloat16)
    low = (matrix - high.astype(np.float64)).astype(ml_dtypes.bfloat16)
    return high, low


def factors(rows, cols, time_step, rate, rank):
    basis_rows = cosine_basis(rows).astype(np.float64)
    basis_cols = cosine_basis(cols).astype(np.float64)
    spectrum = eigen_values(rows).astype(np.float64)[:, None] + eigen_values(cols).astype(np.float64)[None, :]
    factor = 1.0 / (1.0 - time_step * rate * spectrum)
    left, sizes, right = np.linalg.svd(factor)
    if rank is None:
        rank = 1
        while np.abs(factor - (left[:, :rank] * sizes[:rank]) @ right[:rank]).max() > 2.0**-26:
            rank += 1
        return rank
    left = left[:, :rank] * np.sqrt(sizes[:rank])
    right = right[:rank].T * np.sqrt(sizes[:rank])
    scale = left[0, 0]
    left[:, 0] /= scale
    right[:, 0] *= scale
    firsts = [basis_rows @ np.diag(left[:, k]) @ basis_rows.T for k in range(rank)]
    seconds = [basis_cols @ np.diag(right[:, k]) @ basis_cols.T for k in range(rank)]
    firsts[0] = firsts[0] - np.eye(rows)
    seconds[0] = seconds[0] - np.eye(cols)
    return firsts, seconds


@functools.lru_cache(maxsize=None)
def solve_tables(rows, cols, time_step):
    rank = max(factors(rows, cols, time_step, rate, None) for rate in diffusion)
    rank = max(rank, 2)
    species = [factors(rows, cols, time_step, rate, rank) for rate in diffusion]
    short = rank == 2
    rights, lefts = [], []
    for firsts, seconds in species:
        highs, lows = [], []
        for second in seconds:
            high, low = halves(second)
            highs += [high] * 2
            lows += [low] * 2
        high = np.concatenate(highs, 1)
        low = np.concatenate(lows, 1)
        rights.append(np.concatenate([high, high, low], 0))
        pairs = [halves(first) for first in firsts]
        highs = [high for high, low in pairs]
        lows = [low for high, low in pairs]
        if short:
            lefts.append(np.concatenate(highs + highs[:1] + lows[:1], 1))
        else:
            lefts.append(np.concatenate(highs + highs + lows, 1))
    return np.stack(rights), np.stack(lefts)


def kernel(devices, sizes, *refs):
    sources = refs[:INPUTS]
    packed_ref = refs[INPUTS]
    held = refs[INPUTS + 1 : 2 * INPUTS + 1]
    (initial_ref, guess_ref, feed_ref, kill_ref) = held[:4]
    table_refs = (held[4:6], held[6:8], held[8:10])
    (rates, b_buf, s_buf, r_buf, p_buf, e_buf, v_buf, b_out, r_out, p_out) = refs[2 * INPUTS + 1 : 2 * INPUTS + 11]
    (send_b, recv_b, send_s, recv_s, send_r, recv_r, send_p, recv_p, send_e, recv_e, send_f, send_o, load) = refs[
        2 * INPUTS + 11 :
    ]
    rows, cols = sizes
    groups = devices // GROUP
    me = lax.axis_index("tm")
    group = me // GROUP
    member = me % GROUP
    base = group * GROUP
    slot = (member + 2) % GROUP
    wraps = member >= GROUP - 2
    forwards = jnp.logical_and(wraps, group < groups - 1)
    relays = jnp.logical_and(wraps, group > 0)
    first_wrap = member == GROUP - 2
    leads = member == 0
    later = devices - (group + 1) * GROUP

    loads = [pltpu.make_async_copy(source, target, load.at[i]) for i, (source, target) in enumerate(zip(sources, held))]
    for copy in loads:
        copy.start()

    barrier = pltpu.get_barrier_semaphore()

    def greet(other):
        pl.semaphore_signal(barrier, inc=1, device_id=(other,), device_id_type=MESH)

    def peer(i):
        turn = 1 + (jnp.maximum(member - 1, 0) + i) % (GROUP - 1)
        return base + jnp.where(jnp.logical_and(member > 0, i == 0), 0, turn)

    def greet_peer(i, carry):
        greet(peer(i))
        return carry

    def greet_group(other, carry):
        greet(other * GROUP)
        return carry

    lax.fori_loop(0, group, greet_group, 0)

    @pl.when(jnp.logical_and(group > 0, member <= 1))
    def _():
        greet(me - 2)

    @pl.when(jnp.logical_and(group > 0, member == 0))
    def _():
        greet(me - 1)

    @pl.when(relays)
    def _():
        greet(me - GROUP)

    lax.fori_loop(0, GROUP - 1, greet_peer, 0)

    def await_barrier():
        crossing = jnp.where(forwards, member - (GROUP - 4), 0)
        pl.semaphore_wait(barrier, GROUP - 1 + crossing + jnp.where(leads, later, 0))

    def remote(source, target, send, recv, other):
        return pltpu.make_async_remote_copy(
            src_ref=source, dst_ref=target, send_sem=send, recv_sem=recv,
            device_id=(other,), device_id_type=MESH,
        )

    left_half = lax.broadcasted_iota(jnp.int32, (rows, 2 * cols), 1) < cols
    fine_step = interval_time / STEPS_DEV
    steps = (fine_step, interval_time, interval_time * GROUP)
    for copy in loads[:6]:
        copy.wait()
    feed = jnp.concatenate([feed_ref[...]] * 2, axis=1)
    kill = jnp.concatenate([kill_ref[...]] * 2, axis=1)
    for level, step in enumerate(steps):
        rates[3 * level] = 1.0 - step * feed
        rates[3 * level + 1] = step * feed
        rates[3 * level + 2] = 1.0 - step * (feed + kill)

    def double(value):
        return jnp.concatenate([value, value], axis=1)

    def join(state):
        return jnp.where(left_half, state[0], state[1])

    def spread(value):
        turned = pltpu.roll(value, cols, 1)
        return jnp.where(left_half, value, turned), jnp.where(left_half, turned, value)

    def plus(state, other):
        return state[0] + other[0], state[1] + other[1]

    def minus(state, other):
        return state[0] - other[0], state[1] - other[1]

    def split(value):
        high = value.astype(jnp.bfloat16)
        low = (value - high.astype(jnp.float32)).astype(jnp.bfloat16)
        return high, low

    def dot(first, second):
        return jnp.dot(first, second, preferred_element_type=jnp.float32)

    def stacked_rows(values):
        return jnp.concatenate(values, 0) if len(values) > 1 else values[0]

    def spectral(level, kind, main):
        count = main.shape[0] // rows
        high = main.astype(jnp.bfloat16)
        wide = high.astype(jnp.float32)
        mixed = jnp.where(stacked_rows([left_half] * count), wide, main - wide).astype(jnp.bfloat16)
        return dot(jnp.concatenate([mixed, high[:, :cols]], 1), table_refs[level][0][kind])

    def gather_terms(main, product):
        count = main.shape[0] // rows
        terms = product.shape[1] // (2 * cols)
        parts = [product[:, 2 * cols * k : 2 * cols * (k + 1)] for k in range(terms)]
        first = main + parts[0]
        parts[0] = first
        columns = []
        for n in range(count):
            pieces = [part[rows * n : rows * (n + 1)] for part in parts]
            if terms == 2:
                first_high, first_low = split(pieces[0])
                stack = [first_high, pieces[1].astype(jnp.bfloat16), first_low, first_high]
            else:
                pairs = [split(piece) for piece in pieces]
                stack = [a for a, b in pairs] + [b for a, b in pairs] + [a for a, b in pairs]
            columns.append(jnp.concatenate(stack, 0))
        return first, jnp.concatenate(columns, 1) if count > 1 else columns[0]

    def solve(level, mains):
        products = [spectral(level, kind, main) for kind, main in enumerate(mains)]
        gathered = [gather_terms(main, product) for main, product in zip(mains, products)]
        smalls = [dot(table_refs[level][1][kind], stack) for kind, (first, stack) in enumerate(gathered)]
        count = mains[0].shape[0] // rows
        return [
            [first[rows * n : rows * (n + 1)] + small[:, 2 * cols * n : 2 * cols * (n + 1)] for n in range(count)]
            for (first, stack), small in zip(gathered, smalls)
        ]

    def evolve(level, *states):
        step = steps[level]
        reacted = ([], [])
        for substrate, catalyst in states:
            uptake = step * (substrate * (catalyst * catalyst))
            reacted[0].append(rates[3 * level] * substrate + rates[3 * level + 1] - uptake)
            reacted[1].append(rates[3 * level + 2] * catalyst + uptake)
        return list(zip(*solve(level, [stacked_rows(values) for values in reacted])))

    start = double(initial_ref[0]), double(initial_ref[1])
    own = double(guess_ref[0, 0]), double(guess_ref[0, 1])

    def fine_turn(unused, pair):
        return tuple(evolve(0, *pair))

    relaxed, relaxed_zero = lax.fori_loop(0, STEPS_DEV, fine_turn, (own, start), unroll=True)
    zero_packed = join(relaxed_zero)
    r_out[...] = join(relaxed)

    def over_peers(act):
        def turn(i, carry):
            act(i)
            return carry

        lax.fori_loop(0, GROUP - 1, turn, 0)

    for copy in loads[6:]:
        copy.wait()
    arrived, arrived_one = lax.fori_loop(0, STEPS_DEV, fine_turn, (relaxed, relaxed_zero), unroll=True)
    level_relaxed, level_relaxed_zero = evolve(1, relaxed, relaxed_zero)
    p_out[...] = join(arrived)
    b_out[...] = join(minus(arrived, level_relaxed))
    r_copy = remote(r_out, r_buf, send_r, recv_r, me + 1)
    p_copy = remote(p_out, p_buf, send_p, recv_p, me + 2)
    s_forward = remote(r_out, s_buf, send_o, recv_s, me + GROUP)
    b_forward = remote(b_out, b_buf.at[slot], send_f, recv_b.at[slot], me + GROUP)

    def b_copy(i):
        return remote(b_out, b_buf.at[slot], send_b.at[i], recv_b.at[slot], peer(i))

    def b_relay(i):
        return remote(b_buf.at[slot], b_buf.at[slot], send_b.at[i], recv_b.at[slot], peer(i))

    def s_relay(i):
        return remote(s_buf, s_buf, send_s.at[i], recv_s, peer(i))

    await_barrier()

    @pl.when(jnp.logical_and(forwards, first_wrap))
    def _():
        s_forward.start()

    @pl.when(forwards)
    def _():
        b_forward.start()

    @pl.when(jnp.logical_not(wraps))
    def _():
        over_peers(lambda i: b_copy(i).start())
        b_buf[slot] = b_out[...]

    @pl.when(me + 2 < devices)
    def _():
        p_copy.start()

    @pl.when(me + 1 < devices)
    def _():
        r_copy.start()

    @pl.when(group == 0)
    def _():
        (level_start,) = evolve(1, start)
        s_buf[...] = join(start)
        b_buf[0] = join(minus(relaxed_zero, level_start))
        b_buf[1] = join(minus(arrived_one, level_relaxed_zero))

    @pl.when(me == 0)
    def _():
        r_buf[...] = zero_packed
        p_buf[...] = zero_packed

    @pl.when(me == 1)
    def _():
        p_buf[...] = join(arrived_one)

    @pl.when(group > 0)
    def _():
        remote(r_out, s_buf, send_o, recv_s, me).wait_recv()

    @pl.when(jnp.logical_and(relays, first_wrap))
    def _():
        over_peers(lambda i: s_relay(i).start())

    @pl.when(relays)
    def _():
        b_forward.wait_recv()
        over_peers(lambda i: b_relay(i).start())

    group_start = spread(s_buf[...])

    def await_b(k):
        @pl.when(jnp.logical_and(base + k >= 2, k != slot))
        def _():
            remote(b_out, b_buf.at[k], send_b.at[0], recv_b.at[k], me).wait_recv()

    coarse_start, coarse_initial = evolve(2, group_start, start)
    opens = group == 0
    first = jnp.where(opens, 2, 0)
    lead = jnp.where(jnp.logical_or(opens, 2 * member < GROUP), GROUP, LEAD)

    def relax_turn(k, state):
        await_b(k)
        (state,) = evolve(1, state)
        state = plus(state, spread(b_buf[k]))
        v_buf[k] = join(state)
        return state

    opening = tuple(jnp.where(opens, a, b) for a, b in zip(arrived_one, group_start))
    relaxing = lax.fori_loop(first, lead, relax_turn, opening)

    def set_e(closing):
        e_buf[group] = join(minus(closing, coarse_start))

    set_e(relaxing)

    def e_copy(i):
        return remote(e_buf.at[group], e_buf.at[group], send_e.at[i], recv_e.at[group], devices - 1 - i)

    def start_e(i, carry):
        e_copy(i).start()
        return carry

    @pl.when(leads)
    def _():
        lax.fori_loop(0, later, start_e, 0)

    @pl.when(opens)
    def _():
        v_buf[0] = zero_packed
        v_buf[1] = join(arrived_one)

    def await_e(other):
        remote(e_buf.at[other], e_buf.at[other], send_e.at[0], recv_e.at[other], me).wait_recv()

    def coarse_turn(other, before):
        await_e(other)
        (image,) = evolve(2, before)
        return plus(image, spread(e_buf[other]))

    @pl.when(group > 0)
    def _():
        await_e(0)

    first_coarse = plus(coarse_initial, spread(e_buf[0]))
    earlier = tuple(jnp.where(opens, a, b) for a, b in zip(start, first_coarse))
    earlier = lax.fori_loop(1, group, coarse_turn, earlier)

    def joint_turn(i, pair):
        await_b(lead + i)
        relaxing, prior = evolve(1, *pair)
        return plus(relaxing, spread(b_buf[lead + i])), plus(prior, spread(b_buf[i]))

    def replay_turn(i, state):
        (state,) = evolve(1, state)
        return plus(state, spread(b_buf[i]))

    relaxing, prior = lax.fori_loop(0, GROUP - lead, joint_turn, (relaxing, earlier))
    prior = lax.fori_loop(GROUP - lead, jnp.where(opens, 0, member), replay_turn, prior)

    @pl.when(lead < GROUP)
    def _():
        set_e(relaxing)

    kept = spread(v_buf[jnp.maximum(member - 1, 0)])
    prior = tuple(jnp.where(jnp.logical_and(opens, member > 0), a, b) for a, b in zip(kept, prior))
    (mine,) = evolve(2, earlier)
    mine = join(mine) + e_buf[group]
    (ending,) = evolve(1, prior)
    ending = join(ending) + b_buf[member]
    point = prior
    for i in range(STEPS_DEV - 1):
        (point,) = evolve(0, point)
        packed_ref[i] = join(point)
    last = member == GROUP - 1
    packed_ref[STEPS_DEV - 1] = jnp.where(last, mine, ending)
    packed_ref[STEPS_DEV + 1] = mine
    packed_ref[STEPS_DEV + 2] = jnp.where(last, ending - mine, 0.0)

    @pl.when(me >= 1)
    def _():
        remote(r_out, r_buf, send_r, recv_r, me).wait_recv()

    @pl.when(me >= 2)
    def _():
        remote(p_out, p_buf, send_p, recv_p, me).wait_recv()

    packed_ref[STEPS_DEV] = p_buf[...] - r_buf[...]

    @pl.when(jnp.logical_not(wraps))
    def _():
        over_peers(lambda i: b_copy(i).wait_send())

    @pl.when(relays)
    def _():
        over_peers(lambda i: b_relay(i).wait_send())

    @pl.when(jnp.logical_and(relays, first_wrap))
    def _():
        over_peers(lambda i: s_relay(i).wait_send())

    @pl.when(jnp.logical_and(forwards, first_wrap))
    def _():
        s_forward.wait_send()

    @pl.when(forwards)
    def _():
        b_forward.wait_send()

    @pl.when(me + 2 < devices)
    def _():
        p_copy.wait_send()

    @pl.when(me + 1 < devices)
    def _():
        r_copy.wait_send()

    def end_e(i, carry):
        e_copy(i).wait_send()
        return carry

    @pl.when(leads)
    def _():
        lax.fori_loop(0, later, end_e, 0)


def unpack(packed_ref, traj_ref, resid_ref, coarse_ref, defect_ref):
    cols = packed_ref.shape[2] // 2
    places = [(traj_ref, i) for i in range(STEPS_DEV)] + [(resid_ref, 0), (coarse_ref, 0), (defect_ref, 0)]
    for i, (ref, index) in enumerate(places):
        ref[index, 0] = packed_ref[i, :, :cols]
        ref[index, 1] = packed_ref[i, :, cols:]


assert GROUP <= 2 * LEAD <= 2 * GROUP


def shards(devices, initial, coarse_guess, feed_rate, kill_rate):
    rows, cols = initial.shape[1:]
    groups = devices // GROUP
    steps = (interval_time / STEPS_DEV, interval_time, interval_time * GROUP)
    tables = []
    for step in steps:
        tables += [jnp.asarray(table) for table in solve_tables(rows, cols, step)]
    state = (rows, 2 * cols)
    block = (1,) + initial.shape
    dma = pltpu.SemaphoreType.DMA
    whole = pl.BlockSpec(memory_space=pltpu.VMEM)
    inputs = (initial, coarse_guess, feed_rate, kill_rate, *tables)
    buffer = pltpu.VMEM(state, jnp.float32)
    packed = pl.pallas_call(
        functools.partial(kernel, devices, (rows, cols)),
        out_shape=jax.ShapeDtypeStruct((STEPS_DEV + 3,) + state, jnp.float32),
        in_specs=[pl.BlockSpec(memory_space=pltpu.HBM)] * INPUTS,
        out_specs=whole,
        scratch_shapes=[pltpu.VMEM(each.shape, each.dtype) for each in inputs]
        + [
            pltpu.VMEM((9,) + state, jnp.float32),
            pltpu.VMEM((GROUP,) + state, jnp.float32),
            buffer,
            buffer,
            buffer,
            pltpu.VMEM((groups,) + state, jnp.float32),
            pltpu.VMEM((GROUP,) + state, jnp.float32),
        ]
        + [buffer] * 3
        + [dma((GROUP,)), dma((GROUP,)), dma((GROUP,))]
        + [dma] * 5
        + [dma((devices,)), dma((groups,)), dma, dma, dma((INPUTS,))],
        compiler_params=pltpu.CompilerParams(
            collective_id=0, has_side_effects=True, vmem_limit_bytes=VMEM_GRANT
        ),
    )(*inputs)
    return pl.pallas_call(
        unpack,
        out_shape=[
            jax.ShapeDtypeStruct((STEPS_DEV,) + initial.shape, jnp.float32),
            jax.ShapeDtypeStruct(block, jnp.float32),
            jax.ShapeDtypeStruct(block, jnp.float32),
            jax.ShapeDtypeStruct(block, jnp.float32),
        ],
        in_specs=[whole],
        out_specs=[whole] * 4,
        compiler_params=pltpu.CompilerParams(vmem_limit_bytes=VMEM_GRANT),
    )(packed)


def solution(mesh):
    spread = P("tm", None, None, None)
    return jax.shard_map(
        functools.partial(shards, mesh.shape["tm"]),
        mesh=mesh,
        in_specs=(P(), spread, P(), P()),
        out_specs=(spread, spread, spread, spread),
        check_vma=False,
    )
```

```python
import functools

import jax
import jax.numpy as jnp
import ml_dtypes
import numpy as np
from jax import lax
from jax.experimental import pallas as pl
from jax.experimental.pallas import tpu as pltpu
from jax.sharding import PartitionSpec as P

STEPS_DEV = 4
GROUP = 16
INPUTS = 10
LEADERS = 4
VMEM_GRANT = 64000000

diffusion = (0.2, 0.1)
interval_time = 0.03125
MESH = pl.DeviceIdType.MESH
single = np.float32


def cosine_basis(length):
    positions = np.arange(length, dtype=single)
    angles = single(np.pi) * (positions[:, None] + single(0.5)) * positions[None, :] / single(length)
    weight = np.where(positions == 0, np.sqrt(single(1.0 / length)), np.sqrt(single(2.0 / length)))
    return (np.cos(angles) * weight[None, :].astype(single)).astype(single)


def eigen_values(length):
    positions = np.arange(length, dtype=single)
    waves = np.sin(single(np.pi) * positions / single(2.0 * length))
    return (single(-4.0) * waves * waves).astype(single)


def halves(matrix):
    high = matrix.astype(ml_dtypes.bfloat16)
    low = (matrix - high.astype(np.float64)).astype(ml_dtypes.bfloat16)
    return high, low


def factors(rows, cols, time_step, rate, rank):
    basis_rows = cosine_basis(rows).astype(np.float64)
    basis_cols = cosine_basis(cols).astype(np.float64)
    spectrum = eigen_values(rows).astype(np.float64)[:, None] + eigen_values(cols).astype(np.float64)[None, :]
    factor = 1.0 / (1.0 - time_step * rate * spectrum)
    left, sizes, right = np.linalg.svd(factor)
    if rank is None:
        rank = 1
        while np.abs(factor - (left[:, :rank] * sizes[:rank]) @ right[:rank]).max() > 2.0**-26:
            rank += 1
        return rank
    left = left[:, :rank] * np.sqrt(sizes[:rank])
    right = right[:rank].T * np.sqrt(sizes[:rank])
    scale = left[0, 0]
    left[:, 0] /= scale
    right[:, 0] *= scale
    firsts = [basis_rows @ np.diag(left[:, k]) @ basis_rows.T for k in range(rank)]
    seconds = [basis_cols @ np.diag(right[:, k]) @ basis_cols.T for k in range(rank)]
    firsts[0] = firsts[0] - np.eye(rows)
    seconds[0] = seconds[0] - np.eye(cols)
    return firsts, seconds


@functools.lru_cache(maxsize=None)
def solve_tables(rows, cols, time_step):
    rank = max(factors(rows, cols, time_step, rate, None) for rate in diffusion)
    rank = max(rank, 2)
    species = [factors(rows, cols, time_step, rate, rank) for rate in diffusion]
    short = rank == 2
    rights, lefts = [], []
    for firsts, seconds in species:
        highs, lows = [], []
        for second in seconds:
            high, low = halves(second)
            highs += [high] * 2
            lows += [low] * 2
        high = np.concatenate(highs, 1)
        low = np.concatenate(lows, 1)
        rights.append(np.concatenate([high, high, low], 0))
        pairs = [halves(first) for first in firsts]
        highs = [high for high, low in pairs]
        lows = [low for high, low in pairs]
        if short:
            lefts.append(np.concatenate(highs + highs[:1] + lows[:1], 1))
        else:
            lefts.append(np.concatenate(highs + highs + lows, 1))
    return np.stack(rights), np.stack(lefts)


def kernel(devices, sizes, *refs):
    sources = refs[:INPUTS]
    packed_ref = refs[INPUTS]
    held = refs[INPUTS + 1 : 2 * INPUTS + 1]
    (initial_ref, guess_ref, feed_ref, kill_ref) = held[:4]
    table_refs = (held[4:6], held[6:8], held[8:10])
    (rates, b_buf, s_buf, r_buf, p_buf, e_buf, u_buf, prior_buf, end_buf, mine_buf, b_out, r_out, p_out) = refs[
        2 * INPUTS + 1 : 2 * INPUTS + 14
    ]
    (
        send_b, recv_b, send_s, recv_s, send_e, recv_e, send_u, send_w,
        recv_u, recv_v, recv_w, send_r, recv_r, send_p, recv_p, load,
    ) = refs[2 * INPUTS + 14 :]
    rows, cols = sizes
    groups = devices // GROUP
    half = GROUP // 2
    me = lax.axis_index("tm")
    group = me // GROUP
    member = me % GROUP
    base = group * GROUP
    slot = (member + 2) % GROUP
    opens = group == 0
    wraps = member >= GROUP - 2
    forwards = jnp.logical_and(wraps, group < groups - 1)
    leads = jnp.logical_and(member >= half, member % 2 == 1)
    express = me == 0
    announces = jnp.where(opens, express, member == GROUP - 1)
    listeners = LEADERS * (groups - 1 - group)

    loads = [pltpu.make_async_copy(source, target, load.at[i]) for i, (source, target) in enumerate(zip(sources, held))]
    for copy in loads:
        copy.start()

    def leader(i):
        return GROUP - 1 - 2 * i

    barrier = pltpu.get_barrier_semaphore()

    def greet(other):
        pl.semaphore_signal(barrier, inc=1, device_id=(other,), device_id_type=MESH)

    def greet_peer(i, carry):
        greet(base + (member + 1 + i) % GROUP)
        return carry

    def greet_announcer(other, carry):
        greet(other * GROUP + jnp.where(other == 0, 0, GROUP - 1))
        return carry

    @pl.when(leads)
    def _():
        lax.fori_loop(0, group, greet_announcer, 0)

    @pl.when(jnp.logical_and(leads, group > 0))
    def _():
        greet(base - 2)
        greet(base - 1)

    @pl.when(jnp.logical_and(group > 0, member <= 1))
    def _():
        greet(me - 2)

    @pl.when(jnp.logical_and(group > 0, member == 0))
    def _():
        greet(me - 1)

    lax.fori_loop(0, GROUP - 1, greet_peer, 0)

    def await_barrier():
        crossing = jnp.where(forwards, LEADERS + member - (GROUP - 3), 0)
        pl.semaphore_wait(barrier, GROUP - 1 + crossing + jnp.where(announces, listeners, 0))

    def remote(source, target, send, recv, other):
        return pltpu.make_async_remote_copy(
            src_ref=source, dst_ref=target, send_sem=send, recv_sem=recv,
            device_id=(other,), device_id_type=MESH,
        )

    left_half = lax.broadcasted_iota(jnp.int32, (rows, 2 * cols), 1) < cols
    fine_step = interval_time / STEPS_DEV
    steps = (fine_step, interval_time, interval_time * GROUP)
    for copy in loads[:6]:
        copy.wait()
    feed = jnp.concatenate([feed_ref[...]] * 2, axis=1)
    kill = jnp.concatenate([kill_ref[...]] * 2, axis=1)
    for level, step in enumerate(steps):
        rates[3 * level] = 1.0 - step * feed
        rates[3 * level + 1] = step * feed
        rates[3 * level + 2] = 1.0 - step * (feed + kill)

    def double(value):
        return jnp.concatenate([value, value], axis=1)

    def join(state):
        return jnp.where(left_half, state[0], state[1])

    def spread(value):
        turned = pltpu.roll(value, cols, 1)
        return jnp.where(left_half, value, turned), jnp.where(left_half, turned, value)

    def plus(state, other):
        return state[0] + other[0], state[1] + other[1]

    def minus(state, other):
        return state[0] - other[0], state[1] - other[1]

    def split(value):
        high = value.astype(jnp.bfloat16)
        low = (value - high.astype(jnp.float32)).astype(jnp.bfloat16)
        return high, low

    def dot(first, second):
        return jnp.dot(first, second, preferred_element_type=jnp.float32)

    def stacked_rows(values):
        return jnp.concatenate(values, 0) if len(values) > 1 else values[0]

    def spectral(level, kind, main):
        count = main.shape[0] // rows
        high = main.astype(jnp.bfloat16)
        wide = high.astype(jnp.float32)
        mixed = jnp.where(stacked_rows([left_half] * count), wide, main - wide).astype(jnp.bfloat16)
        return dot(jnp.concatenate([mixed, high[:, :cols]], 1), table_refs[level][0][kind])

    def gather_terms(main, product):
        count = main.shape[0] // rows
        terms = product.shape[1] // (2 * cols)
        parts = [product[:, 2 * cols * k : 2 * cols * (k + 1)] for k in range(terms)]
        first = main + parts[0]
        parts[0] = first
        columns = []
        for n in range(count):
            pieces = [part[rows * n : rows * (n + 1)] for part in parts]
            if terms == 2:
                first_high, first_low = split(pieces[0])
                stack = [first_high, pieces[1].astype(jnp.bfloat16), first_low, first_high]
            else:
                pairs = [split(piece) for piece in pieces]
                stack = [a for a, b in pairs] + [b for a, b in pairs] + [a for a, b in pairs]
            columns.append(jnp.concatenate(stack, 0))
        return first, jnp.concatenate(columns, 1) if count > 1 else columns[0]

    def solve(level, mains):
        products = [spectral(level, kind, main) for kind, main in enumerate(mains)]
        gathered = [gather_terms(main, product) for main, product in zip(mains, products)]
        smalls = [dot(table_refs[level][1][kind], stack) for kind, (first, stack) in enumerate(gathered)]
        count = mains[0].shape[0] // rows
        return [
            [first[rows * n : rows * (n + 1)] + small[:, 2 * cols * n : 2 * cols * (n + 1)] for n in range(count)]
            for (first, stack), small in zip(gathered, smalls)
        ]

    def evolve(level, *states):
        step = steps[level]
        reacted = ([], [])
        for substrate, catalyst in states:
            uptake = step * (substrate * (catalyst * catalyst))
            reacted[0].append(rates[3 * level] * substrate + rates[3 * level + 1] - uptake)
            reacted[1].append(rates[3 * level + 2] * catalyst + uptake)
        return list(zip(*solve(level, [stacked_rows(values) for values in reacted])))

    start = double(initial_ref[0]), double(initial_ref[1])
    own = double(guess_ref[0, 0]), double(guess_ref[0, 1])

    def fine_turn(unused, pair):
        return tuple(evolve(0, *pair))

    relaxed, relaxed_zero = lax.fori_loop(0, STEPS_DEV, fine_turn, (own, start), unroll=True)
    zero_packed = join(relaxed_zero)
    r_out[...] = join(relaxed)

    for copy in loads[6:]:
        copy.wait()
    arrived, arrived_one = lax.fori_loop(0, STEPS_DEV, fine_turn, (relaxed, relaxed_zero), unroll=True)
    (level_relaxed,) = evolve(1, relaxed)
    p_out[...] = join(arrived)
    b_out[...] = join(minus(arrived, level_relaxed))
    r_copy = remote(r_out, r_buf, send_r, recv_r, me + 1)
    p_copy = remote(p_out, p_buf, send_p, recv_p, me + 2)
    reach = base + jnp.where(wraps, GROUP, 0)

    def b_copy(i, other):
        return remote(b_out, b_buf.at[slot], send_b.at[i], recv_b.at[slot], other)

    def s_copy(i):
        return remote(r_out, s_buf, send_s.at[i], recv_s, reach + leader(i))

    def over_b(act):
        @pl.when(jnp.logical_and(opens, jnp.logical_and(member > 0, jnp.logical_not(wraps))))
        def _():
            act(b_copy(LEADERS, 0))

        for i in range(LEADERS):

            @pl.when(jnp.logical_and(jnp.logical_or(forwards, jnp.logical_not(wraps)), me != reach + leader(i)))
            def _():
                act(b_copy(i, reach + leader(i)))

            @pl.when(jnp.logical_and(forwards, member == GROUP - 2))
            def _():
                act(s_copy(i))

    await_barrier()
    over_b(lambda copy: copy.start())

    @pl.when(me + 2 < devices)
    def _():
        p_copy.start()

    @pl.when(me + 1 < devices)
    def _():
        r_copy.start()

    @pl.when(jnp.logical_and(jnp.logical_or(leads, express), jnp.logical_not(wraps)))
    def _():
        b_buf[slot] = b_out[...]

    @pl.when(me == 0)
    def _():
        r_buf[...] = zero_packed
        p_buf[...] = zero_packed

    @pl.when(me == 1)
    def _():
        p_buf[...] = join(arrived_one)

    below = member - half - 1
    clients = (below, below + 1, member - 1)

    def u_copy(j):
        return remote(u_buf.at[clients[j]], prior_buf, send_u.at[j], recv_u, base + clients[j])

    def v_copy(j):
        return remote(u_buf.at[clients[j] + 1], end_buf, send_u.at[3 + j], recv_v, base + clients[j])

    def w_copy(j):
        return remote(mine_buf, mine_buf, send_w.at[j], recv_w, base + clients[j])

    def e_copy(i):
        other = (group + 1 + i // LEADERS) * GROUP + GROUP - 1 - 2 * (i % LEADERS)
        return remote(e_buf.at[group], e_buf.at[group], send_e.at[i], recv_e.at[group], other)

    def await_b(k):
        @pl.when(jnp.logical_and(base + k >= 2, jnp.logical_or(k != slot, wraps)))
        def _():
            remote(b_out, b_buf.at[k], send_b.at[0], recv_b.at[k], me).wait_recv()

    def await_e(other):
        remote(e_buf.at[other], e_buf.at[other], send_e.at[0], recv_e.at[other], me).wait_recv()

    def relax_turn(k, state):
        await_b(k)
        (state,) = evolve(1, state)
        state = plus(state, spread(b_buf[k]))
        u_buf[k + 1] = join(state)
        return state

    def coarse_turn(other, before):
        await_e(other)
        (image,) = evolve(2, before)
        return plus(image, spread(e_buf[other]))

    def serve(reached):
        @pl.when(jnp.logical_or(jnp.logical_and(reached >= below, reached <= below + 2), reached >= member - 1))
        def _():
            @pl.when(reached == below)
            def _():
                u_copy(0).start()

            @pl.when(reached == below + 1)
            def _():
                u_copy(1).start()
                v_copy(0).start()

            @pl.when(reached == below + 2)
            def _():
                v_copy(1).start()

            @pl.when(reached == member - 1)
            def _():
                u_copy(2).start()

            @pl.when(reached == member)
            def _():
                v_copy(2).start()

    def replay_turn(k, state):
        (state,) = evolve(1, state)
        state = plus(state, spread(b_buf[k]))
        u_buf[k + 1] = join(state)
        serve(k + 1)
        return state

    @pl.when(jnp.logical_or(leads, express))
    def _():
        @pl.when(opens)
        def _():
            s_buf[...] = join(start)
            u_buf[0] = join(start)
            u_buf[1] = zero_packed
            u_buf[2] = join(arrived_one)

        @pl.when(group > 0)
        def _():
            remote(r_out, s_buf, send_s.at[0], recv_s, me).wait_recv()

        group_start = spread(s_buf[...])
        coarse_start, coarse_initial = evolve(2, group_start, start)
        opening = tuple(jnp.where(opens, a, b) for a, b in zip(arrived_one, group_start))
        closing = lax.fori_loop(jnp.where(opens, 2, 0), GROUP, relax_turn, opening)
        e_buf[group] = join(minus(closing, coarse_start))

        @pl.when(announces)
        def _():
            def start_e(i, carry):
                e_copy(i).start()
                return carry

            lax.fori_loop(0, listeners, start_e, 0)

        @pl.when(leads)
        def _():
            @pl.when(group > 0)
            def _():
                await_e(0)

            first_coarse = plus(coarse_initial, spread(e_buf[0]))
            earlier = tuple(jnp.where(opens, a, b) for a, b in zip(start, first_coarse))
            earlier = lax.fori_loop(1, group, coarse_turn, earlier)

            @pl.when(group > 0)
            def _():
                u_buf[0] = join(earlier)
                serve(0)
                (mine,) = evolve(2, earlier)
                mine_buf[...] = join(mine) + e_buf[group]
                lax.fori_loop(0, member, replay_turn, earlier)

            @pl.when(opens)
            def _():
                mine_buf[...] = join(coarse_initial) + e_buf[0]
                for j in range(3):
                    u_copy(j).start()
                    v_copy(j).start()

            for j in range(3):
                w_copy(j).start()
            prior_buf[...] = u_buf[member]

    follows = jnp.logical_not(leads)

    @pl.when(follows)
    def _():
        remote(u_buf.at[0], prior_buf, send_u.at[0], recv_u, me).wait_recv()

    prior = spread(prior_buf[...])
    (ending,) = evolve(1, prior)
    ending = join(ending) + b_buf[member]
    point = prior
    for i in range(STEPS_DEV - 1):
        (point,) = evolve(0, point)
        packed_ref[i] = join(point)

    @pl.when(follows)
    def _():
        remote(u_buf.at[0], end_buf, send_u.at[0], recv_v, me).wait_recv()
        remote(mine_buf, mine_buf, send_w.at[0], recv_w, me).wait_recv()

    @pl.when(leads)
    def _():
        end_buf[...] = ending

    ending = end_buf[...]
    mine = mine_buf[...]
    last = member == GROUP - 1
    packed_ref[STEPS_DEV - 1] = jnp.where(last, mine, ending)
    packed_ref[STEPS_DEV + 1] = mine
    packed_ref[STEPS_DEV + 2] = jnp.where(last, ending - mine, 0.0)

    @pl.when(me >= 1)
    def _():
        remote(r_out, r_buf, send_r, recv_r, me).wait_recv()

    @pl.when(me >= 2)
    def _():
        remote(p_out, p_buf, send_p, recv_p, me).wait_recv()

    packed_ref[STEPS_DEV] = p_buf[...] - r_buf[...]
    over_b(lambda copy: copy.wait_send())

    @pl.when(me + 2 < devices)
    def _():
        p_copy.wait_send()

    @pl.when(me + 1 < devices)
    def _():
        r_copy.wait_send()

    @pl.when(leads)
    def _():
        for j in range(3):
            u_copy(j).wait_send()
            v_copy(j).wait_send()
            w_copy(j).wait_send()

    @pl.when(announces)
    def _():
        def end_e(i, carry):
            e_copy(i).wait_send()
            return carry

        lax.fori_loop(0, listeners, end_e, 0)


def unpack(packed_ref, traj_ref, resid_ref, coarse_ref, defect_ref):
    cols = packed_ref.shape[2] // 2
    places = [(traj_ref, i) for i in range(STEPS_DEV)] + [(resid_ref, 0), (coarse_ref, 0), (defect_ref, 0)]
    for i, (ref, index) in enumerate(places):
        ref[index, 0] = packed_ref[i, :, :cols]
        ref[index, 1] = packed_ref[i, :, cols:]


assert 4 * LEADERS == GROUP


def shards(devices, initial, coarse_guess, feed_rate, kill_rate):
    rows, cols = initial.shape[1:]
    groups = devices // GROUP
    steps = (interval_time / STEPS_DEV, interval_time, interval_time * GROUP)
    tables = []
    for step in steps:
        tables += [jnp.asarray(table) for table in solve_tables(rows, cols, step)]
    state = (rows, 2 * cols)
    block = (1,) + initial.shape
    dma = pltpu.SemaphoreType.DMA
    whole = pl.BlockSpec(memory_space=pltpu.VMEM)
    inputs = (initial, coarse_guess, feed_rate, kill_rate, *tables)
    buffer = pltpu.VMEM(state, jnp.float32)
    packed = pl.pallas_call(
        functools.partial(kernel, devices, (rows, cols)),
        out_shape=jax.ShapeDtypeStruct((STEPS_DEV + 3,) + state, jnp.float32),
        in_specs=[pl.BlockSpec(memory_space=pltpu.HBM)] * INPUTS,
        out_specs=whole,
        scratch_shapes=[pltpu.VMEM(each.shape, each.dtype) for each in inputs]
        + [
            pltpu.VMEM((9,) + state, jnp.float32),
            pltpu.VMEM((GROUP,) + state, jnp.float32),
            buffer,
            buffer,
            buffer,
            pltpu.VMEM((groups,) + state, jnp.float32),
            pltpu.VMEM((GROUP + 1,) + state, jnp.float32),
        ]
        + [buffer] * 6
        + [dma((LEADERS + 1,)), dma((GROUP,)), dma((LEADERS,)), dma]
        + [dma((LEADERS * groups,)), dma((groups,)), dma((6,)), dma((3,))]
        + [dma] * 7
        + [dma((INPUTS,))],
        compiler_params=pltpu.CompilerParams(
            collective_id=0, has_side_effects=True, vmem_limit_bytes=VMEM_GRANT
        ),
    )(*inputs)
    return pl.pallas_call(
        unpack,
        out_shape=[
            jax.ShapeDtypeStruct((STEPS_DEV,) + initial.shape, jnp.float32),
            jax.ShapeDtypeStruct(block, jnp.float32),
            jax.ShapeDtypeStruct(block, jnp.float32),
            jax.ShapeDtypeStruct(block, jnp.float32),
        ],
        in_specs=[whole],
        out_specs=[whole] * 4,
        compiler_params=pltpu.CompilerParams(vmem_limit_bytes=VMEM_GRANT),
    )(packed)


def solution(mesh):
    spread = P("tm", None, None, None)
    return jax.shard_map(
        functools.partial(shards, mesh.shape["tm"]),
        mesh=mesh,
        in_specs=(P(), spread, P(), P()),
        out_specs=(spread, spread, spread, spread),
        check_vma=False,
    )
```

```python
import functools

import jax
import jax.numpy as jnp
import ml_dtypes
import numpy as np
from jax import lax
from jax.experimental import pallas as pl
from jax.experimental.pallas import tpu as pltpu
from jax.sharding import PartitionSpec as P

STEPS_DEV = 4
GROUP = 16
INPUTS = 10
LEADERS = 4
PIECES = STEPS_DEV + 3
VMEM_GRANT = 64000000

diffusion = (0.2, 0.1)
interval_time = 0.03125
MESH = pl.DeviceIdType.MESH
single = np.float32


def cosine_basis(length):
    positions = np.arange(length, dtype=single)
    angles = single(np.pi) * (positions[:, None] + single(0.5)) * positions[None, :] / single(length)
    weight = np.where(positions == 0, np.sqrt(single(1.0 / length)), np.sqrt(single(2.0 / length)))
    return (np.cos(angles) * weight[None, :].astype(single)).astype(single)


def eigen_values(length):
    positions = np.arange(length, dtype=single)
    waves = np.sin(single(np.pi) * positions / single(2.0 * length))
    return (single(-4.0) * waves * waves).astype(single)


def halves(matrix):
    high = matrix.astype(ml_dtypes.bfloat16)
    low = (matrix - high.astype(np.float64)).astype(ml_dtypes.bfloat16)
    return high, low


def factors(rows, cols, time_step, rate, rank):
    basis_rows = cosine_basis(rows).astype(np.float64)
    basis_cols = cosine_basis(cols).astype(np.float64)
    spectrum = eigen_values(rows).astype(np.float64)[:, None] + eigen_values(cols).astype(np.float64)[None, :]
    factor = 1.0 / (1.0 - time_step * rate * spectrum)
    left, sizes, right = np.linalg.svd(factor)
    if rank is None:
        rank = 1
        while np.abs(factor - (left[:, :rank] * sizes[:rank]) @ right[:rank]).max() > 2.0**-26:
            rank += 1
        return rank
    left = left[:, :rank] * np.sqrt(sizes[:rank])
    right = right[:rank].T * np.sqrt(sizes[:rank])
    scale = left[0, 0]
    left[:, 0] /= scale
    right[:, 0] *= scale
    firsts = [basis_rows @ np.diag(left[:, k]) @ basis_rows.T for k in range(rank)]
    seconds = [basis_cols @ np.diag(right[:, k]) @ basis_cols.T for k in range(rank)]
    firsts[0] = firsts[0] - np.eye(rows)
    seconds[0] = seconds[0] - np.eye(cols)
    return firsts, seconds


@functools.lru_cache(maxsize=None)
def solve_tables(rows, cols, time_step):
    rank = max(factors(rows, cols, time_step, rate, None) for rate in diffusion)
    rank = max(rank, 2)
    species = [factors(rows, cols, time_step, rate, rank) for rate in diffusion]
    short = rank == 2
    rights, lefts = [], []
    for firsts, seconds in species:
        highs, lows = [], []
        for second in seconds:
            high, low = halves(second)
            highs += [high] * 2
            lows += [low] * 2
        high = np.concatenate(highs, 1)
        low = np.concatenate(lows, 1)
        rights.append(np.concatenate([high, high, low], 0))
        pairs = [halves(first) for first in firsts]
        highs = [high for high, low in pairs]
        lows = [low for high, low in pairs]
        if short:
            lefts.append(np.concatenate(highs + highs[:1] + lows[:1], 1))
        else:
            lefts.append(np.concatenate(highs + highs + lows, 1))
    return np.stack(rights), np.stack(lefts)


def kernel(devices, sizes, *refs):
    sources = refs[:INPUTS]
    packed_ref = refs[INPUTS]
    held = refs[INPUTS + 1 : 2 * INPUTS + 1]
    (initial_ref, guess_ref, feed_ref, kill_ref) = held[:4]
    table_refs = (held[4:6], held[6:8], held[8:10])
    (rates, b_buf, s_buf, r_buf, p_buf, e_buf, u_buf, prior_buf, end_buf, mine_buf, b_out, r_out, p_out, stage) = refs[
        2 * INPUTS + 1 : 2 * INPUTS + 15
    ]
    (
        send_b, recv_b, send_s, recv_s, send_e, recv_e, send_u, send_w,
        recv_u, recv_v, recv_w, send_r, recv_r, send_p, recv_p, load, save,
    ) = refs[2 * INPUTS + 15 :]
    rows, cols = sizes
    groups = devices // GROUP
    half = GROUP // 2
    me = lax.axis_index("tm")
    group = me // GROUP
    member = me % GROUP
    base = group * GROUP
    slot = (member + 2) % GROUP
    opens = group == 0
    wraps = member >= GROUP - 2
    forwards = jnp.logical_and(wraps, group < groups - 1)
    leads = jnp.logical_and(member >= half, member % 2 == 1)
    express = me == 0
    announces = jnp.where(opens, express, member == GROUP - 1)
    listeners = LEADERS * (groups - 1 - group)

    loads = [pltpu.make_async_copy(source, target, load.at[i]) for i, (source, target) in enumerate(zip(sources, held))]
    for copy in loads:
        copy.start()

    def leader(i):
        return GROUP - 1 - 2 * i

    barrier = pltpu.get_barrier_semaphore()

    def greet(other):
        pl.semaphore_signal(barrier, inc=1, device_id=(other,), device_id_type=MESH)

    def greet_peer(i, carry):
        greet(base + (member + 1 + i) % GROUP)
        return carry

    def greet_announcer(other, carry):
        greet(other * GROUP + jnp.where(other == 0, 0, GROUP - 1))
        return carry

    @pl.when(leads)
    def _():
        lax.fori_loop(0, group, greet_announcer, 0)

    @pl.when(jnp.logical_and(leads, group > 0))
    def _():
        greet(base - 2)
        greet(base - 1)

    @pl.when(jnp.logical_and(group > 0, member <= 1))
    def _():
        greet(me - 2)

    @pl.when(jnp.logical_and(group > 0, member == 0))
    def _():
        greet(me - 1)

    lax.fori_loop(0, GROUP - 1, greet_peer, 0)

    def await_barrier():
        crossing = jnp.where(forwards, LEADERS + member - (GROUP - 3), 0)
        pl.semaphore_wait(barrier, GROUP - 1 + crossing + jnp.where(announces, listeners, 0))

    def remote(source, target, send, recv, other):
        return pltpu.make_async_remote_copy(
            src_ref=source, dst_ref=target, send_sem=send, recv_sem=recv,
            device_id=(other,), device_id_type=MESH,
        )

    left_half = lax.broadcasted_iota(jnp.int32, (rows, 2 * cols), 1) < cols
    fine_step = interval_time / STEPS_DEV
    steps = (fine_step, interval_time, interval_time * GROUP)
    for copy in loads[:6]:
        copy.wait()
    feed = jnp.concatenate([feed_ref[...]] * 2, axis=1)
    kill = jnp.concatenate([kill_ref[...]] * 2, axis=1)
    for level, step in enumerate(steps):
        rates[3 * level] = 1.0 - step * feed
        rates[3 * level + 1] = step * feed
        rates[3 * level + 2] = 1.0 - step * (feed + kill)

    def double(value):
        return jnp.concatenate([value, value], axis=1)

    def join(state):
        return jnp.where(left_half, state[0], state[1])

    def spread(value):
        turned = pltpu.roll(value, cols, 1)
        return jnp.where(left_half, value, turned), jnp.where(left_half, turned, value)

    def plus(state, other):
        return state[0] + other[0], state[1] + other[1]

    def minus(state, other):
        return state[0] - other[0], state[1] - other[1]

    def split(value):
        high = value.astype(jnp.bfloat16)
        low = (value - high.astype(jnp.float32)).astype(jnp.bfloat16)
        return high, low

    def dot(first, second):
        return jnp.dot(first, second, preferred_element_type=jnp.float32)

    def stacked_rows(values):
        return jnp.concatenate(values, 0) if len(values) > 1 else values[0]

    def spectral(level, kind, main):
        count = main.shape[0] // rows
        high = main.astype(jnp.bfloat16)
        wide = high.astype(jnp.float32)
        mixed = jnp.where(stacked_rows([left_half] * count), wide, main - wide).astype(jnp.bfloat16)
        return dot(jnp.concatenate([mixed, high[:, :cols]], 1), table_refs[level][0][kind])

    def gather_terms(main, product):
        count = main.shape[0] // rows
        terms = product.shape[1] // (2 * cols)
        parts = [product[:, 2 * cols * k : 2 * cols * (k + 1)] for k in range(terms)]
        first = main + parts[0]
        parts[0] = first
        columns = []
        for n in range(count):
            pieces = [part[rows * n : rows * (n + 1)] for part in parts]
            if terms == 2:
                first_high, first_low = split(pieces[0])
                stack = [first_high, pieces[1].astype(jnp.bfloat16), first_low, first_high]
            else:
                pairs = [split(piece) for piece in pieces]
                stack = [a for a, b in pairs] + [b for a, b in pairs] + [a for a, b in pairs]
            columns.append(jnp.concatenate(stack, 0))
        return first, jnp.concatenate(columns, 1) if count > 1 else columns[0]

    def solve(level, mains):
        products = [spectral(level, kind, main) for kind, main in enumerate(mains)]
        gathered = [gather_terms(main, product) for main, product in zip(mains, products)]
        smalls = [dot(table_refs[level][1][kind], stack) for kind, (first, stack) in enumerate(gathered)]
        count = mains[0].shape[0] // rows
        return [
            [first[rows * n : rows * (n + 1)] + small[:, 2 * cols * n : 2 * cols * (n + 1)] for n in range(count)]
            for (first, stack), small in zip(gathered, smalls)
        ]

    def evolve(level, *states):
        step = steps[level]
        reacted = ([], [])
        for substrate, catalyst in states:
            uptake = step * (substrate * (catalyst * catalyst))
            reacted[0].append(rates[3 * level] * substrate + rates[3 * level + 1] - uptake)
            reacted[1].append(rates[3 * level + 2] * catalyst + uptake)
        return list(zip(*solve(level, [stacked_rows(values) for values in reacted])))

    start = double(initial_ref[0]), double(initial_ref[1])
    own = double(guess_ref[0, 0]), double(guess_ref[0, 1])

    def fine_turn(unused, pair):
        return tuple(evolve(0, *pair))

    relaxed, relaxed_zero = lax.fori_loop(0, STEPS_DEV, fine_turn, (own, start), unroll=True)
    zero_packed = join(relaxed_zero)
    r_out[...] = join(relaxed)

    for copy in loads[6:]:
        copy.wait()
    arrived, arrived_one = lax.fori_loop(0, STEPS_DEV, fine_turn, (relaxed, relaxed_zero), unroll=True)
    (level_relaxed,) = evolve(1, relaxed)
    p_out[...] = join(arrived)
    b_out[...] = join(minus(arrived, level_relaxed))
    r_copy = remote(r_out, r_buf, send_r, recv_r, me + 1)
    p_copy = remote(p_out, p_buf, send_p, recv_p, me + 2)
    reach = base + jnp.where(wraps, GROUP, 0)

    def b_copy(i, other):
        return remote(b_out, b_buf.at[slot], send_b.at[i], recv_b.at[slot], other)

    def s_copy(i):
        return remote(r_out, s_buf, send_s.at[i], recv_s, reach + leader(i))

    def over_b(act):
        @pl.when(jnp.logical_and(opens, jnp.logical_and(member > 0, jnp.logical_not(wraps))))
        def _():
            act(b_copy(LEADERS, 0))

        for i in range(LEADERS):

            @pl.when(jnp.logical_and(jnp.logical_or(forwards, jnp.logical_not(wraps)), me != reach + leader(i)))
            def _():
                act(b_copy(i, reach + leader(i)))

            @pl.when(jnp.logical_and(forwards, member == GROUP - 2))
            def _():
                act(s_copy(i))

    await_barrier()
    over_b(lambda copy: copy.start())

    @pl.when(me + 2 < devices)
    def _():
        p_copy.start()

    @pl.when(me + 1 < devices)
    def _():
        r_copy.start()

    @pl.when(jnp.logical_and(jnp.logical_or(leads, express), jnp.logical_not(wraps)))
    def _():
        b_buf[slot] = b_out[...]

    @pl.when(me == 0)
    def _():
        r_buf[...] = zero_packed
        p_buf[...] = zero_packed

    @pl.when(me == 1)
    def _():
        p_buf[...] = join(arrived_one)

    below = member - half - 1
    clients = (below, below + 1, member - 1)

    def u_copy(j):
        return remote(u_buf.at[clients[j]], prior_buf, send_u.at[j], recv_u, base + clients[j])

    def v_copy(j):
        return remote(u_buf.at[clients[j] + 1], end_buf, send_u.at[3 + j], recv_v, base + clients[j])

    def w_copy(j):
        return remote(mine_buf, mine_buf, send_w.at[j], recv_w, base + clients[j])

    def e_copy(i):
        other = (group + 1 + i // LEADERS) * GROUP + GROUP - 1 - 2 * (i % LEADERS)
        return remote(e_buf.at[group], e_buf.at[group], send_e.at[i], recv_e.at[group], other)

    def start_w():
        for j in range(3):
            w_copy(j).start()

    def await_b(k):
        @pl.when(jnp.logical_and(base + k >= 2, jnp.logical_or(k != slot, wraps)))
        def _():
            remote(b_out, b_buf.at[k], send_b.at[0], recv_b.at[k], me).wait_recv()

    def await_e(other):
        remote(e_buf.at[other], e_buf.at[other], send_e.at[0], recv_e.at[other], me).wait_recv()

    def relax_turn(k, state):
        await_b(k)
        (state,) = evolve(1, state)
        state = plus(state, spread(b_buf[k]))
        u_buf[k + 1] = join(state)
        return state

    def coarse_turn(other, before):
        await_e(other)
        (image,) = evolve(2, before)
        return plus(image, spread(e_buf[other]))

    def serve(reached):
        @pl.when(reached == below)
        def _():
            u_copy(0).start()

        @pl.when(reached == below + 2)
        def _():
            u_copy(1).start()
            v_copy(0).start()
            v_copy(1).start()

        @pl.when(reached == member - 1)
        def _():
            u_copy(2).start()

    def replay_turn(k, state):
        (state,) = evolve(1, state)
        state = plus(state, spread(b_buf[k]))
        u_buf[k + 1] = join(state)
        return state

    def replay_pair(n, state):
        state = replay_turn(2 * n + 1, replay_turn(2 * n, state))
        serve(2 * n + 2)
        return state

    def relax_pair(n, state):
        return relax_turn(2 * n + 1, relax_turn(2 * n, state))

    @pl.when(jnp.logical_or(leads, express))
    def _():
        @pl.when(opens)
        def _():
            s_buf[...] = join(start)
            u_buf[0] = join(start)
            u_buf[1] = zero_packed
            u_buf[2] = join(arrived_one)

        @pl.when(group > 0)
        def _():
            remote(r_out, s_buf, send_s.at[0], recv_s, me).wait_recv()

        group_start = spread(s_buf[...])
        coarse_start, coarse_initial = evolve(2, group_start, start)
        opening = tuple(jnp.where(opens, a, b) for a, b in zip(arrived_one, group_start))
        closing = lax.fori_loop(jnp.where(opens, 1, 0), GROUP // 2, relax_pair, opening)
        e_buf[group] = join(minus(closing, coarse_start))

        @pl.when(announces)
        def _():
            def start_e(i, carry):
                e_copy(i).start()
                return carry

            lax.fori_loop(0, listeners, start_e, 0)

        @pl.when(leads)
        def _():
            @pl.when(group > 0)
            def _():
                await_e(0)

            first_coarse = plus(coarse_initial, spread(e_buf[0]))
            earlier = tuple(jnp.where(opens, a, b) for a, b in zip(start, first_coarse))
            earlier = lax.fori_loop(1, group, coarse_turn, earlier)

            @pl.when(group > 0)
            def _():
                u_buf[0] = join(earlier)
                serve(0)
                (mine,) = evolve(2, earlier)
                state = replay_pair(0, earlier)
                mine_buf[...] = join(mine) + e_buf[group]
                start_w()
                state = lax.fori_loop(1, member // 2, replay_pair, state)
                replay_turn(member - 1, state)
                v_copy(2).start()

            @pl.when(opens)
            def _():
                mine_buf[...] = join(coarse_initial) + e_buf[0]
                for j in range(3):
                    u_copy(j).start()
                    v_copy(j).start()
                start_w()

            prior_buf[...] = u_buf[member]

    follows = jnp.logical_not(leads)

    @pl.when(me >= 1)
    def _():
        remote(r_out, r_buf, send_r, recv_r, me).wait_recv()

    @pl.when(me >= 2)
    def _():
        remote(p_out, p_buf, send_p, recv_p, me).wait_recv()

    stores = [pltpu.make_async_copy(stage.at[i], packed_ref.at[i], save.at[i]) for i in range(PIECES)]

    def put(i, value):
        stage[i] = value
        stores[i].start()

    put(STEPS_DEV, p_buf[...] - r_buf[...])

    @pl.when(follows)
    def _():
        remote(u_buf.at[0], prior_buf, send_u.at[0], recv_u, me).wait_recv()

    prior = spread(prior_buf[...])
    (ending,) = evolve(1, prior)
    ending = join(ending) + b_buf[member]
    point = prior
    for i in range(STEPS_DEV - 1):
        (point,) = evolve(0, point)
        put(i, join(point))

    @pl.when(follows)
    def _():
        remote(u_buf.at[0], end_buf, send_u.at[0], recv_v, me).wait_recv()
        remote(mine_buf, mine_buf, send_w.at[0], recv_w, me).wait_recv()

    @pl.when(leads)
    def _():
        end_buf[...] = ending

    ending = end_buf[...]
    mine = mine_buf[...]
    last = member == GROUP - 1
    put(STEPS_DEV - 1, jnp.where(last, mine, ending))
    put(STEPS_DEV + 1, mine)
    put(STEPS_DEV + 2, jnp.where(last, ending - mine, 0.0))
    over_b(lambda copy: copy.wait_send())

    @pl.when(me + 2 < devices)
    def _():
        p_copy.wait_send()

    @pl.when(me + 1 < devices)
    def _():
        r_copy.wait_send()

    @pl.when(leads)
    def _():
        for j in range(3):
            u_copy(j).wait_send()
            v_copy(j).wait_send()
            w_copy(j).wait_send()

    @pl.when(announces)
    def _():
        def end_e(i, carry):
            e_copy(i).wait_send()
            return carry

        lax.fori_loop(0, listeners, end_e, 0)

    for copy in stores:
        copy.wait()


def unpack(packed_ref, traj_ref, resid_ref, coarse_ref, defect_ref, stage, parts, load, save):
    cols = packed_ref.shape[2] // 2
    places = [(traj_ref, i) for i in range(STEPS_DEV)] + [(resid_ref, 0), (coarse_ref, 0), (defect_ref, 0)]
    loads = [pltpu.make_async_copy(packed_ref.at[i], stage.at[i], load.at[i]) for i in range(PIECES)]
    stores = [pltpu.make_async_copy(parts.at[i], ref.at[n], save.at[i]) for i, (ref, n) in enumerate(places)]
    for copy in loads:
        copy.start()
    for i in range(PIECES):
        loads[i].wait()
        parts[i, 0] = stage[i, :, :cols]
        parts[i, 1] = stage[i, :, cols:]
        stores[i].start()
    for copy in stores:
        copy.wait()


assert 4 * LEADERS == GROUP


def shards(devices, initial, coarse_guess, feed_rate, kill_rate):
    rows, cols = initial.shape[1:]
    groups = devices // GROUP
    steps = (interval_time / STEPS_DEV, interval_time, interval_time * GROUP)
    tables = []
    for step in steps:
        tables += [jnp.asarray(table) for table in solve_tables(rows, cols, step)]
    state = (rows, 2 * cols)
    block = (1,) + initial.shape
    dma = pltpu.SemaphoreType.DMA
    remain = pl.BlockSpec(memory_space=pltpu.HBM)
    inputs = (initial, coarse_guess, feed_rate, kill_rate, *tables)
    buffer = pltpu.VMEM(state, jnp.float32)
    packed = pl.pallas_call(
        functools.partial(kernel, devices, (rows, cols)),
        out_shape=jax.ShapeDtypeStruct((PIECES,) + state, jnp.float32),
        in_specs=[remain] * INPUTS,
        out_specs=remain,
        scratch_shapes=[pltpu.VMEM(each.shape, each.dtype) for each in inputs]
        + [
            pltpu.VMEM((9,) + state, jnp.float32),
            pltpu.VMEM((GROUP,) + state, jnp.float32),
            buffer,
            buffer,
            buffer,
            pltpu.VMEM((groups,) + state, jnp.float32),
            pltpu.VMEM((GROUP + 1,) + state, jnp.float32),
        ]
        + [buffer] * 6
        + [pltpu.VMEM((PIECES,) + state, jnp.float32)]
        + [dma((LEADERS + 1,)), dma((GROUP,)), dma((LEADERS,)), dma]
        + [dma((LEADERS * groups,)), dma((groups,)), dma((6,)), dma((3,))]
        + [dma] * 7
        + [dma((INPUTS,)), dma((PIECES,))],
        compiler_params=pltpu.CompilerParams(
            collective_id=0, has_side_effects=True, vmem_limit_bytes=VMEM_GRANT
        ),
    )(*inputs)
    return pl.pallas_call(
        unpack,
        out_shape=[
            jax.ShapeDtypeStruct((STEPS_DEV,) + initial.shape, jnp.float32),
            jax.ShapeDtypeStruct(block, jnp.float32),
            jax.ShapeDtypeStruct(block, jnp.float32),
            jax.ShapeDtypeStruct(block, jnp.float32),
        ],
        in_specs=[remain],
        out_specs=[remain] * 4,
        scratch_shapes=[pltpu.VMEM((PIECES,) + state, jnp.float32), pltpu.VMEM((PIECES,) + initial.shape, jnp.float32)]
        + [dma((PIECES,))] * 2,
        compiler_params=pltpu.CompilerParams(vmem_limit_bytes=VMEM_GRANT),
    )(packed)


def solution(mesh):
    spread = P("tm", None, None, None)
    return jax.shard_map(
        functools.partial(shards, mesh.shape["tm"]),
        mesh=mesh,
        in_specs=(P(), spread, P(), P()),
        out_specs=(spread, spread, spread, spread),
        check_vma=False,
    )
```

```python
import functools

import jax
import jax.numpy as jnp
import ml_dtypes
import numpy as np
from jax import lax
from jax.experimental import pallas as pl
from jax.experimental.pallas import tpu as pltpu
from jax.sharding import PartitionSpec as P

STEPS_DEV = 4
GROUP = 16
INPUTS = 10
LEADERS = 4
PIECES = STEPS_DEV + 3
VMEM_GRANT = 64000000

diffusion = (0.2, 0.1)
interval_time = 0.03125
MESH = pl.DeviceIdType.MESH
single = np.float32


def cosine_basis(length):
    positions = np.arange(length, dtype=single)
    angles = single(np.pi) * (positions[:, None] + single(0.5)) * positions[None, :] / single(length)
    weight = np.where(positions == 0, np.sqrt(single(1.0 / length)), np.sqrt(single(2.0 / length)))
    return (np.cos(angles) * weight[None, :].astype(single)).astype(single)


def eigen_values(length):
    positions = np.arange(length, dtype=single)
    waves = np.sin(single(np.pi) * positions / single(2.0 * length))
    return (single(-4.0) * waves * waves).astype(single)


def halves(matrix):
    high = matrix.astype(ml_dtypes.bfloat16)
    low = (matrix - high.astype(np.float64)).astype(ml_dtypes.bfloat16)
    return high, low


def factors(rows, cols, time_step, rate, rank):
    basis_rows = cosine_basis(rows).astype(np.float64)
    basis_cols = cosine_basis(cols).astype(np.float64)
    spectrum = eigen_values(rows).astype(np.float64)[:, None] + eigen_values(cols).astype(np.float64)[None, :]
    factor = 1.0 / (1.0 - time_step * rate * spectrum)
    left, sizes, right = np.linalg.svd(factor)
    if rank is None:
        rank = 1
        while np.abs(factor - (left[:, :rank] * sizes[:rank]) @ right[:rank]).max() > 2.0**-26:
            rank += 1
        return rank
    left = left[:, :rank] * np.sqrt(sizes[:rank])
    right = right[:rank].T * np.sqrt(sizes[:rank])
    scale = left[0, 0]
    left[:, 0] /= scale
    right[:, 0] *= scale
    firsts = [basis_rows @ np.diag(left[:, k]) @ basis_rows.T for k in range(rank)]
    seconds = [basis_cols @ np.diag(right[:, k]) @ basis_cols.T for k in range(rank)]
    firsts[0] = firsts[0] - np.eye(rows)
    seconds[0] = seconds[0] - np.eye(cols)
    return firsts, seconds


@functools.lru_cache(maxsize=None)
def solve_tables(rows, cols, time_step):
    rank = max(factors(rows, cols, time_step, rate, None) for rate in diffusion)
    rank = max(rank, 2)
    species = [factors(rows, cols, time_step, rate, rank) for rate in diffusion]
    short = rank == 2
    rights, lefts = [], []
    for firsts, seconds in species:
        highs, lows = [], []
        for second in seconds:
            high, low = halves(second)
            highs += [high] * 2
            lows += [low] * 2
        high = np.concatenate(highs, 1)
        low = np.concatenate(lows, 1)
        rights.append(np.concatenate([high, high, low], 0))
        pairs = [halves(first) for first in firsts]
        highs = [high for high, low in pairs]
        lows = [low for high, low in pairs]
        if short:
            lefts.append(np.concatenate(highs + highs[:1] + lows[:1], 1))
        else:
            lefts.append(np.concatenate(highs + highs + lows, 1))
    return np.stack(rights), np.stack(lefts)


def kernel(devices, sizes, *refs):
    sources = refs[:INPUTS]
    packed_ref = refs[INPUTS]
    held = refs[INPUTS + 1 : 2 * INPUTS + 1]
    (initial_ref, guess_ref, feed_ref, kill_ref) = held[:4]
    table_refs = (held[4:6], held[6:8], held[8:10])
    (rates, b_buf, s_buf, r_buf, p_buf, e_buf, u_buf, prior_buf, end_buf, mine_buf, b_out, r_out, p_out, stage) = refs[
        2 * INPUTS + 1 : 2 * INPUTS + 15
    ]
    (
        send_b, recv_b, send_s, recv_s, send_e, recv_e, send_u, send_w,
        recv_u, recv_v, recv_w, send_r, recv_r, send_p, recv_p, load, save,
    ) = refs[2 * INPUTS + 15 :]
    rows, cols = sizes
    groups = devices // GROUP
    half = GROUP // 2
    me = lax.axis_index("tm")
    group = me // GROUP
    member = me % GROUP
    base = group * GROUP
    slot = (member + 2) % GROUP
    opens = group == 0
    wraps = member >= GROUP - 2
    forwards = jnp.logical_and(wraps, group < groups - 1)
    leads = jnp.logical_and(member >= half, member % 2 == 1)
    relaxes = member == jnp.where(opens, 0, half - 1)
    listeners = LEADERS * (groups - 1 - group)

    loads = [pltpu.make_async_copy(source, target, load.at[i]) for i, (source, target) in enumerate(zip(sources, held))]
    for copy in loads:
        copy.start()

    def leader(i):
        return GROUP - 1 - 2 * i

    barrier = pltpu.get_barrier_semaphore()

    def greet(other):
        pl.semaphore_signal(barrier, inc=1, device_id=(other,), device_id_type=MESH)

    def greet_peer(i, carry):
        greet(base + (member + 1 + i) % GROUP)
        return carry

    def relaxer(other):
        return other * GROUP + jnp.where(other == 0, 0, half - 1)

    def greet_relaxer(other, carry):
        greet(relaxer(other))
        return carry

    @pl.when(leads)
    def _():
        lax.fori_loop(0, group, greet_relaxer, 0)

    @pl.when(jnp.logical_and(jnp.logical_or(leads, relaxes), group > 0))
    def _():
        greet(base - 2)
        greet(base - 1)

    @pl.when(jnp.logical_and(group > 0, member <= 1))
    def _():
        greet(me - 2)

    @pl.when(jnp.logical_and(group > 0, member == 0))
    def _():
        greet(me - 1)

    lax.fori_loop(0, GROUP - 1, greet_peer, 0)

    def await_barrier():
        crossing = jnp.where(forwards, LEADERS + member - (GROUP - 4), 0)
        pl.semaphore_wait(barrier, GROUP - 1 + crossing + jnp.where(relaxes, listeners, 0))

    def remote(source, target, send, recv, other):
        return pltpu.make_async_remote_copy(
            src_ref=source, dst_ref=target, send_sem=send, recv_sem=recv,
            device_id=(other,), device_id_type=MESH,
        )

    left_half = lax.broadcasted_iota(jnp.int32, (rows, 2 * cols), 1) < cols
    fine_step = interval_time / STEPS_DEV
    steps = (fine_step, interval_time, interval_time * GROUP)
    for copy in loads[:6]:
        copy.wait()
    feed = jnp.concatenate([feed_ref[...]] * 2, axis=1)
    kill = jnp.concatenate([kill_ref[...]] * 2, axis=1)
    for level, step in enumerate(steps):
        rates[3 * level] = 1.0 - step * feed
        rates[3 * level + 1] = step * feed
        rates[3 * level + 2] = 1.0 - step * (feed + kill)

    def double(value):
        return jnp.concatenate([value, value], axis=1)

    def join(state):
        return jnp.where(left_half, state[0], state[1])

    def spread(value):
        turned = pltpu.roll(value, cols, 1)
        return jnp.where(left_half, value, turned), jnp.where(left_half, turned, value)

    def plus(state, other):
        return state[0] + other[0], state[1] + other[1]

    def minus(state, other):
        return state[0] - other[0], state[1] - other[1]

    def split(value):
        high = value.astype(jnp.bfloat16)
        low = (value - high.astype(jnp.float32)).astype(jnp.bfloat16)
        return high, low

    def dot(first, second):
        return jnp.dot(first, second, preferred_element_type=jnp.float32)

    def stacked_rows(values):
        return jnp.concatenate(values, 0) if len(values) > 1 else values[0]

    def spectral(level, kind, main):
        count = main.shape[0] // rows
        high = main.astype(jnp.bfloat16)
        wide = high.astype(jnp.float32)
        mixed = jnp.where(stacked_rows([left_half] * count), wide, main - wide).astype(jnp.bfloat16)
        return dot(jnp.concatenate([mixed, high[:, :cols]], 1), table_refs[level][0][kind])

    def gather_terms(main, product):
        count = main.shape[0] // rows
        terms = product.shape[1] // (2 * cols)
        parts = [product[:, 2 * cols * k : 2 * cols * (k + 1)] for k in range(terms)]
        first = main + parts[0]
        parts[0] = first
        columns = []
        for n in range(count):
            pieces = [part[rows * n : rows * (n + 1)] for part in parts]
            if terms == 2:
                first_high, first_low = split(pieces[0])
                stack = [first_high, pieces[1].astype(jnp.bfloat16), first_low, first_high]
            else:
                pairs = [split(piece) for piece in pieces]
                stack = [a for a, b in pairs] + [b for a, b in pairs] + [a for a, b in pairs]
            columns.append(jnp.concatenate(stack, 0))
        return first, jnp.concatenate(columns, 1) if count > 1 else columns[0]

    def solve(level, mains):
        products = [spectral(level, kind, main) for kind, main in enumerate(mains)]
        gathered = [gather_terms(main, product) for main, product in zip(mains, products)]
        smalls = [dot(table_refs[level][1][kind], stack) for kind, (first, stack) in enumerate(gathered)]
        count = mains[0].shape[0] // rows
        return [
            [first[rows * n : rows * (n + 1)] + small[:, 2 * cols * n : 2 * cols * (n + 1)] for n in range(count)]
            for (first, stack), small in zip(gathered, smalls)
        ]

    def evolve(level, *states):
        step = steps[level]
        reacted = ([], [])
        for substrate, catalyst in states:
            uptake = step * (substrate * (catalyst * catalyst))
            reacted[0].append(rates[3 * level] * substrate + rates[3 * level + 1] - uptake)
            reacted[1].append(rates[3 * level + 2] * catalyst + uptake)
        return list(zip(*solve(level, [stacked_rows(values) for values in reacted])))

    start = double(initial_ref[0]), double(initial_ref[1])
    own = double(guess_ref[0, 0]), double(guess_ref[0, 1])

    def fine_turn(unused, pair):
        return tuple(evolve(0, *pair))

    relaxed, relaxed_zero = lax.fori_loop(0, STEPS_DEV, fine_turn, (own, start), unroll=True)
    zero_packed = join(relaxed_zero)
    r_out[...] = join(relaxed)

    for copy in loads[6:]:
        copy.wait()
    arrived, arrived_one = lax.fori_loop(0, STEPS_DEV, fine_turn, (relaxed, relaxed_zero), unroll=True)
    (level_relaxed,) = evolve(1, relaxed)
    p_out[...] = join(arrived)
    b_out[...] = join(minus(arrived, level_relaxed))
    r_copy = remote(r_out, r_buf, send_r, recv_r, me + 1)
    p_copy = remote(p_out, p_buf, send_p, recv_p, me + 2)
    reach = base + jnp.where(wraps, GROUP, 0)

    def b_copy(i, other):
        return remote(b_out, b_buf.at[slot], send_b.at[i], recv_b.at[slot], other)

    reached_relaxer = relaxer(group + jnp.where(wraps, 1, 0))
    s_copy = remote(r_out, s_buf, send_s, recv_s, reached_relaxer)

    def over_b(act):
        sends = jnp.logical_or(forwards, jnp.logical_not(wraps))

        @pl.when(jnp.logical_and(forwards, member == GROUP - 2))
        def _():
            act(s_copy)

        @pl.when(jnp.logical_and(sends, me != reached_relaxer))
        def _():
            act(b_copy(LEADERS, reached_relaxer))

        for i in range(LEADERS):

            @pl.when(jnp.logical_and(sends, slot <= leader(i)))
            def _():
                act(b_copy(i, reach + leader(i)))

    await_barrier()
    over_b(lambda copy: copy.start())

    @pl.when(me + 2 < devices)
    def _():
        p_copy.start()

    @pl.when(me + 1 < devices)
    def _():
        r_copy.start()

    @pl.when(relaxes)
    def _():
        b_buf[slot] = b_out[...]

    @pl.when(me == 0)
    def _():
        r_buf[...] = zero_packed
        p_buf[...] = zero_packed

    @pl.when(me == 1)
    def _():
        p_buf[...] = join(arrived_one)

    below = member - half - 1
    clients = (below, below + 1, member - 1)

    def u_copy(j):
        return remote(u_buf.at[clients[j]], prior_buf, send_u.at[j], recv_u, base + clients[j])

    def v_copy(j):
        return remote(u_buf.at[clients[j] + 1], end_buf, send_u.at[3 + j], recv_v, base + clients[j])

    def w_copy(j):
        return remote(mine_buf, mine_buf, send_w.at[j], recv_w, base + clients[j])

    def e_copy(i):
        later = (group + 1 + i // LEADERS) * GROUP + GROUP - 1 - 2 * (i % LEADERS)
        mate = GROUP - 1 - (i - listeners)
        mate = base + mate - jnp.where(mate <= member, 1, 0)
        other = jnp.where(i < listeners, later, mate)
        return remote(e_buf.at[group], e_buf.at[group], send_e.at[i], recv_e.at[group], other)

    def start_w():
        for j in range(3):
            w_copy(j).start()

    def await_b(k):
        @pl.when(jnp.logical_and(base + k >= 2, jnp.logical_or(k != slot, wraps)))
        def _():
            remote(b_out, b_buf.at[k], send_b.at[0], recv_b.at[k], me).wait_recv()

    def await_e(other):
        remote(e_buf.at[other], e_buf.at[other], send_e.at[0], recv_e.at[other], me).wait_recv()

    def relax_turn(k, state):
        await_b(k)
        (state,) = evolve(1, state)
        return plus(state, spread(b_buf[k]))

    def coarse_turn(other, before):
        await_e(other)
        (image,) = evolve(2, before)
        return plus(image, spread(e_buf[other]))

    def serve(reached):
        @pl.when(reached == below)
        def _():
            u_copy(0).start()

        @pl.when(reached == below + 2)
        def _():
            u_copy(1).start()
            v_copy(0).start()
            v_copy(1).start()

        @pl.when(reached == member - 1)
        def _():
            u_copy(2).start()

    def relax_pair(n, state):
        return relax_turn(2 * n + 1, relax_turn(2 * n, state))

    def replay_turn(k, state):
        state = relax_turn(k, state)
        u_buf[k + 1] = join(state)
        return state

    def replay_pair(n, state):
        state = replay_turn(2 * n + 1, replay_turn(2 * n, state))
        serve(2 * n + 2)
        return state

    def pick(first, second):
        return tuple(jnp.where(opens, a, b) for a, b in zip(first, second))

    @pl.when(relaxes)
    def _():
        @pl.when(opens)
        def _():
            s_buf[...] = join(start)

        @pl.when(group > 0)
        def _():
            remote(r_out, s_buf, send_s, recv_s, me).wait_recv()

        group_start = spread(s_buf[...])
        (coarse_start,) = evolve(2, group_start)
        opening = pick(arrived_one, group_start)
        closing = lax.fori_loop(jnp.where(opens, 1, 0), GROUP // 2, relax_pair, opening)
        e_buf[group] = join(minus(closing, coarse_start))

        def start_e(i, carry):
            e_copy(i).start()
            return carry

        lax.fori_loop(0, listeners + GROUP - 1, start_e, 0)

    @pl.when(leads)
    def _():
        (coarse_initial,) = evolve(2, start)

        @pl.when(opens)
        def _():
            u_buf[0] = join(start)

        @pl.when(group > 0)
        def _():
            await_e(0)
            first_coarse = plus(coarse_initial, spread(e_buf[0]))
            u_buf[0] = join(lax.fori_loop(1, group, coarse_turn, first_coarse))

        earlier = spread(u_buf[0])
        serve(0)
        await_b(0)
        await_b(1)
        (image,) = evolve(2, earlier)
        (state,) = evolve(1, earlier)
        state = pick(relaxed_zero, plus(state, spread(b_buf[0])))
        u_buf[1] = join(state)
        (state,) = evolve(1, state)
        state = pick(arrived_one, plus(state, spread(b_buf[1])))
        u_buf[2] = join(state)
        serve(2)
        mine_buf[...] = join(image)
        start_w()
        state = lax.fori_loop(1, member // 2, replay_pair, state)
        replay_turn(member - 1, state)
        v_copy(2).start()
        await_b(member)
        prior_buf[...] = u_buf[member]

    follows = jnp.logical_not(leads)

    @pl.when(me >= 1)
    def _():
        remote(r_out, r_buf, send_r, recv_r, me).wait_recv()

    @pl.when(me >= 2)
    def _():
        remote(p_out, p_buf, send_p, recv_p, me).wait_recv()

    stores = [pltpu.make_async_copy(stage.at[i], packed_ref.at[i], save.at[i]) for i in range(PIECES)]

    def put(i, value):
        stage[i] = value
        stores[i].start()

    put(STEPS_DEV, p_buf[...] - r_buf[...])

    @pl.when(follows)
    def _():
        remote(u_buf.at[0], prior_buf, send_u.at[0], recv_u, me).wait_recv()

    prior = spread(prior_buf[...])
    (ending,) = evolve(1, prior)
    ending = join(ending) + b_buf[member]
    point = prior
    for i in range(STEPS_DEV - 1):
        (point,) = evolve(0, point)
        put(i, join(point))

    @pl.when(follows)
    def _():
        remote(u_buf.at[0], end_buf, send_u.at[0], recv_v, me).wait_recv()
        remote(mine_buf, mine_buf, send_w.at[0], recv_w, me).wait_recv()

    @pl.when(jnp.logical_not(relaxes))
    def _():
        await_e(group)

    @pl.when(leads)
    def _():
        end_buf[...] = ending

    ending = end_buf[...]
    mine = mine_buf[...] + e_buf[group]
    last = member == GROUP - 1
    put(STEPS_DEV - 1, jnp.where(last, mine, ending))
    put(STEPS_DEV + 1, mine)
    put(STEPS_DEV + 2, jnp.where(last, ending - mine, 0.0))
    over_b(lambda copy: copy.wait_send())

    @pl.when(me + 2 < devices)
    def _():
        p_copy.wait_send()

    @pl.when(me + 1 < devices)
    def _():
        r_copy.wait_send()

    @pl.when(leads)
    def _():
        for j in range(3):
            u_copy(j).wait_send()
            v_copy(j).wait_send()
            w_copy(j).wait_send()

    @pl.when(relaxes)
    def _():
        def end_e(i, carry):
            e_copy(i).wait_send()
            return carry

        lax.fori_loop(0, listeners + GROUP - 1, end_e, 0)

    for copy in stores:
        copy.wait()


def unpack(packed_ref, traj_ref, resid_ref, coarse_ref, defect_ref):
    cols = packed_ref.shape[2] // 2
    places = [(traj_ref, i) for i in range(STEPS_DEV)] + [(resid_ref, 0), (coarse_ref, 0), (defect_ref, 0)]
    for i, (ref, index) in enumerate(places):
        ref[index, 0] = packed_ref[i, :, :cols]
        ref[index, 1] = packed_ref[i, :, cols:]


assert 4 * LEADERS == GROUP


def shards(devices, initial, coarse_guess, feed_rate, kill_rate):
    rows, cols = initial.shape[1:]
    groups = devices // GROUP
    steps = (interval_time / STEPS_DEV, interval_time, interval_time * GROUP)
    tables = []
    for step in steps:
        tables += [jnp.asarray(table) for table in solve_tables(rows, cols, step)]
    state = (rows, 2 * cols)
    block = (1,) + initial.shape
    dma = pltpu.SemaphoreType.DMA
    whole = pl.BlockSpec(memory_space=pltpu.VMEM)
    remain = pl.BlockSpec(memory_space=pltpu.HBM)
    inputs = (initial, coarse_guess, feed_rate, kill_rate, *tables)
    buffer = pltpu.VMEM(state, jnp.float32)
    packed = pl.pallas_call(
        functools.partial(kernel, devices, (rows, cols)),
        out_shape=jax.ShapeDtypeStruct((PIECES,) + state, jnp.float32),
        in_specs=[remain] * INPUTS,
        out_specs=remain,
        scratch_shapes=[pltpu.VMEM(each.shape, each.dtype) for each in inputs]
        + [
            pltpu.VMEM((9,) + state, jnp.float32),
            pltpu.VMEM((GROUP,) + state, jnp.float32),
            buffer,
            buffer,
            buffer,
            pltpu.VMEM((groups,) + state, jnp.float32),
            pltpu.VMEM((GROUP + 1,) + state, jnp.float32),
        ]
        + [buffer] * 6
        + [pltpu.VMEM((PIECES,) + state, jnp.float32)]
        + [dma((LEADERS + 1,)), dma((GROUP,)), dma, dma]
        + [dma((LEADERS * groups + GROUP,)), dma((groups,)), dma((6,)), dma((3,))]
        + [dma] * 7
        + [dma((INPUTS,)), dma((PIECES,))],
        compiler_params=pltpu.CompilerParams(
            collective_id=0, has_side_effects=True, vmem_limit_bytes=VMEM_GRANT
        ),
    )(*inputs)
    return pl.pallas_call(
        unpack,
        out_shape=[
            jax.ShapeDtypeStruct((STEPS_DEV,) + initial.shape, jnp.float32),
            jax.ShapeDtypeStruct(block, jnp.float32),
            jax.ShapeDtypeStruct(block, jnp.float32),
            jax.ShapeDtypeStruct(block, jnp.float32),
        ],
        in_specs=[whole],
        out_specs=[whole] * 4,
        compiler_params=pltpu.CompilerParams(vmem_limit_bytes=VMEM_GRANT),
    )(packed)


def solution(mesh):
    spread = P("tm", None, None, None)
    return jax.shard_map(
        functools.partial(shards, mesh.shape["tm"]),
        mesh=mesh,
        in_specs=(P(), spread, P(), P()),
        out_specs=(spread, spread, spread, spread),
        check_vma=False,
    )
```

```python
import functools

import jax
import jax.numpy as jnp
import ml_dtypes
import numpy as np
from jax import lax
from jax.experimental import pallas as pl
from jax.experimental.pallas import tpu as pltpu
from jax.sharding import PartitionSpec as P

STEPS_DEV = 4
GROUP = 16
INPUTS = 10
LEADERS = 4
PIECES = STEPS_DEV + 3
VMEM_GRANT = 64000000

diffusion = (0.2, 0.1)
interval_time = 0.03125
MESH = pl.DeviceIdType.MESH
single = np.float32


def cosine_basis(length):
    positions = np.arange(length, dtype=single)
    angles = single(np.pi) * (positions[:, None] + single(0.5)) * positions[None, :] / single(length)
    weight = np.where(positions == 0, np.sqrt(single(1.0 / length)), np.sqrt(single(2.0 / length)))
    return (np.cos(angles) * weight[None, :].astype(single)).astype(single)


def eigen_values(length):
    positions = np.arange(length, dtype=single)
    waves = np.sin(single(np.pi) * positions / single(2.0 * length))
    return (single(-4.0) * waves * waves).astype(single)


def halves(matrix):
    high = matrix.astype(ml_dtypes.bfloat16)
    low = (matrix - high.astype(np.float64)).astype(ml_dtypes.bfloat16)
    return high, low


def factors(rows, cols, time_step, rate, rank):
    basis_rows = cosine_basis(rows).astype(np.float64)
    basis_cols = cosine_basis(cols).astype(np.float64)
    spectrum = eigen_values(rows).astype(np.float64)[:, None] + eigen_values(cols).astype(np.float64)[None, :]
    factor = 1.0 / (1.0 - time_step * rate * spectrum)
    left, sizes, right = np.linalg.svd(factor)
    if rank is None:
        rank = 1
        while np.abs(factor - (left[:, :rank] * sizes[:rank]) @ right[:rank]).max() > 2.0**-26:
            rank += 1
        return rank
    left = left[:, :rank] * np.sqrt(sizes[:rank])
    right = right[:rank].T * np.sqrt(sizes[:rank])
    scale = left[0, 0]
    left[:, 0] /= scale
    right[:, 0] *= scale
    firsts = [basis_rows @ np.diag(left[:, k]) @ basis_rows.T for k in range(rank)]
    seconds = [basis_cols @ np.diag(right[:, k]) @ basis_cols.T for k in range(rank)]
    firsts[0] = firsts[0] - np.eye(rows)
    seconds[0] = seconds[0] - np.eye(cols)
    return firsts, seconds


@functools.lru_cache(maxsize=None)
def solve_tables(rows, cols, time_step):
    rank = max(factors(rows, cols, time_step, rate, None) for rate in diffusion)
    rank = max(rank, 2)
    species = [factors(rows, cols, time_step, rate, rank) for rate in diffusion]
    short = rank == 2
    rights, lefts = [], []
    for firsts, seconds in species:
        highs, lows = [], []
        for second in seconds:
            high, low = halves(second)
            highs += [high] * 2
            lows += [low] * 2
        high = np.concatenate(highs, 1)
        low = np.concatenate(lows, 1)
        rights.append(np.concatenate([high, high, low], 0))
        pairs = [halves(first) for first in firsts]
        highs = [high for high, low in pairs]
        lows = [low for high, low in pairs]
        if short:
            lefts.append(np.concatenate(highs + highs[:1] + lows[:1], 1))
        else:
            lefts.append(np.concatenate(highs + highs + lows, 1))
    return np.stack(rights), np.stack(lefts)


def kernel(devices, sizes, *refs):
    sources = refs[:INPUTS]
    packed_ref = refs[INPUTS]
    held = refs[INPUTS + 1 : 2 * INPUTS + 1]
    (initial_ref, guess_ref, feed_ref, kill_ref) = held[:4]
    table_refs = (held[4:6], held[6:8], held[8:10])
    (rates, b_buf, s_buf, r_buf, p_buf, e_buf, u_buf, prior_buf, end_buf, mine_buf, b_out, r_out, p_out, stage, zero_buf) = refs[
        2 * INPUTS + 1 : 2 * INPUTS + 16
    ]
    (
        send_b, recv_b, send_s, recv_s, send_e, recv_e, send_u, send_w,
        recv_u, recv_v, recv_w, send_r, recv_r, send_p, recv_p, load, save,
    ) = refs[2 * INPUTS + 16 :]
    rows, cols = sizes
    groups = devices // GROUP
    half = GROUP // 2
    me = lax.axis_index("tm")
    group = me // GROUP
    member = me % GROUP
    base = group * GROUP
    slot = (member + 2) % GROUP
    opens = group == 0
    wraps = member >= GROUP - 2
    forwards = jnp.logical_and(wraps, group < groups - 1)
    leads = jnp.logical_and(member >= half, member % 2 == 1)
    relaxes = member == jnp.where(opens, 0, half - 1)
    listeners = LEADERS * (groups - 1 - group)

    loads = [pltpu.make_async_copy(source, target, load.at[i]) for i, (source, target) in enumerate(zip(sources, held))]
    for copy in loads:
        copy.start()

    def leader(i):
        return GROUP - 1 - 2 * i

    barrier = pltpu.get_barrier_semaphore()

    def greet(other):
        pl.semaphore_signal(barrier, inc=1, device_id=(other,), device_id_type=MESH)

    def greet_peer(i, carry):
        greet(base + (member + 1 + i) % GROUP)
        return carry

    def relaxer(other):
        return other * GROUP + jnp.where(other == 0, 0, half - 1)

    def greet_relaxer(other, carry):
        greet(relaxer(other))
        return carry

    @pl.when(leads)
    def _():
        lax.fori_loop(0, group, greet_relaxer, 0)

    @pl.when(jnp.logical_and(jnp.logical_or(leads, relaxes), group > 0))
    def _():
        greet(base - 2)
        greet(base - 1)

    @pl.when(jnp.logical_and(group > 0, member <= 1))
    def _():
        greet(me - 2)

    @pl.when(jnp.logical_and(group > 0, member == 0))
    def _():
        greet(me - 1)

    lax.fori_loop(0, GROUP - 1, greet_peer, 0)

    def await_barrier():
        crossing = jnp.where(forwards, LEADERS + member - (GROUP - 4), 0)
        pl.semaphore_wait(barrier, GROUP - 1 + crossing + jnp.where(relaxes, listeners, 0))

    def remote(source, target, send, recv, other):
        return pltpu.make_async_remote_copy(
            src_ref=source, dst_ref=target, send_sem=send, recv_sem=recv,
            device_id=(other,), device_id_type=MESH,
        )

    left_half = lax.broadcasted_iota(jnp.int32, (rows, 2 * cols), 1) < cols
    fine_step = interval_time / STEPS_DEV
    steps = (fine_step, interval_time, interval_time * GROUP)
    for copy in loads[:6]:
        copy.wait()
    feed = jnp.concatenate([feed_ref[...]] * 2, axis=1)
    kill = jnp.concatenate([kill_ref[...]] * 2, axis=1)
    for level, step in enumerate(steps):
        rates[3 * level] = 1.0 - step * feed
        rates[3 * level + 1] = step * feed
        rates[3 * level + 2] = 1.0 - step * (feed + kill)

    def double(value):
        return jnp.concatenate([value, value], axis=1)

    def join(state):
        return jnp.where(left_half, state[0], state[1])

    def spread(value):
        turned = pltpu.roll(value, cols, 1)
        return jnp.where(left_half, value, turned), jnp.where(left_half, turned, value)

    def plus(state, other):
        return state[0] + other[0], state[1] + other[1]

    def minus(state, other):
        return state[0] - other[0], state[1] - other[1]

    def split(value):
        high = value.astype(jnp.bfloat16)
        low = (value - high.astype(jnp.float32)).astype(jnp.bfloat16)
        return high, low

    def dot(first, second):
        return jnp.dot(first, second, preferred_element_type=jnp.float32)

    def stacked_rows(values):
        return jnp.concatenate(values, 0) if len(values) > 1 else values[0]

    def spectral(level, kind, main):
        count = main.shape[0] // rows
        high = main.astype(jnp.bfloat16)
        wide = high.astype(jnp.float32)
        mixed = jnp.where(stacked_rows([left_half] * count), wide, main - wide).astype(jnp.bfloat16)
        return dot(jnp.concatenate([mixed, high[:, :cols]], 1), table_refs[level][0][kind])

    def gather_terms(main, product):
        count = main.shape[0] // rows
        terms = product.shape[1] // (2 * cols)
        parts = [product[:, 2 * cols * k : 2 * cols * (k + 1)] for k in range(terms)]
        first = main + parts[0]
        parts[0] = first
        columns = []
        for n in range(count):
            pieces = [part[rows * n : rows * (n + 1)] for part in parts]
            if terms == 2:
                first_high, first_low = split(pieces[0])
                stack = [first_high, pieces[1].astype(jnp.bfloat16), first_low, first_high]
            else:
                pairs = [split(piece) for piece in pieces]
                stack = [a for a, b in pairs] + [b for a, b in pairs] + [a for a, b in pairs]
            columns.append(jnp.concatenate(stack, 0))
        return first, jnp.concatenate(columns, 1) if count > 1 else columns[0]

    def solve(level, mains):
        products = [spectral(level, kind, main) for kind, main in enumerate(mains)]
        gathered = [gather_terms(main, product) for main, product in zip(mains, products)]
        smalls = [dot(table_refs[level][1][kind], stack) for kind, (first, stack) in enumerate(gathered)]
        count = mains[0].shape[0] // rows
        return [
            [first[rows * n : rows * (n + 1)] + small[:, 2 * cols * n : 2 * cols * (n + 1)] for n in range(count)]
            for (first, stack), small in zip(gathered, smalls)
        ]

    def evolve(level, *states):
        step = steps[level]
        reacted = ([], [])
        for substrate, catalyst in states:
            uptake = step * (substrate * (catalyst * catalyst))
            reacted[0].append(rates[3 * level] * substrate + rates[3 * level + 1] - uptake)
            reacted[1].append(rates[3 * level + 2] * catalyst + uptake)
        return list(zip(*solve(level, [stacked_rows(values) for values in reacted])))

    start = double(initial_ref[0]), double(initial_ref[1])
    own = double(guess_ref[0, 0]), double(guess_ref[0, 1])

    def fine_turn(unused, states):
        return tuple(evolve(0, *states))

    def prepare(*states):
        relaxed = lax.fori_loop(0, STEPS_DEV, fine_turn, states, unroll=True)
        r_out[...] = join(relaxed[0])
        for copy in loads[6:]:
            copy.wait()
        arrived = lax.fori_loop(0, STEPS_DEV, fine_turn, relaxed, unroll=True)
        (image,) = evolve(1, relaxed[0])
        p_out[...] = join(arrived[0])
        b_out[...] = join(minus(arrived[0], image))
        if len(states) > 1:
            zero_buf[0] = join(relaxed[1])
            zero_buf[1] = join(arrived[1])

    pairs = jnp.logical_and(opens, jnp.logical_or(leads, member <= 1))

    @pl.when(pairs)
    def _():
        prepare(own, start)

    @pl.when(jnp.logical_not(pairs))
    def _():
        prepare(own)

    r_copy = remote(r_out, r_buf, send_r, recv_r, me + 1)
    p_copy = remote(p_out, p_buf, send_p, recv_p, me + 2)
    reach = base + jnp.where(wraps, GROUP, 0)

    def b_copy(i, other):
        return remote(b_out, b_buf.at[slot], send_b.at[i], recv_b.at[slot], other)

    reached_relaxer = relaxer(group + jnp.where(wraps, 1, 0))
    s_copy = remote(r_out, s_buf, send_s, recv_s, reached_relaxer)

    sends = jnp.logical_or(forwards, jnp.logical_not(wraps))
    defers = me < 0

    def over_relaxer(act):
        @pl.when(jnp.logical_and(forwards, member == GROUP - 2))
        def _():
            act(s_copy)

        @pl.when(jnp.logical_and(sends, me != reached_relaxer))
        def _():
            act(b_copy(LEADERS, reached_relaxer))

    def over_leaders(act, where):
        for i in range(LEADERS):

            @pl.when(jnp.logical_and(jnp.logical_and(sends, where), slot <= leader(i)))
            def _():
                act(b_copy(i, reach + leader(i)))

    await_barrier()

    @pl.when(jnp.logical_not(defers))
    def _():
        over_relaxer(lambda copy: copy.start())

    over_leaders(lambda copy: copy.start(), me >= 0)

    @pl.when(defers)
    def _():
        over_leaders(lambda copy: copy.wait_send(), me >= 0)
        over_relaxer(lambda copy: copy.start())

    @pl.when(me + 2 < devices)
    def _():
        p_copy.start()

    @pl.when(me + 1 < devices)
    def _():
        r_copy.start()

    @pl.when(relaxes)
    def _():
        b_buf[slot] = b_out[...]

    @pl.when(me == 0)
    def _():
        r_buf[...] = zero_buf[0]
        p_buf[...] = zero_buf[0]

    @pl.when(me == 1)
    def _():
        p_buf[...] = zero_buf[1]

    below = member - half - 1
    clients = (below, below + 1, member - 1)

    def u_copy(j):
        return remote(u_buf.at[clients[j]], prior_buf, send_u.at[j], recv_u, base + clients[j])

    def v_copy(j):
        return remote(u_buf.at[clients[j] + 1], end_buf, send_u.at[3 + j], recv_v, base + clients[j])

    def w_copy(j):
        return remote(mine_buf, mine_buf, send_w.at[j], recv_w, base + clients[j])

    def e_copy(i):
        later = (group + 1 + i // LEADERS) * GROUP + GROUP - 1 - 2 * (i % LEADERS)
        mate = GROUP - 1 - (i - listeners)
        mate = base + mate - jnp.where(mate <= member, 1, 0)
        other = jnp.where(i < listeners, later, mate)
        return remote(e_buf.at[group], e_buf.at[group], send_e.at[i], recv_e.at[group], other)

    def start_w():
        for j in range(3):
            w_copy(j).start()

    def await_b(k):
        @pl.when(jnp.logical_and(base + k >= 2, jnp.logical_or(k != slot, wraps)))
        def _():
            remote(b_out, b_buf.at[k], send_b.at[0], recv_b.at[k], me).wait_recv()

    def await_e(other):
        remote(e_buf.at[other], e_buf.at[other], send_e.at[0], recv_e.at[other], me).wait_recv()

    def relax_turn(k, state):
        await_b(k)
        (state,) = evolve(1, state)
        return plus(state, spread(b_buf[k]))

    def coarse_turn(other, before):
        await_e(other)
        (image,) = evolve(2, before)
        return plus(image, spread(e_buf[other]))

    def serve(reached):
        @pl.when(reached == below)
        def _():
            u_copy(0).start()

        @pl.when(reached == below + 1)
        def _():
            u_copy(1).start()
            v_copy(0).start()

        @pl.when(reached == below + 2)
        def _():
            v_copy(1).start()

    def relax_pair(n, state):
        return relax_turn(2 * n + 1, relax_turn(2 * n, state))

    def replay_turn(k, state):
        state = relax_turn(k, state)
        u_buf[k + 1] = join(state)
        return state

    def replay_pair(n, state):
        return replay_turn(2 * n + 1, replay_turn(2 * n, state))

    def serving_turn(k, state):
        state = replay_turn(k, state)
        serve(k + 1)
        return state

    def pick(first, second):
        return tuple(jnp.where(opens, a, b) for a, b in zip(first, second))

    @pl.when(relaxes)
    def _():
        @pl.when(opens)
        def _():
            s_buf[...] = join(start)

        @pl.when(group > 0)
        def _():
            remote(r_out, s_buf, send_s, recv_s, me).wait_recv()

        group_start = spread(s_buf[...])
        (coarse_start,) = evolve(2, group_start)
        opening = pick(spread(zero_buf[1]), group_start)
        closing = lax.fori_loop(jnp.where(opens, 1, 0), GROUP // 2, relax_pair, opening)
        e_buf[group] = join(minus(closing, coarse_start))

        def start_e(i, carry):
            e_copy(i).start()
            return carry

        lax.fori_loop(0, listeners + GROUP - 1, start_e, 0)

    @pl.when(leads)
    def _():
        (coarse_initial,) = evolve(2, start)

        @pl.when(opens)
        def _():
            u_buf[0] = join(start)

        @pl.when(group > 0)
        def _():
            await_e(0)
            first_coarse = plus(coarse_initial, spread(e_buf[0]))
            u_buf[0] = join(lax.fori_loop(1, group, coarse_turn, first_coarse))

        earlier = spread(u_buf[0])
        serve(0)
        await_b(0)
        await_b(1)
        (image,) = evolve(2, earlier)
        (state,) = evolve(1, earlier)
        state = pick(spread(zero_buf[0]), plus(state, spread(b_buf[0])))
        u_buf[1] = join(state)
        serve(1)
        (state,) = evolve(1, state)
        state = pick(spread(zero_buf[1]), plus(state, spread(b_buf[1])))
        u_buf[2] = join(state)
        serve(2)
        mine_buf[...] = join(image)
        start_w()
        state = lax.fori_loop(1, below // 2, replay_pair, state)

        @pl.when(below > 2)
        def _():
            serve(below)

        state = lax.fori_loop(jnp.maximum(below, 2), below + 2, serving_turn, state)
        state = lax.fori_loop(below // 2 + 1, member // 2, replay_pair, state)
        u_copy(2).start()
        replay_turn(member - 1, state)
        v_copy(2).start()
        await_b(member)
        prior_buf[...] = u_buf[member]

    follows = jnp.logical_not(leads)

    @pl.when(me >= 1)
    def _():
        remote(r_out, r_buf, send_r, recv_r, me).wait_recv()

    @pl.when(me >= 2)
    def _():
        remote(p_out, p_buf, send_p, recv_p, me).wait_recv()

    stores = [pltpu.make_async_copy(stage.at[i], packed_ref.at[i], save.at[i]) for i in range(PIECES)]

    def put(i, value):
        stage[i] = value
        stores[i].start()

    put(STEPS_DEV, p_buf[...] - r_buf[...])

    @pl.when(follows)
    def _():
        remote(u_buf.at[0], prior_buf, send_u.at[0], recv_u, me).wait_recv()

    prior = spread(prior_buf[...])
    (ending,) = evolve(1, prior)
    ending = join(ending) + b_buf[member]
    point = prior
    for i in range(STEPS_DEV - 1):
        (point,) = evolve(0, point)
        put(i, join(point))

    @pl.when(follows)
    def _():
        remote(u_buf.at[0], end_buf, send_u.at[0], recv_v, me).wait_recv()
        remote(mine_buf, mine_buf, send_w.at[0], recv_w, me).wait_recv()

    @pl.when(jnp.logical_not(relaxes))
    def _():
        await_e(group)

    @pl.when(leads)
    def _():
        end_buf[...] = ending

    ending = end_buf[...]
    mine = mine_buf[...] + e_buf[group]
    last = member == GROUP - 1
    put(STEPS_DEV - 1, jnp.where(last, mine, ending))
    put(STEPS_DEV + 1, mine)
    put(STEPS_DEV + 2, jnp.where(last, ending - mine, 0.0))
    over_relaxer(lambda copy: copy.wait_send())
    over_leaders(lambda copy: copy.wait_send(), jnp.logical_not(defers))

    @pl.when(me + 2 < devices)
    def _():
        p_copy.wait_send()

    @pl.when(me + 1 < devices)
    def _():
        r_copy.wait_send()

    @pl.when(leads)
    def _():
        for j in range(3):
            u_copy(j).wait_send()
            v_copy(j).wait_send()
            w_copy(j).wait_send()

    @pl.when(relaxes)
    def _():
        def end_e(i, carry):
            e_copy(i).wait_send()
            return carry

        lax.fori_loop(0, listeners + GROUP - 1, end_e, 0)

    for copy in stores:
        copy.wait()


def unpack(packed_ref, traj_ref, resid_ref, coarse_ref, defect_ref):
    cols = packed_ref.shape[2] // 2
    places = [(traj_ref, i) for i in range(STEPS_DEV)] + [(resid_ref, 0), (coarse_ref, 0), (defect_ref, 0)]
    for i, (ref, index) in enumerate(places):
        ref[index, 0] = packed_ref[i, :, :cols]
        ref[index, 1] = packed_ref[i, :, cols:]


assert 4 * LEADERS == GROUP


def shards(devices, initial, coarse_guess, feed_rate, kill_rate):
    rows, cols = initial.shape[1:]
    groups = devices // GROUP
    steps = (interval_time / STEPS_DEV, interval_time, interval_time * GROUP)
    tables = []
    for step in steps:
        tables += [jnp.asarray(table) for table in solve_tables(rows, cols, step)]
    state = (rows, 2 * cols)
    block = (1,) + initial.shape
    dma = pltpu.SemaphoreType.DMA
    whole = pl.BlockSpec(memory_space=pltpu.VMEM)
    remain = pl.BlockSpec(memory_space=pltpu.HBM)
    inputs = (initial, coarse_guess, feed_rate, kill_rate, *tables)
    buffer = pltpu.VMEM(state, jnp.float32)
    packed = pl.pallas_call(
        functools.partial(kernel, devices, (rows, cols)),
        out_shape=jax.ShapeDtypeStruct((PIECES,) + state, jnp.float32),
        in_specs=[remain] * INPUTS,
        out_specs=remain,
        scratch_shapes=[pltpu.VMEM(each.shape, each.dtype) for each in inputs]
        + [
            pltpu.VMEM((9,) + state, jnp.float32),
            pltpu.VMEM((GROUP,) + state, jnp.float32),
            buffer,
            buffer,
            buffer,
            pltpu.VMEM((groups,) + state, jnp.float32),
            pltpu.VMEM((GROUP + 1,) + state, jnp.float32),
        ]
        + [buffer] * 6
        + [pltpu.VMEM((PIECES,) + state, jnp.float32), pltpu.VMEM((2,) + state, jnp.float32)]
        + [dma((LEADERS + 1,)), dma((GROUP,)), dma, dma]
        + [dma((LEADERS * groups + GROUP,)), dma((groups,)), dma((6,)), dma((3,))]
        + [dma] * 7
        + [dma((INPUTS,)), dma((PIECES,))],
        compiler_params=pltpu.CompilerParams(
            collective_id=0, has_side_effects=True, vmem_limit_bytes=VMEM_GRANT
        ),
    )(*inputs)
    return pl.pallas_call(
        unpack,
        out_shape=[
            jax.ShapeDtypeStruct((STEPS_DEV,) + initial.shape, jnp.float32),
            jax.ShapeDtypeStruct(block, jnp.float32),
            jax.ShapeDtypeStruct(block, jnp.float32),
            jax.ShapeDtypeStruct(block, jnp.float32),
        ],
        in_specs=[whole],
        out_specs=[whole] * 4,
        compiler_params=pltpu.CompilerParams(vmem_limit_bytes=VMEM_GRANT),
    )(packed)


def solution(mesh):
    spread = P("tm", None, None, None)
    return jax.shard_map(
        functools.partial(shards, mesh.shape["tm"]),
        mesh=mesh,
        in_specs=(P(), spread, P(), P()),
        out_specs=(spread, spread, spread, spread),
        check_vma=False,
    )
```

```python
import functools

import jax
import jax.numpy as jnp
import ml_dtypes
import numpy as np
from jax import lax
from jax.experimental import pallas as pl
from jax.experimental.pallas import tpu as pltpu
from jax.sharding import PartitionSpec as P

STEPS_DEV = 4
GROUP = 16
INPUTS = 10
LEADERS = 4
PIECES = STEPS_DEV + 3
VMEM_GRANT = 16 * 2**20

diffusion = (0.2, 0.1)
interval_time = 0.03125
MESH = pl.DeviceIdType.MESH
single = np.float32


def cosine_basis(length):
    positions = np.arange(length, dtype=single)
    angles = single(np.pi) * (positions[:, None] + single(0.5)) * positions[None, :] / single(length)
    weight = np.where(positions == 0, np.sqrt(single(1.0 / length)), np.sqrt(single(2.0 / length)))
    return (np.cos(angles) * weight[None, :].astype(single)).astype(single)


def eigen_values(length):
    positions = np.arange(length, dtype=single)
    waves = np.sin(single(np.pi) * positions / single(2.0 * length))
    return (single(-4.0) * waves * waves).astype(single)


def halves(matrix):
    high = matrix.astype(ml_dtypes.bfloat16)
    low = (matrix - high.astype(np.float64)).astype(ml_dtypes.bfloat16)
    return high, low


def factors(rows, cols, time_step, rate, rank):
    basis_rows = cosine_basis(rows).astype(np.float64)
    basis_cols = cosine_basis(cols).astype(np.float64)
    spectrum = eigen_values(rows).astype(np.float64)[:, None] + eigen_values(cols).astype(np.float64)[None, :]
    factor = 1.0 / (1.0 - time_step * rate * spectrum)
    left, sizes, right = np.linalg.svd(factor)
    if rank is None:
        rank = 1
        while np.abs(factor - (left[:, :rank] * sizes[:rank]) @ right[:rank]).max() > 2.0**-26:
            rank += 1
        return rank
    left = left[:, :rank] * np.sqrt(sizes[:rank])
    right = right[:rank].T * np.sqrt(sizes[:rank])
    scale = left[0, 0]
    left[:, 0] /= scale
    right[:, 0] *= scale
    firsts = [basis_rows @ np.diag(left[:, k]) @ basis_rows.T for k in range(rank)]
    seconds = [basis_cols @ np.diag(right[:, k]) @ basis_cols.T for k in range(rank)]
    firsts[0] = firsts[0] - np.eye(rows)
    seconds[0] = seconds[0] - np.eye(cols)
    return firsts, seconds


@functools.lru_cache(maxsize=None)
def solve_tables(rows, cols, time_step):
    rank = max(factors(rows, cols, time_step, rate, None) for rate in diffusion)
    rank = max(rank, 2)
    species = [factors(rows, cols, time_step, rate, rank) for rate in diffusion]
    short = rank == 2
    rights, lefts = [], []
    for firsts, seconds in species:
        highs, lows = [], []
        for second in seconds:
            high, low = halves(second)
            highs += [high] * 2
            lows += [low] * 2
        high = np.concatenate(highs, 1)
        low = np.concatenate(lows, 1)
        rights.append(np.concatenate([high, high, low], 0))
        pairs = [halves(first) for first in firsts]
        highs = [high for high, low in pairs]
        lows = [low for high, low in pairs]
        if short:
            lefts.append(np.concatenate(highs + highs[:1] + lows[:1], 1))
        else:
            lefts.append(np.concatenate(highs + highs + lows, 1))
    return np.stack(rights), np.stack(lefts)


def kernel(devices, sizes, *refs):
    sources = refs[:INPUTS]
    packed_ref = refs[INPUTS]
    held = refs[INPUTS + 1 : 2 * INPUTS + 1]
    (initial_ref, guess_ref, feed_ref, kill_ref) = held[:4]
    table_refs = (held[4:6], held[6:8], held[8:10])
    (rates, b_buf, s_buf, r_buf, p_buf, e_buf, u_buf, prior_buf, end_buf, mine_buf, b_out, r_out, p_out, zero_buf) = refs[
        2 * INPUTS + 1 : 2 * INPUTS + 15
    ]
    (
        send_b, recv_b, send_s, recv_s, send_e, recv_e, send_u, send_w,
        recv_u, recv_v, recv_w, send_r, recv_r, send_p, recv_p, load,
    ) = refs[2 * INPUTS + 15 :]
    rows, cols = sizes
    groups = devices // GROUP
    half = GROUP // 2
    me = lax.axis_index("tm")
    group = me // GROUP
    member = me % GROUP
    base = group * GROUP
    slot = (member + 2) % GROUP
    opens = group == 0
    wraps = member >= GROUP - 2
    forwards = jnp.logical_and(wraps, group < groups - 1)
    leads = jnp.logical_and(member >= half, member % 2 == 1)
    relaxes = member == jnp.where(opens, 0, half - 1)
    listeners = LEADERS * (groups - 1 - group)

    loads = [pltpu.make_async_copy(source, target, load.at[i]) for i, (source, target) in enumerate(zip(sources, held))]
    for copy in loads:
        copy.start()

    def leader(i):
        return GROUP - 1 - 2 * i

    barrier = pltpu.get_barrier_semaphore()

    def greet(other):
        pl.semaphore_signal(barrier, inc=1, device_id=(other,), device_id_type=MESH)

    def greet_peer(i, carry):
        greet(base + (member + 1 + i) % GROUP)
        return carry

    def relaxer(other):
        return other * GROUP + jnp.where(other == 0, 0, half - 1)

    def greet_relaxer(other, carry):
        greet(relaxer(other))
        return carry

    @pl.when(leads)
    def _():
        lax.fori_loop(0, group, greet_relaxer, 0)

    @pl.when(jnp.logical_and(jnp.logical_or(leads, relaxes), group > 0))
    def _():
        greet(base - 2)
        greet(base - 1)

    @pl.when(jnp.logical_and(group > 0, member <= 1))
    def _():
        greet(me - 2)

    @pl.when(jnp.logical_and(group > 0, member == 0))
    def _():
        greet(me - 1)

    lax.fori_loop(0, GROUP - 1, greet_peer, 0)

    def await_barrier():
        crossing = jnp.where(forwards, LEADERS + member - (GROUP - 4), 0)
        pl.semaphore_wait(barrier, GROUP - 1 + crossing + jnp.where(relaxes, listeners, 0))

    def remote(source, target, send, recv, other):
        return pltpu.make_async_remote_copy(
            src_ref=source, dst_ref=target, send_sem=send, recv_sem=recv,
            device_id=(other,), device_id_type=MESH,
        )

    left_half = lax.broadcasted_iota(jnp.int32, (rows, 2 * cols), 1) < cols
    fine_step = interval_time / STEPS_DEV
    steps = (fine_step, interval_time, interval_time * GROUP)
    for copy in loads[:6]:
        copy.wait()
    feed = jnp.concatenate([feed_ref[...]] * 2, axis=1)
    kill = jnp.concatenate([kill_ref[...]] * 2, axis=1)
    for level, step in enumerate(steps):
        rates[3 * level] = 1.0 - step * feed
        rates[3 * level + 1] = step * feed
        rates[3 * level + 2] = 1.0 - step * (feed + kill)

    def double(value):
        return jnp.concatenate([value, value], axis=1)

    def join(state):
        return jnp.where(left_half, state[0], state[1])

    def spread(value):
        turned = pltpu.roll(value, cols, 1)
        return jnp.where(left_half, value, turned), jnp.where(left_half, turned, value)

    def plus(state, other):
        return state[0] + other[0], state[1] + other[1]

    def minus(state, other):
        return state[0] - other[0], state[1] - other[1]

    def split(value):
        high = value.astype(jnp.bfloat16)
        low = (value - high.astype(jnp.float32)).astype(jnp.bfloat16)
        return high, low

    def dot(first, second):
        return jnp.dot(first, second, preferred_element_type=jnp.float32)

    def stacked_rows(values):
        return jnp.concatenate(values, 0) if len(values) > 1 else values[0]

    def spectral(level, kind, main):
        count = main.shape[0] // rows
        high = main.astype(jnp.bfloat16)
        wide = high.astype(jnp.float32)
        mixed = jnp.where(stacked_rows([left_half] * count), wide, main - wide).astype(jnp.bfloat16)
        return dot(jnp.concatenate([mixed, high[:, :cols]], 1), table_refs[level][0][kind])

    def gather_terms(main, product):
        count = main.shape[0] // rows
        terms = product.shape[1] // (2 * cols)
        parts = [product[:, 2 * cols * k : 2 * cols * (k + 1)] for k in range(terms)]
        first = main + parts[0]
        parts[0] = first
        columns = []
        for n in range(count):
            pieces = [part[rows * n : rows * (n + 1)] for part in parts]
            if terms == 2:
                first_high, first_low = split(pieces[0])
                stack = [first_high, pieces[1].astype(jnp.bfloat16), first_low, first_high]
            else:
                pairs = [split(piece) for piece in pieces]
                stack = [a for a, b in pairs] + [b for a, b in pairs] + [a for a, b in pairs]
            columns.append(jnp.concatenate(stack, 0))
        return first, jnp.concatenate(columns, 1) if count > 1 else columns[0]

    def solve(level, mains):
        products = [spectral(level, kind, main) for kind, main in enumerate(mains)]
        gathered = [gather_terms(main, product) for main, product in zip(mains, products)]
        smalls = [dot(table_refs[level][1][kind], stack) for kind, (first, stack) in enumerate(gathered)]
        count = mains[0].shape[0] // rows
        return [
            [first[rows * n : rows * (n + 1)] + small[:, 2 * cols * n : 2 * cols * (n + 1)] for n in range(count)]
            for (first, stack), small in zip(gathered, smalls)
        ]

    def evolve(level, *states):
        step = steps[level]
        reacted = ([], [])
        for substrate, catalyst in states:
            uptake = step * (substrate * (catalyst * catalyst))
            reacted[0].append(rates[3 * level] * substrate + rates[3 * level + 1] - uptake)
            reacted[1].append(rates[3 * level + 2] * catalyst + uptake)
        return list(zip(*solve(level, [stacked_rows(values) for values in reacted])))

    start = double(initial_ref[0]), double(initial_ref[1])
    own = double(guess_ref[0, 0]), double(guess_ref[0, 1])

    def fine_turn(unused, states):
        return tuple(evolve(0, *states))

    def prepare(*states):
        relaxed = lax.fori_loop(0, STEPS_DEV, fine_turn, states, unroll=True)
        r_out[...] = join(relaxed[0])
        for copy in loads[6:]:
            copy.wait()
        arrived = lax.fori_loop(0, STEPS_DEV, fine_turn, relaxed, unroll=True)
        (image,) = evolve(1, relaxed[0])
        p_out[...] = join(arrived[0])
        b_out[...] = join(minus(arrived[0], image))
        if len(states) > 1:
            zero_buf[0] = join(relaxed[1])
            zero_buf[1] = join(arrived[1])

    pairs = jnp.logical_and(opens, jnp.logical_or(member >= half, member <= 1))

    @pl.when(pairs)
    def _():
        prepare(own, start)

    @pl.when(jnp.logical_not(pairs))
    def _():
        prepare(own)

    r_copy = remote(r_out, r_buf, send_r, recv_r, me + 1)
    p_copy = remote(p_out, p_buf, send_p, recv_p, me + 2)
    reach = base + jnp.where(wraps, GROUP, 0)

    def b_copy(i, other):
        return remote(b_out, b_buf.at[slot], send_b.at[i], recv_b.at[slot], other)

    reached_relaxer = relaxer(group + jnp.where(wraps, 1, 0))
    s_copy = remote(r_out, s_buf, send_s, recv_s, reached_relaxer)

    sends = jnp.logical_or(forwards, jnp.logical_not(wraps))
    defers = me < 0

    def over_relaxer(act):
        @pl.when(jnp.logical_and(forwards, member == GROUP - 2))
        def _():
            act(s_copy)

        @pl.when(jnp.logical_and(sends, me != reached_relaxer))
        def _():
            act(b_copy(LEADERS, reached_relaxer))

    def over_leaders(act, where):
        for i in range(LEADERS):

            @pl.when(jnp.logical_and(jnp.logical_and(sends, where), slot <= leader(i)))
            def _():
                act(b_copy(i, reach + leader(i)))

    await_barrier()

    @pl.when(jnp.logical_not(defers))
    def _():
        over_relaxer(lambda copy: copy.start())

    over_leaders(lambda copy: copy.start(), me >= 0)

    @pl.when(defers)
    def _():
        over_leaders(lambda copy: copy.wait_send(), me >= 0)
        over_relaxer(lambda copy: copy.start())

    @pl.when(me + 2 < devices)
    def _():
        p_copy.start()

    @pl.when(me + 1 < devices)
    def _():
        r_copy.start()

    @pl.when(relaxes)
    def _():
        pltpu.make_async_copy(b_out, b_buf.at[slot], recv_b.at[slot]).start()

    @pl.when(me == 0)
    def _():
        r_buf[...] = zero_buf[0]
        p_buf[...] = zero_buf[0]

    @pl.when(me == 1)
    def _():
        p_buf[...] = zero_buf[1]

    below = member - half - 1
    clients = (below, below + 1, member - 1)

    def u_copy(j):
        return remote(u_buf.at[clients[j]], prior_buf, send_u.at[j], recv_u, base + clients[j])

    def v_copy(j):
        return remote(u_buf.at[clients[j] + 1], end_buf, send_u.at[3 + j], recv_v, base + clients[j])

    def w_copy(j):
        return remote(mine_buf, mine_buf, send_w.at[j], recv_w, base + clients[j])

    def e_copy(i):
        later = (group + 1 + i // LEADERS) * GROUP + GROUP - 1 - 2 * (i % LEADERS)
        mate = GROUP - 1 - (i - listeners)
        mate = base + mate - jnp.where(mate <= member, 1, 0)
        other = jnp.where(i < listeners, later, mate)
        return remote(e_buf.at[group], e_buf.at[group], send_e.at[i], recv_e.at[group], other)

    def start_w():
        for j in range(3):
            w_copy(j).start()

    def await_b(k):
        remote(b_out, b_buf.at[k], send_b.at[0], recv_b.at[k], me).wait_recv()

    def await_e(other):
        remote(e_buf.at[other], e_buf.at[other], send_e.at[0], recv_e.at[other], me).wait_recv()

    def relax_turn(k, state):
        await_b(k)
        (state,) = evolve(1, state)
        return plus(state, spread(b_buf[k]))

    def coarse_turn(other, before):
        await_e(other)
        (image,) = evolve(2, before)
        return plus(image, spread(e_buf[other]))

    def serve(reached):
        @pl.when(reached == below)
        def _():
            u_copy(0).start()

        @pl.when(reached == below + 1)
        def _():
            u_copy(1).start()
            v_copy(0).start()

        @pl.when(reached == below + 2)
        def _():
            v_copy(1).start()

    def relax_pair(n, state):
        return relax_turn(2 * n + 1, relax_turn(2 * n, state))

    def replay_turn(k, state):
        state = relax_turn(k, state)
        u_buf[k + 1] = join(state)
        return state

    def replay_pair(n, state):
        return replay_turn(2 * n + 1, replay_turn(2 * n, state))

    def serving_turn(k, state):
        state = replay_turn(k, state)
        serve(k + 1)
        return state

    def pick(first, second):
        return tuple(jnp.where(opens, a, b) for a, b in zip(first, second))

    @pl.when(relaxes)
    def _():
        @pl.when(opens)
        def _():
            s_buf[...] = join(start)

        @pl.when(group > 0)
        def _():
            remote(r_out, s_buf, send_s, recv_s, me).wait_recv()

        group_start = spread(s_buf[...])
        (coarse_start,) = evolve(2, group_start)
        opening = pick(spread(zero_buf[1]), group_start)
        closing = lax.fori_loop(jnp.where(opens, 1, 0), GROUP // 2, relax_pair, opening)
        e_buf[group] = join(minus(closing, coarse_start))

        def start_e(i, carry):
            e_copy(i).start()
            return carry

        lax.fori_loop(0, listeners + GROUP - 1, start_e, 0)

    @pl.when(leads)
    def _():
        (coarse_initial,) = evolve(2, start)

        @pl.when(opens)
        def _():
            u_buf[0] = join(start)

        @pl.when(group > 0)
        def _():
            await_e(0)
            first_coarse = plus(coarse_initial, spread(e_buf[0]))
            u_buf[0] = join(lax.fori_loop(1, group, coarse_turn, first_coarse))

        earlier = spread(u_buf[0])
        serve(0)

        @pl.when(group > 0)
        def _():
            await_b(0)
            await_b(1)

        (image,) = evolve(2, earlier)
        (state,) = evolve(1, earlier)
        state = pick(spread(zero_buf[0]), plus(state, spread(b_buf[0])))
        u_buf[1] = join(state)
        serve(1)
        (state,) = evolve(1, state)
        state = pick(spread(zero_buf[1]), plus(state, spread(b_buf[1])))
        u_buf[2] = join(state)
        serve(2)
        mine_buf[...] = join(image)
        start_w()
        state = lax.fori_loop(1, below // 2, replay_pair, state)

        @pl.when(below > 2)
        def _():
            serve(below)

        state = lax.fori_loop(jnp.maximum(below, 2), below + 2, serving_turn, state)
        state = lax.fori_loop(below // 2 + 1, member // 2, replay_pair, state)
        u_copy(2).start()
        replay_turn(member - 1, state)
        v_copy(2).start()
        await_b(member)
        prior_buf[...] = u_buf[member]

    follows = jnp.logical_not(leads)

    @pl.when(me >= 1)
    def _():
        remote(r_out, r_buf, send_r, recv_r, me).wait_recv()

    @pl.when(me >= 2)
    def _():
        remote(p_out, p_buf, send_p, recv_p, me).wait_recv()

    packed_ref[STEPS_DEV] = p_buf[...] - r_buf[...]

    @pl.when(follows)
    def _():
        remote(u_buf.at[0], prior_buf, send_u.at[0], recv_u, me).wait_recv()

    prior = spread(prior_buf[...])
    (ending,) = evolve(1, prior)
    ending = join(ending) + b_buf[member]
    point = prior
    for i in range(STEPS_DEV - 1):
        (point,) = evolve(0, point)
        packed_ref[i] = join(point)

    @pl.when(follows)
    def _():
        remote(u_buf.at[0], end_buf, send_u.at[0], recv_v, me).wait_recv()
        remote(mine_buf, mine_buf, send_w.at[0], recv_w, me).wait_recv()

    @pl.when(jnp.logical_not(relaxes))
    def _():
        await_e(group)

    @pl.when(leads)
    def _():
        end_buf[...] = ending

    ending = end_buf[...]
    mine = mine_buf[...] + e_buf[group]
    last = member == GROUP - 1
    packed_ref[STEPS_DEV - 1] = jnp.where(last, mine, ending)
    packed_ref[STEPS_DEV + 1] = mine
    packed_ref[STEPS_DEV + 2] = jnp.where(last, ending - mine, 0.0)
    over_relaxer(lambda copy: copy.wait_send())
    over_leaders(lambda copy: copy.wait_send(), jnp.logical_not(defers))

    @pl.when(me + 2 < devices)
    def _():
        p_copy.wait_send()

    @pl.when(me + 1 < devices)
    def _():
        r_copy.wait_send()

    @pl.when(leads)
    def _():
        for j in range(3):
            u_copy(j).wait_send()
            v_copy(j).wait_send()
            w_copy(j).wait_send()

    @pl.when(relaxes)
    def _():
        def end_e(i, carry):
            e_copy(i).wait_send()
            return carry

        lax.fori_loop(0, listeners + GROUP - 1, end_e, 0)


def unpack(packed_ref, traj_ref, resid_ref, coarse_ref, defect_ref):
    cols = packed_ref.shape[2] // 2
    places = [(traj_ref, i) for i in range(STEPS_DEV)] + [(resid_ref, 0), (coarse_ref, 0), (defect_ref, 0)]
    for i, (ref, index) in enumerate(places):
        ref[index, 0] = packed_ref[i, :, :cols]
        ref[index, 1] = packed_ref[i, :, cols:]


assert 4 * LEADERS == GROUP


def shards(devices, initial, coarse_guess, feed_rate, kill_rate):
    rows, cols = initial.shape[1:]
    groups = devices // GROUP
    steps = (interval_time / STEPS_DEV, interval_time, interval_time * GROUP)
    tables = []
    for step in steps:
        tables += [jnp.asarray(table) for table in solve_tables(rows, cols, step)]
    state = (rows, 2 * cols)
    block = (1,) + initial.shape
    dma = pltpu.SemaphoreType.DMA
    whole = pl.BlockSpec(memory_space=pltpu.VMEM)
    remain = pl.BlockSpec(memory_space=pltpu.HBM)
    inputs = (initial, coarse_guess, feed_rate, kill_rate, *tables)
    buffer = pltpu.VMEM(state, jnp.float32)
    packed = pl.pallas_call(
        functools.partial(kernel, devices, (rows, cols)),
        out_shape=jax.ShapeDtypeStruct((PIECES,) + state, jnp.float32),
        in_specs=[remain] * INPUTS,
        out_specs=whole,
        scratch_shapes=[pltpu.VMEM(each.shape, each.dtype) for each in inputs]
        + [
            pltpu.VMEM((9,) + state, jnp.float32),
            pltpu.VMEM((GROUP,) + state, jnp.float32),
            buffer,
            buffer,
            buffer,
            pltpu.VMEM((groups,) + state, jnp.float32),
            pltpu.VMEM((GROUP + 1,) + state, jnp.float32),
        ]
        + [buffer] * 6
        + [pltpu.VMEM((2,) + state, jnp.float32)]
        + [dma((LEADERS + 1,)), dma((GROUP,)), dma, dma]
        + [dma((LEADERS * groups + GROUP,)), dma((groups,)), dma((6,)), dma((3,))]
        + [dma] * 7
        + [dma((INPUTS,))],
        compiler_params=pltpu.CompilerParams(
            collective_id=0, has_side_effects=True, vmem_limit_bytes=VMEM_GRANT
        ),
    )(*[pltpu.with_memory_space_constraint(each, pltpu.HBM) for each in inputs])
    return pl.pallas_call(
        unpack,
        out_shape=[
            jax.ShapeDtypeStruct((STEPS_DEV,) + initial.shape, jnp.float32),
            jax.ShapeDtypeStruct(block, jnp.float32),
            jax.ShapeDtypeStruct(block, jnp.float32),
            jax.ShapeDtypeStruct(block, jnp.float32),
        ],
        in_specs=[whole],
        out_specs=[whole] * 4,
        compiler_params=pltpu.CompilerParams(vmem_limit_bytes=VMEM_GRANT),
    )(pltpu.with_memory_space_constraint(packed, pltpu.VMEM))


def solution(mesh):
    spread = P("tm", None, None, None)
    return jax.shard_map(
        functools.partial(shards, mesh.shape["tm"]),
        mesh=mesh,
        in_specs=(P(), spread, P(), P()),
        out_specs=(spread, spread, spread, spread),
        check_vma=False,
    )
```

```python
import functools

import jax
import jax.numpy as jnp
import ml_dtypes
import numpy as np
from jax import lax
from jax.experimental import pallas as pl
from jax.experimental.pallas import tpu as pltpu
from jax.sharding import PartitionSpec as P

STEPS_DEV = 4
GROUP = 16
INPUTS = 10
LEADERS = 4
PIECES = STEPS_DEV + 3
VMEM_GRANT = 16 * 2**20

diffusion = (0.2, 0.1)
interval_time = 0.03125
MESH = pl.DeviceIdType.MESH
single = np.float32


def cosine_basis(length):
    positions = np.arange(length, dtype=single)
    angles = single(np.pi) * (positions[:, None] + single(0.5)) * positions[None, :] / single(length)
    weight = np.where(positions == 0, np.sqrt(single(1.0 / length)), np.sqrt(single(2.0 / length)))
    return (np.cos(angles) * weight[None, :].astype(single)).astype(single)


def eigen_values(length):
    positions = np.arange(length, dtype=single)
    waves = np.sin(single(np.pi) * positions / single(2.0 * length))
    return (single(-4.0) * waves * waves).astype(single)


def halves(matrix):
    high = matrix.astype(ml_dtypes.bfloat16)
    low = (matrix - high.astype(np.float64)).astype(ml_dtypes.bfloat16)
    return high, low


def factors(rows, cols, time_step, rate, rank):
    basis_rows = cosine_basis(rows).astype(np.float64)
    basis_cols = cosine_basis(cols).astype(np.float64)
    spectrum = eigen_values(rows).astype(np.float64)[:, None] + eigen_values(cols).astype(np.float64)[None, :]
    factor = 1.0 / (1.0 - time_step * rate * spectrum)
    left, sizes, right = np.linalg.svd(factor)
    if rank is None:
        rank = 1
        while np.abs(factor - (left[:, :rank] * sizes[:rank]) @ right[:rank]).max() > 2.0**-26:
            rank += 1
        return rank
    left = left[:, :rank] * np.sqrt(sizes[:rank])
    right = right[:rank].T * np.sqrt(sizes[:rank])
    scale = left[0, 0]
    left[:, 0] /= scale
    right[:, 0] *= scale
    firsts = [basis_rows @ np.diag(left[:, k]) @ basis_rows.T for k in range(rank)]
    seconds = [basis_cols @ np.diag(right[:, k]) @ basis_cols.T for k in range(rank)]
    firsts[0] = firsts[0] - np.eye(rows)
    seconds[0] = seconds[0] - np.eye(cols)
    return firsts, seconds


@functools.lru_cache(maxsize=None)
def solve_tables(rows, cols, time_step):
    rank = max(factors(rows, cols, time_step, rate, None) for rate in diffusion)
    rank = max(rank, 2)
    species = [factors(rows, cols, time_step, rate, rank) for rate in diffusion]
    short = rank == 2
    rights, lefts = [], []
    for firsts, seconds in species:
        highs, lows = [], []
        for second in seconds:
            high, low = halves(second)
            highs += [high] * 2
            lows += [low] * 2
        high = np.concatenate(highs, 1)
        low = np.concatenate(lows, 1)
        rights.append(np.concatenate([high, high, low], 0))
        pairs = [halves(first) for first in firsts]
        highs = [high for high, low in pairs]
        lows = [low for high, low in pairs]
        if short:
            lefts.append(np.concatenate(highs + highs[:1] + lows[:1], 1))
        else:
            lefts.append(np.concatenate(highs + highs + lows, 1))
    return np.stack(rights), np.stack(lefts)


def kernel(devices, sizes, *refs):
    sources = refs[:INPUTS]
    packed_ref = refs[INPUTS]
    held = refs[INPUTS + 1 : 2 * INPUTS + 1]
    (initial_ref, guess_ref, feed_ref, kill_ref) = held[:4]
    table_refs = (held[4:6], held[6:8], held[8:10])
    (rates, b_buf, s_buf, r_buf, p_buf, e_buf, u_buf, prior_buf, end_buf, mine_buf, b_out, r_out, p_out, zero_buf) = refs[
        2 * INPUTS + 1 : 2 * INPUTS + 15
    ]
    (
        send_b, recv_b, send_s, recv_s, send_e, recv_e, send_u, send_w,
        recv_u, recv_v, recv_w, send_r, recv_r, send_p, recv_p, load,
    ) = refs[2 * INPUTS + 15 :]
    rows, cols = sizes
    groups = devices // GROUP
    half = GROUP // 2
    me = lax.axis_index("tm")
    group = me // GROUP
    member = me % GROUP
    base = group * GROUP
    slot = (member + 2) % GROUP
    opens = group == 0
    wraps = member >= GROUP - 2
    forwards = jnp.logical_and(wraps, group < groups - 1)
    leads = jnp.logical_and(member >= half, member % 2 == 1)
    relaxes = member == jnp.where(opens, 0, half - 1)
    listeners = LEADERS * (groups - 1 - group)

    loads = [pltpu.make_async_copy(source, target, load.at[i]) for i, (source, target) in enumerate(zip(sources, held))]
    for copy in loads:
        copy.start()

    def leader(i):
        return GROUP - 1 - 2 * i

    barrier = pltpu.get_barrier_semaphore()

    def greet(other):
        pl.semaphore_signal(barrier, inc=1, device_id=(other,), device_id_type=MESH)

    def greet_peer(i, carry):
        greet(base + (member + 1 + i) % GROUP)
        return carry

    def relaxer(other):
        return other * GROUP + jnp.where(other == 0, 0, half - 1)

    def greet_relaxer(other, carry):
        greet(relaxer(other))
        return carry

    @pl.when(leads)
    def _():
        lax.fori_loop(0, group, greet_relaxer, 0)

    @pl.when(jnp.logical_and(jnp.logical_or(leads, relaxes), group > 0))
    def _():
        greet(base - 2)
        greet(base - 1)

    @pl.when(jnp.logical_and(group > 0, member <= 1))
    def _():
        greet(me - 2)

    @pl.when(jnp.logical_and(group > 0, member == 0))
    def _():
        greet(me - 1)

    lax.fori_loop(0, GROUP - 1, greet_peer, 0)

    def await_barrier():
        crossing = jnp.where(forwards, LEADERS + member - (GROUP - 4), 0)
        pl.semaphore_wait(barrier, GROUP - 1 + crossing + jnp.where(relaxes, listeners, 0))

    def remote(source, target, send, recv, other):
        return pltpu.make_async_remote_copy(
            src_ref=source, dst_ref=target, send_sem=send, recv_sem=recv,
            device_id=(other,), device_id_type=MESH,
        )

    left_half = lax.broadcasted_iota(jnp.int32, (rows, 2 * cols), 1) < cols
    fine_step = interval_time / STEPS_DEV
    steps = (fine_step, interval_time, interval_time * GROUP)
    for copy in loads[:6]:
        copy.wait()
    feed = jnp.concatenate([feed_ref[...]] * 2, axis=1)
    kill = jnp.concatenate([kill_ref[...]] * 2, axis=1)
    for level, step in enumerate(steps):
        rates[3 * level] = 1.0 - step * feed
        rates[3 * level + 1] = step * feed
        rates[3 * level + 2] = 1.0 - step * (feed + kill)

    def double(value):
        return jnp.concatenate([value, value], axis=1)

    def join(state):
        return jnp.where(left_half, state[0], state[1])

    def spread(value):
        turned = pltpu.roll(value, cols, 1)
        return jnp.where(left_half, value, turned), jnp.where(left_half, turned, value)

    def plus(state, other):
        return state[0] + other[0], state[1] + other[1]

    def minus(state, other):
        return state[0] - other[0], state[1] - other[1]

    def split(value):
        high = value.astype(jnp.bfloat16)
        low = (value - high.astype(jnp.float32)).astype(jnp.bfloat16)
        return high, low

    def dot(first, second):
        return jnp.dot(first, second, preferred_element_type=jnp.float32)

    def stacked_rows(values):
        return jnp.concatenate(values, 0) if len(values) > 1 else values[0]

    def spectral(level, kind, main):
        count = main.shape[0] // rows
        high = main.astype(jnp.bfloat16)
        wide = high.astype(jnp.float32)
        mixed = jnp.where(stacked_rows([left_half] * count), wide, main - wide).astype(jnp.bfloat16)
        return dot(jnp.concatenate([mixed, high[:, :cols]], 1), table_refs[level][0][kind])

    def gather_terms(main, product):
        count = main.shape[0] // rows
        terms = product.shape[1] // (2 * cols)
        parts = [product[:, 2 * cols * k : 2 * cols * (k + 1)] for k in range(terms)]
        first = main + parts[0]
        parts[0] = first
        columns = []
        for n in range(count):
            pieces = [part[rows * n : rows * (n + 1)] for part in parts]
            if terms == 2:
                first_high, first_low = split(pieces[0])
                stack = [first_high, pieces[1].astype(jnp.bfloat16), first_low, first_high]
            else:
                pairs = [split(piece) for piece in pieces]
                stack = [a for a, b in pairs] + [b for a, b in pairs] + [a for a, b in pairs]
            columns.append(jnp.concatenate(stack, 0))
        return first, jnp.concatenate(columns, 1) if count > 1 else columns[0]

    def react(level, states):
        step = steps[level]
        reacted = ([], [])
        for substrate, catalyst in states:
            uptake = step * (substrate * (catalyst * catalyst))
            reacted[0].append(rates[3 * level] * substrate + rates[3 * level + 1] - uptake)
            reacted[1].append(rates[3 * level + 2] * catalyst + uptake)
        return [stacked_rows(values) for values in reacted]

    def evolve_all(*items):
        mains = [(level, kind, main) for level, states in items for kind, main in enumerate(react(level, states))]
        products = [spectral(level, kind, main) for level, kind, main in mains]
        gathered = [gather_terms(main, product) for (_, _, main), product in zip(mains, products)]
        smalls = [dot(table_refs[level][1][kind], stack) for (level, kind, _), (_, stack) in zip(mains, gathered)]
        solved = [
            [first[rows * n : rows * (n + 1)] + small[:, 2 * cols * n : 2 * cols * (n + 1)] for n in range(first.shape[0] // rows)]
            for (first, stack), small in zip(gathered, smalls)
        ]
        return [list(zip(*solved[2 * i : 2 * i + 2])) for i in range(len(items))]

    def evolve(level, *states):
        return evolve_all((level, states))[0]

    start = double(initial_ref[0]), double(initial_ref[1])
    own = double(guess_ref[0, 0]), double(guess_ref[0, 1])

    def fine_turn(unused, states):
        return tuple(evolve(0, *states))

    def prepare(*states):
        relaxed = lax.fori_loop(0, STEPS_DEV, fine_turn, states, unroll=True)
        r_out[...] = join(relaxed[0])
        for copy in loads[6:]:
            copy.wait()
        arrived, (image,) = evolve_all((0, relaxed), (1, relaxed[:1]))
        arrived = lax.fori_loop(1, STEPS_DEV, fine_turn, tuple(arrived), unroll=True)
        p_out[...] = join(arrived[0])
        b_out[...] = join(minus(arrived[0], image))
        if len(states) > 1:
            zero_buf[0] = join(relaxed[1])
            zero_buf[1] = join(arrived[1])

    pairs = jnp.logical_and(opens, jnp.logical_or(member >= half, member <= 1))

    @pl.when(pairs)
    def _():
        prepare(own, start)

    @pl.when(jnp.logical_not(pairs))
    def _():
        prepare(own)

    r_copy = remote(r_out, r_buf, send_r, recv_r, me + 1)
    p_copy = remote(p_out, p_buf, send_p, recv_p, me + 2)
    reach = base + jnp.where(wraps, GROUP, 0)

    def b_copy(i, other):
        return remote(b_out, b_buf.at[slot], send_b.at[i], recv_b.at[slot], other)

    reached_relaxer = relaxer(group + jnp.where(wraps, 1, 0))
    s_copy = remote(r_out, s_buf, send_s, recv_s, reached_relaxer)

    sends = jnp.logical_or(forwards, jnp.logical_not(wraps))
    defers = jnp.logical_and(opens, jnp.logical_and(member >= half + LEADERS, jnp.logical_not(wraps)))

    def over_relaxer(act):
        @pl.when(jnp.logical_and(forwards, member == GROUP - 2))
        def _():
            act(s_copy)

        @pl.when(jnp.logical_and(sends, me != reached_relaxer))
        def _():
            act(b_copy(LEADERS, reached_relaxer))

    def over_leaders(act, where):
        for i in range(LEADERS):

            @pl.when(jnp.logical_and(jnp.logical_and(sends, where), slot <= leader(i)))
            def _():
                act(b_copy(i, reach + leader(i)))

    await_barrier()

    @pl.when(jnp.logical_not(defers))
    def _():
        over_relaxer(lambda copy: copy.start())

    over_leaders(lambda copy: copy.start(), me >= 0)

    @pl.when(defers)
    def _():
        over_leaders(lambda copy: copy.wait_send(), me >= 0)
        over_relaxer(lambda copy: copy.start())

    @pl.when(me + 2 < devices)
    def _():
        p_copy.start()

    @pl.when(me + 1 < devices)
    def _():
        r_copy.start()

    @pl.when(relaxes)
    def _():
        pltpu.make_async_copy(b_out, b_buf.at[slot], recv_b.at[slot]).start()

    @pl.when(me == 0)
    def _():
        r_buf[...] = zero_buf[0]
        p_buf[...] = zero_buf[0]

    @pl.when(me == 1)
    def _():
        p_buf[...] = zero_buf[1]

    below = member - half - 1
    clients = (below, below + 1, member - 1)

    def u_copy(j):
        return remote(u_buf.at[clients[j]], prior_buf, send_u.at[j], recv_u, base + clients[j])

    def v_copy(j):
        return remote(u_buf.at[clients[j] + 1], end_buf, send_u.at[3 + j], recv_v, base + clients[j])

    def w_copy(j):
        return remote(mine_buf, mine_buf, send_w.at[j], recv_w, base + clients[j])

    def e_copy(i):
        later = (group + 1 + i // LEADERS) * GROUP + GROUP - 1 - 2 * (i % LEADERS)
        mate = GROUP - 1 - (i - listeners)
        mate = base + mate - jnp.where(mate <= member, 1, 0)
        other = jnp.where(i < listeners, later, mate)
        return remote(e_buf.at[group], e_buf.at[group], send_e.at[i], recv_e.at[group], other)

    def start_w():
        for j in range(3):
            w_copy(j).start()

    def await_b(k):
        remote(b_out, b_buf.at[k], send_b.at[0], recv_b.at[k], me).wait_recv()

    def await_e(other):
        remote(e_buf.at[other], e_buf.at[other], send_e.at[0], recv_e.at[other], me).wait_recv()

    def relax_turn(k, state):
        await_b(k)
        (state,) = evolve(1, state)
        return plus(state, spread(b_buf[k]))

    def coarse_turn(other, before):
        await_e(other)
        (image,) = evolve(2, before)
        return plus(image, spread(e_buf[other]))

    def serve(reached):
        @pl.when(reached == below)
        def _():
            u_copy(0).start()

        @pl.when(reached == below + 1)
        def _():
            u_copy(1).start()
            v_copy(0).start()

        @pl.when(reached == below + 2)
        def _():
            v_copy(1).start()

    def relax_pair(n, state):
        return relax_turn(2 * n + 1, relax_turn(2 * n, state))

    def replay_turn(k, state):
        state = relax_turn(k, state)
        u_buf[k + 1] = join(state)
        return state

    def replay_pair(n, state):
        return replay_turn(2 * n + 1, replay_turn(2 * n, state))

    def serving_turn(k, state):
        state = replay_turn(k, state)
        serve(k + 1)
        return state

    def pick(first, second):
        return tuple(jnp.where(opens, a, b) for a, b in zip(first, second))

    @pl.when(relaxes)
    def _():
        @pl.when(opens)
        def _():
            s_buf[...] = join(start)

        @pl.when(group > 0)
        def _():
            remote(r_out, s_buf, send_s, recv_s, me).wait_recv()

        group_start = spread(s_buf[...])
        (coarse_start,) = evolve(2, group_start)
        opening = pick(spread(zero_buf[1]), group_start)
        closing = lax.fori_loop(jnp.where(opens, 1, 0), GROUP // 2, relax_pair, opening)
        e_buf[group] = join(minus(closing, coarse_start))

        def start_e(i, carry):
            e_copy(i).start()
            return carry

        lax.fori_loop(0, listeners + GROUP - 1, start_e, 0)

    @pl.when(leads)
    def _():
        (coarse_initial,) = evolve(2, start)

        @pl.when(opens)
        def _():
            u_buf[0] = join(start)

        @pl.when(group > 0)
        def _():
            await_e(0)
            first_coarse = plus(coarse_initial, spread(e_buf[0]))
            u_buf[0] = join(lax.fori_loop(1, group, coarse_turn, first_coarse))

        earlier = spread(u_buf[0])
        serve(0)

        @pl.when(group > 0)
        def _():
            await_b(0)
            await_b(1)

        (state,), (image,) = evolve_all((1, (earlier,)), (2, (earlier,)))
        state = pick(spread(zero_buf[0]), plus(state, spread(b_buf[0])))
        u_buf[1] = join(state)
        serve(1)
        (state,) = evolve(1, state)
        state = pick(spread(zero_buf[1]), plus(state, spread(b_buf[1])))
        u_buf[2] = join(state)
        serve(2)
        mine_buf[...] = join(image)
        start_w()
        state = lax.fori_loop(1, below // 2, replay_pair, state)

        @pl.when(below > 2)
        def _():
            serve(below)

        state = lax.fori_loop(jnp.maximum(below, 2), below + 2, serving_turn, state)
        for i in range(GROUP // 4 - 1):
            state = replay_pair(below // 2 + 1 + i, state)
        u_copy(2).start()
        replay_turn(member - 1, state)
        v_copy(2).start()
        await_b(member)
        prior_buf[...] = u_buf[member]

    follows = jnp.logical_not(leads)

    @pl.when(me >= 1)
    def _():
        remote(r_out, r_buf, send_r, recv_r, me).wait_recv()

    @pl.when(me >= 2)
    def _():
        remote(p_out, p_buf, send_p, recv_p, me).wait_recv()

    packed_ref[STEPS_DEV] = p_buf[...] - r_buf[...]

    @pl.when(follows)
    def _():
        remote(u_buf.at[0], prior_buf, send_u.at[0], recv_u, me).wait_recv()

    prior = spread(prior_buf[...])
    (point,), (ending,) = evolve_all((0, (prior,)), (1, (prior,)))
    ending = join(ending) + b_buf[member]
    packed_ref[0] = join(point)
    for i in range(1, STEPS_DEV - 1):
        (point,) = evolve(0, point)
        packed_ref[i] = join(point)

    @pl.when(follows)
    def _():
        remote(u_buf.at[0], end_buf, send_u.at[0], recv_v, me).wait_recv()
        remote(mine_buf, mine_buf, send_w.at[0], recv_w, me).wait_recv()

    @pl.when(jnp.logical_not(relaxes))
    def _():
        await_e(group)

    @pl.when(leads)
    def _():
        end_buf[...] = ending

    ending = end_buf[...]
    mine = mine_buf[...] + e_buf[group]
    last = member == GROUP - 1
    packed_ref[STEPS_DEV - 1] = jnp.where(last, mine, ending)
    packed_ref[STEPS_DEV + 1] = mine
    packed_ref[STEPS_DEV + 2] = jnp.where(last, ending - mine, 0.0)
    over_relaxer(lambda copy: copy.wait_send())
    over_leaders(lambda copy: copy.wait_send(), jnp.logical_not(defers))

    @pl.when(me + 2 < devices)
    def _():
        p_copy.wait_send()

    @pl.when(me + 1 < devices)
    def _():
        r_copy.wait_send()

    @pl.when(leads)
    def _():
        for j in range(3):
            u_copy(j).wait_send()
            v_copy(j).wait_send()
            w_copy(j).wait_send()

    @pl.when(relaxes)
    def _():
        def end_e(i, carry):
            e_copy(i).wait_send()
            return carry

        lax.fori_loop(0, listeners + GROUP - 1, end_e, 0)


def unpack(packed_ref, traj_ref, resid_ref, coarse_ref, defect_ref):
    cols = packed_ref.shape[2] // 2
    places = [(traj_ref, i) for i in range(STEPS_DEV)] + [(resid_ref, 0), (coarse_ref, 0), (defect_ref, 0)]
    for i, (ref, index) in enumerate(places):
        ref[index, 0] = packed_ref[i, :, :cols]
        ref[index, 1] = packed_ref[i, :, cols:]


assert 4 * LEADERS == GROUP


def shards(devices, initial, coarse_guess, feed_rate, kill_rate):
    rows, cols = initial.shape[1:]
    groups = devices // GROUP
    steps = (interval_time / STEPS_DEV, interval_time, interval_time * GROUP)
    tables = []
    for step in steps:
        tables += [jnp.asarray(table) for table in solve_tables(rows, cols, step)]
    state = (rows, 2 * cols)
    block = (1,) + initial.shape
    dma = pltpu.SemaphoreType.DMA
    whole = pl.BlockSpec(memory_space=pltpu.VMEM)
    remain = pl.BlockSpec(memory_space=pltpu.HBM)
    inputs = (initial, coarse_guess, feed_rate, kill_rate, *tables)
    buffer = pltpu.VMEM(state, jnp.float32)
    packed = pl.pallas_call(
        functools.partial(kernel, devices, (rows, cols)),
        out_shape=jax.ShapeDtypeStruct((PIECES,) + state, jnp.float32),
        in_specs=[remain] * INPUTS,
        out_specs=whole,
        scratch_shapes=[pltpu.VMEM(each.shape, each.dtype) for each in inputs]
        + [
            pltpu.VMEM((9,) + state, jnp.float32),
            pltpu.VMEM((GROUP,) + state, jnp.float32),
            buffer,
            buffer,
            buffer,
            pltpu.VMEM((groups,) + state, jnp.float32),
            pltpu.VMEM((GROUP + 1,) + state, jnp.float32),
        ]
        + [buffer] * 6
        + [pltpu.VMEM((2,) + state, jnp.float32)]
        + [dma((LEADERS + 1,)), dma((GROUP,)), dma, dma]
        + [dma((LEADERS * groups + GROUP,)), dma((groups,)), dma((6,)), dma((3,))]
        + [dma] * 7
        + [dma((INPUTS,))],
        compiler_params=pltpu.CompilerParams(
            collective_id=0, has_side_effects=True, vmem_limit_bytes=VMEM_GRANT
        ),
    )(*[pltpu.with_memory_space_constraint(each, pltpu.HBM) for each in inputs])
    return pl.pallas_call(
        unpack,
        out_shape=[
            jax.ShapeDtypeStruct((STEPS_DEV,) + initial.shape, jnp.float32),
            jax.ShapeDtypeStruct(block, jnp.float32),
            jax.ShapeDtypeStruct(block, jnp.float32),
            jax.ShapeDtypeStruct(block, jnp.float32),
        ],
        in_specs=[whole],
        out_specs=[whole] * 4,
        compiler_params=pltpu.CompilerParams(vmem_limit_bytes=VMEM_GRANT),
    )(pltpu.with_memory_space_constraint(packed, pltpu.VMEM))


def solution(mesh):
    spread = P("tm", None, None, None)
    return jax.shard_map(
        functools.partial(shards, mesh.shape["tm"]),
        mesh=mesh,
        in_specs=(P(), spread, P(), P()),
        out_specs=(spread, spread, spread, spread),
        check_vma=False,
    )
```

```python
import functools

import jax
import jax.numpy as jnp
import ml_dtypes
import numpy as np
from jax import lax
from jax.experimental import pallas as pl
from jax.experimental.pallas import tpu as pltpu
from jax.sharding import PartitionSpec as P

STEPS_DEV = 4
GROUP = 16
INPUTS = 10
LEADERS = 4
PIECES = STEPS_DEV + 3
VMEM_GRANT = 16 * 2**20

diffusion = (0.2, 0.1)
interval_time = 0.03125
MESH = pl.DeviceIdType.MESH
single = np.float32


def cosine_basis(length):
    positions = np.arange(length, dtype=single)
    angles = single(np.pi) * (positions[:, None] + single(0.5)) * positions[None, :] / single(length)
    weight = np.where(positions == 0, np.sqrt(single(1.0 / length)), np.sqrt(single(2.0 / length)))
    return (np.cos(angles) * weight[None, :].astype(single)).astype(single)


def eigen_values(length):
    positions = np.arange(length, dtype=single)
    waves = np.sin(single(np.pi) * positions / single(2.0 * length))
    return (single(-4.0) * waves * waves).astype(single)


def halves(matrix):
    high = matrix.astype(ml_dtypes.bfloat16)
    low = (matrix - high.astype(np.float64)).astype(ml_dtypes.bfloat16)
    return high, low


def factors(rows, cols, time_step, rate, rank):
    basis_rows = cosine_basis(rows).astype(np.float64)
    basis_cols = cosine_basis(cols).astype(np.float64)
    spectrum = eigen_values(rows).astype(np.float64)[:, None] + eigen_values(cols).astype(np.float64)[None, :]
    factor = 1.0 / (1.0 - time_step * rate * spectrum)
    left, sizes, right = np.linalg.svd(factor)
    if rank is None:
        rank = 1
        while np.abs(factor - (left[:, :rank] * sizes[:rank]) @ right[:rank]).max() > 2.0**-26:
            rank += 1
        return rank
    left = left[:, :rank] * np.sqrt(sizes[:rank])
    right = right[:rank].T * np.sqrt(sizes[:rank])
    scale = left[0, 0]
    left[:, 0] /= scale
    right[:, 0] *= scale
    firsts = [basis_rows @ np.diag(left[:, k]) @ basis_rows.T for k in range(rank)]
    seconds = [basis_cols @ np.diag(right[:, k]) @ basis_cols.T for k in range(rank)]
    firsts[0] = firsts[0] - np.eye(rows)
    seconds[0] = seconds[0] - np.eye(cols)
    return firsts, seconds


@functools.lru_cache(maxsize=None)
def solve_tables(rows, cols, time_step):
    rank = max(factors(rows, cols, time_step, rate, None) for rate in diffusion)
    rank = max(rank, 2)
    species = [factors(rows, cols, time_step, rate, rank) for rate in diffusion]
    short = rank == 2
    rights, lefts = [], []
    for firsts, seconds in species:
        highs, lows = [], []
        for second in seconds:
            high, low = halves(second)
            highs += [high] * 2
            lows += [low] * 2
        high = np.concatenate(highs, 1)
        low = np.concatenate(lows, 1)
        rights.append(np.concatenate([high, high, low], 0))
        pairs = [halves(first) for first in firsts]
        highs = [high for high, low in pairs]
        lows = [low for high, low in pairs]
        if short:
            lefts.append(np.concatenate(highs + highs[:1] + lows[:1], 1))
        else:
            lefts.append(np.concatenate(highs + highs + lows, 1))
    return np.stack(rights), np.stack(lefts)


def kernel(devices, sizes, *refs):
    sources = refs[:INPUTS]
    packed_ref = refs[INPUTS]
    held = refs[INPUTS + 1 : 2 * INPUTS + 1]
    (initial_ref, guess_ref, feed_ref, kill_ref) = held[:4]
    table_refs = (held[4:6], held[6:8], held[8:10])
    (rates, b_buf, s_buf, r_buf, p_buf, e_buf, u_buf, prior_buf, end_buf, mine_buf, b_out, r_out, p_out, zero_buf, own_buf, tail_buf) = refs[
        2 * INPUTS + 1 : 2 * INPUTS + 17
    ]
    (
        send_b, recv_b, send_s, recv_s, send_e, recv_e, send_u, send_w,
        recv_u, recv_v, recv_w, send_r, recv_r, send_p, recv_p, load, send_own, recv_own,
    ) = refs[2 * INPUTS + 17 :]
    rows, cols = sizes
    groups = devices // GROUP
    half = GROUP // 2
    me = lax.axis_index("tm")
    group = me // GROUP
    member = me % GROUP
    base = group * GROUP
    slot = (member + 2) % GROUP
    opens = group == 0
    wraps = member >= GROUP - 2
    forwards = jnp.logical_and(wraps, group < groups - 1)
    leads = jnp.logical_and(member >= half, member % 2 == 1)
    relaxes = member == jnp.where(opens, 0, half - 1)
    corrects = jnp.logical_and(relaxes, group > 0)
    serves = jnp.logical_and(leads, jnp.logical_or(opens, member < GROUP - 1))
    listeners = (LEADERS + 1) * (groups - 1 - group)

    loads = [pltpu.make_async_copy(source, target, load.at[i]) for i, (source, target) in enumerate(zip(sources, held))]
    for i in (4, 5, 1, 2, 3, 0, 6, 7, 8, 9):
        loads[i].start()

    def leader(i):
        return GROUP - 1 - 2 * i

    barrier = pltpu.get_barrier_semaphore()

    def greet(other):
        pl.semaphore_signal(barrier, inc=1, device_id=(other,), device_id_type=MESH)

    def greet_peer(i, carry):
        greet(base + (member + 1 + i) % GROUP)
        return carry

    def relaxer(other):
        return other * GROUP + jnp.where(other == 0, 0, half - 1)

    def greet_relaxer(other, carry):
        greet(relaxer(other))
        return carry

    @pl.when(jnp.logical_or(leads, relaxes))
    def _():
        lax.fori_loop(0, group, greet_relaxer, 0)

    @pl.when(jnp.logical_and(jnp.logical_or(leads, relaxes), group > 0))
    def _():
        greet(base - 2)
        greet(base - 1)

    @pl.when(jnp.logical_and(group > 0, member <= 1))
    def _():
        greet(me - 2)

    @pl.when(jnp.logical_and(group > 0, member == 0))
    def _():
        greet(me - 1)

    lax.fori_loop(0, GROUP - 1, greet_peer, 0)

    def await_barrier():
        crossing = jnp.where(forwards, LEADERS + member - (GROUP - 4), 0)
        pl.semaphore_wait(barrier, GROUP - 1 + crossing + jnp.where(relaxes, listeners, 0))

    def remote(source, target, send, recv, other):
        return pltpu.make_async_remote_copy(
            src_ref=source, dst_ref=target, send_sem=send, recv_sem=recv,
            device_id=(other,), device_id_type=MESH,
        )

    left_half = lax.broadcasted_iota(jnp.int32, (rows, 2 * cols), 1) < cols
    fine_step = interval_time / STEPS_DEV
    steps = (fine_step, interval_time, interval_time * GROUP)
    for copy in loads[:6]:
        copy.wait()
    feed = jnp.concatenate([feed_ref[...]] * 2, axis=1)
    kill = jnp.concatenate([kill_ref[...]] * 2, axis=1)
    for level, step in enumerate(steps):
        rates[3 * level] = 1.0 - step * feed
        rates[3 * level + 1] = step * feed
        rates[3 * level + 2] = 1.0 - step * (feed + kill)

    def double(value):
        return jnp.concatenate([value, value], axis=1)

    def join(state):
        return jnp.where(left_half, state[0], state[1])

    def spread(value):
        turned = pltpu.roll(value, cols, 1)
        return jnp.where(left_half, value, turned), jnp.where(left_half, turned, value)

    def plus(state, other):
        return state[0] + other[0], state[1] + other[1]

    def minus(state, other):
        return state[0] - other[0], state[1] - other[1]

    def split(value):
        high = value.astype(jnp.bfloat16)
        low = (value - high.astype(jnp.float32)).astype(jnp.bfloat16)
        return high, low

    def dot(first, second):
        return jnp.dot(first, second, preferred_element_type=jnp.float32)

    def stacked_rows(values):
        return jnp.concatenate(values, 0) if len(values) > 1 else values[0]

    def spectral(level, kind, main):
        count = main.shape[0] // rows
        high = main.astype(jnp.bfloat16)
        wide = high.astype(jnp.float32)
        mixed = jnp.where(stacked_rows([left_half] * count), wide, main - wide).astype(jnp.bfloat16)
        return dot(jnp.concatenate([mixed, high[:, :cols]], 1), table_refs[level][0][kind])

    def gather_terms(main, product):
        count = main.shape[0] // rows
        terms = product.shape[1] // (2 * cols)
        parts = [product[:, 2 * cols * k : 2 * cols * (k + 1)] for k in range(terms)]
        first = main + parts[0]
        parts[0] = first
        columns = []
        for n in range(count):
            pieces = [part[rows * n : rows * (n + 1)] for part in parts]
            if terms == 2:
                first_high, first_low = split(pieces[0])
                stack = [first_high, pieces[1].astype(jnp.bfloat16), first_low, first_high]
            else:
                pairs = [split(piece) for piece in pieces]
                stack = [a for a, b in pairs] + [b for a, b in pairs] + [a for a, b in pairs]
            columns.append(jnp.concatenate(stack, 0))
        return first, jnp.concatenate(columns, 1) if count > 1 else columns[0]

    def react(level, states):
        step = steps[level]
        reacted = ([], [])
        for substrate, catalyst in states:
            uptake = step * (substrate * (catalyst * catalyst))
            reacted[0].append(rates[3 * level] * substrate + rates[3 * level + 1] - uptake)
            reacted[1].append(rates[3 * level + 2] * catalyst + uptake)
        return [stacked_rows(values) for values in reacted]

    def evolve_all(*items):
        mains = [(level, kind, main) for level, states in items for kind, main in enumerate(react(level, states))]
        products = [spectral(level, kind, main) for level, kind, main in mains]
        gathered = [gather_terms(main, product) for (_, _, main), product in zip(mains, products)]
        smalls = [dot(table_refs[level][1][kind], stack) for (level, kind, _), (_, stack) in zip(mains, gathered)]
        solved = [
            [first[rows * n : rows * (n + 1)] + small[:, 2 * cols * n : 2 * cols * (n + 1)] for n in range(first.shape[0] // rows)]
            for (first, stack), small in zip(gathered, smalls)
        ]
        return [list(zip(*solved[2 * i : 2 * i + 2])) for i in range(len(items))]

    def evolve(level, *states):
        return evolve_all((level, states))[0]

    start = double(initial_ref[0]), double(initial_ref[1])
    own = double(guess_ref[0, 0]), double(guess_ref[0, 1])

    def fine_turn(unused, states):
        return tuple(evolve(0, *states))

    def prepare(*states):
        relaxed = lax.fori_loop(0, STEPS_DEV, fine_turn, states, unroll=True)
        r_out[...] = join(relaxed[0])
        for copy in loads[6:]:
            copy.wait()
        arrived, (image,) = evolve_all((0, relaxed), (1, relaxed[:1]))
        arrived = lax.fori_loop(1, STEPS_DEV, fine_turn, tuple(arrived), unroll=True)
        p_out[...] = join(arrived[0])
        b_out[...] = join(minus(arrived[0], image))
        if len(states) > 1:
            zero_buf[0] = join(relaxed[1])
            zero_buf[1] = join(arrived[1])

    pairs = jnp.logical_and(opens, jnp.logical_or(member >= half, member <= 1))

    @pl.when(pairs)
    def _():
        prepare(own, start)

    @pl.when(jnp.logical_not(pairs))
    def _():
        prepare(own)

    r_copy = remote(r_out, r_buf, send_r, recv_r, me + 1)
    p_copy = remote(p_out, p_buf, send_p, recv_p, me + 2)
    reach = base + jnp.where(wraps, GROUP, 0)

    def b_copy(i, other):
        return remote(b_out, b_buf.at[slot], send_b.at[i], recv_b.at[slot], other)

    reached_relaxer = relaxer(group + jnp.where(wraps, 1, 0))
    s_copy = remote(r_out, s_buf, send_s, recv_s, reached_relaxer)

    sends = jnp.logical_or(forwards, jnp.logical_not(wraps))
    defers = jnp.logical_and(opens, jnp.logical_and(member >= half + LEADERS, jnp.logical_not(wraps)))

    def over_relaxer(act):
        @pl.when(jnp.logical_and(forwards, member == GROUP - 2))
        def _():
            act(s_copy)

        @pl.when(jnp.logical_and(sends, me != reached_relaxer))
        def _():
            act(b_copy(LEADERS, reached_relaxer))

    def over_leaders(act, where):
        for i in range(LEADERS):

            @pl.when(jnp.logical_and(jnp.logical_and(sends, where), slot <= leader(i)))
            def _():
                act(b_copy(i, reach + leader(i)))

    await_barrier()

    @pl.when(jnp.logical_not(defers))
    def _():
        over_relaxer(lambda copy: copy.start())

    over_leaders(lambda copy: copy.start(), me >= 0)

    @pl.when(defers)
    def _():
        over_leaders(lambda copy: copy.wait_send(), me >= 0)
        over_relaxer(lambda copy: copy.start())

    @pl.when(me + 2 < devices)
    def _():
        p_copy.start()

    @pl.when(me + 1 < devices)
    def _():
        r_copy.start()

    @pl.when(relaxes)
    def _():
        pltpu.make_async_copy(b_out, b_buf.at[slot], recv_b.at[slot]).start()

    @pl.when(me == 0)
    def _():
        r_buf[...] = zero_buf[0]
        p_buf[...] = zero_buf[0]

    @pl.when(me == 1)
    def _():
        p_buf[...] = zero_buf[1]

    below = member - half - 1
    clients = (below, below + 1, member - 1)

    def u_copy(j):
        return remote(u_buf.at[clients[j]], prior_buf, send_u.at[j], recv_u, base + clients[j])

    def v_copy(j):
        return remote(u_buf.at[clients[j] + 1], end_buf, send_u.at[3 + j], recv_v, base + clients[j])

    def w_copy(j):
        return remote(mine_buf, mine_buf, send_w.at[j], recv_w, base + clients[j])

    def e_copy(i):
        other = (group + 1 + i // (LEADERS + 1)) * GROUP + GROUP - 1 - 2 * (i % (LEADERS + 1))
        return remote(own_buf, e_buf.at[group], send_e.at[i], recv_e.at[group], other)

    def own_copy(i):
        mate = GROUP - 1 - i
        mate = base + mate - jnp.where(mate <= member, 1, 0)
        return remote(own_buf, own_buf, send_own.at[i], recv_own, mate)

    def start_w():
        w_copy(2).start()

        @pl.when(serves)
        def _():
            w_copy(0).start()
            w_copy(1).start()

    def await_b(k):
        remote(b_out, b_buf.at[k], send_b.at[0], recv_b.at[k], me).wait_recv()

    def await_e(other):
        remote(e_buf.at[other], e_buf.at[other], send_e.at[0], recv_e.at[other], me).wait_recv()

    def relax_turn(k, state):
        await_b(k)
        (state,) = evolve(1, state)
        return plus(state, spread(b_buf[k]))

    def coarse_turn(other, before):
        await_e(other)
        (image,) = evolve(2, before)
        return plus(image, spread(e_buf[other]))

    def before_group(first):
        return lax.fori_loop(1, group, coarse_turn, first) if groups > 2 else first

    def serve(reached):
        reached = jnp.where(serves, reached, -1)

        @pl.when(reached == below)
        def _():
            u_copy(0).start()

        @pl.when(reached == below + 1)
        def _():
            u_copy(1).start()
            v_copy(0).start()

        @pl.when(reached == below + 2)
        def _():
            v_copy(1).start()

    def relax_pair(n, state):
        return relax_turn(2 * n + 1, relax_turn(2 * n, state))

    def replay_turn(k, state):
        state = relax_turn(k, state)
        u_buf[k + 1] = join(state)
        return state

    def replay_pair(n, state):
        return replay_turn(2 * n + 1, replay_turn(2 * n, state))

    def serving_turn(k, state):
        state = replay_turn(k, state)
        serve(k + 1)
        return state

    def pick(first, second):
        return tuple(jnp.where(opens, a, b) for a, b in zip(first, second))

    @pl.when(relaxes)
    def _():
        @pl.when(opens)
        def _():
            s_buf[...] = join(start)

        @pl.when(group > 0)
        def _():
            remote(r_out, s_buf, send_s, recv_s, me).wait_recv()

        group_start = spread(s_buf[...])
        (coarse_start,) = evolve(2, group_start)
        opening = pick(spread(zero_buf[1]), group_start)
        closing = lax.fori_loop(jnp.where(opens, 1, 0), 2, relax_pair, opening)
        for n in range(2, GROUP // 2):
            closing = relax_pair(n, closing)
        own_buf[...] = join(minus(closing, coarse_start))

        def start_e(i, carry):
            e_copy(i).start()
            return carry

        def start_own(i, carry):
            own_copy(i).start()
            return carry

        lax.fori_loop(0, listeners, start_e, 0)
        lax.fori_loop(0, GROUP - 1, start_own, 0)

    @pl.when(corrects)
    def _():
        (coarse_initial,) = evolve(2, start)
        await_e(0)
        earlier = before_group(plus(coarse_initial, spread(e_buf[0])))
        (state,), (image,) = evolve_all((1, (earlier,)), (2, (earlier,)))
        state = plus(state, spread(b_buf[0]))
        mine_buf[...] = join(image)
        for k in range(1, half - 1):
            (state,) = evolve(1, state)
            state = plus(state, spread(b_buf[k]))
            if k == half - 3:
                u_buf[half - 2] = join(state)
                u_copy(2).start()
                w_copy(2).start()
        u_buf[half - 1] = join(state)
        v_copy(2).start()
        tail_buf[0], tail_buf[1] = state

    @pl.when(leads)
    def _():
        (coarse_initial,) = evolve(2, start)

        @pl.when(group > 0)
        def _():
            await_b(0)
            await_b(1)
            await_e(0)

        earlier = before_group(pick(start, plus(coarse_initial, spread(e_buf[0]))))
        u_buf[0] = join(earlier)
        serve(0)

        (state,), (image,) = evolve_all((1, (earlier,)), (2, (earlier,)))
        state = pick(spread(zero_buf[0]), plus(state, spread(b_buf[0])))
        u_buf[1] = join(state)
        serve(1)
        (state,) = evolve(1, state)
        state = pick(spread(zero_buf[1]), plus(state, spread(b_buf[1])))
        u_buf[2] = join(state)
        serve(2)
        mine_buf[...] = join(image)

        @pl.when(below > 2)
        def _():
            start_w()

        state = lax.fori_loop(1, below // 2, replay_pair, state)

        @pl.when(below > 2)
        def _():
            serve(below)

        state = lax.fori_loop(jnp.maximum(below, 2), below + 2, serving_turn, state)
        @pl.when(below <= 2)
        def _():
            start_w()

        for i in range(GROUP // 4 - 1):
            state = replay_pair(below // 2 + 1 + i, state)
        u_copy(2).start()
        state = replay_turn(member - 1, state)
        tail_buf[0], tail_buf[1] = state
        v_copy(2).start()
        await_b(member)

    chains = jnp.logical_or(leads, corrects)
    follows = jnp.logical_not(chains)

    @pl.when(me >= 1)
    def _():
        remote(r_out, r_buf, send_r, recv_r, me).wait_recv()

    @pl.when(me >= 2)
    def _():
        remote(p_out, p_buf, send_p, recv_p, me).wait_recv()

    packed_ref[STEPS_DEV] = p_buf[...] - r_buf[...]

    @pl.when(follows)
    def _():
        remote(u_buf.at[0], prior_buf, send_u.at[0], recv_u, me).wait_recv()
        tail_buf[0], tail_buf[1] = spread(prior_buf[...])

    prior = tail_buf[0], tail_buf[1]
    (point,), (ending,) = evolve_all((0, (prior,)), (1, (prior,)))
    ending = join(ending) + b_buf[member]
    packed_ref[0] = join(point)
    for i in range(1, STEPS_DEV - 1):
        (point,) = evolve(0, point)
        packed_ref[i] = join(point)

    @pl.when(follows)
    def _():
        remote(u_buf.at[0], end_buf, send_u.at[0], recv_v, me).wait_recv()
        remote(mine_buf, mine_buf, send_w.at[0], recv_w, me).wait_recv()

    @pl.when(jnp.logical_not(relaxes))
    def _():
        remote(own_buf, own_buf, send_own.at[0], recv_own, me).wait_recv()

    @pl.when(chains)
    def _():
        end_buf[...] = ending

    ending = end_buf[...]
    mine = mine_buf[...] + own_buf[...]
    last = member == GROUP - 1
    packed_ref[STEPS_DEV - 1] = jnp.where(last, mine, ending)
    packed_ref[STEPS_DEV + 1] = mine
    packed_ref[STEPS_DEV + 2] = jnp.where(last, ending - mine, 0.0)
    over_relaxer(lambda copy: copy.wait_send())
    over_leaders(lambda copy: copy.wait_send(), jnp.logical_not(defers))

    @pl.when(me + 2 < devices)
    def _():
        p_copy.wait_send()

    @pl.when(me + 1 < devices)
    def _():
        r_copy.wait_send()

    def end_client(j):
        u_copy(j).wait_send()
        v_copy(j).wait_send()
        w_copy(j).wait_send()

    @pl.when(chains)
    def _():
        end_client(2)

    @pl.when(serves)
    def _():
        end_client(0)
        end_client(1)

    @pl.when(relaxes)
    def _():
        def end_e(i, carry):
            e_copy(i).wait_send()
            return carry

        def end_own(i, carry):
            own_copy(i).wait_send()
            return carry

        lax.fori_loop(0, listeners, end_e, 0)
        lax.fori_loop(0, GROUP - 1, end_own, 0)


def unpack(packed_ref, traj_ref, resid_ref, coarse_ref, defect_ref):
    cols = packed_ref.shape[2] // 2
    places = [(traj_ref, i) for i in range(STEPS_DEV)] + [(resid_ref, 0), (coarse_ref, 0), (defect_ref, 0)]
    for i, (ref, index) in enumerate(places):
        ref[index, 0] = packed_ref[i, :, :cols]
        ref[index, 1] = packed_ref[i, :, cols:]


assert 4 * LEADERS == GROUP


def shards(devices, initial, coarse_guess, feed_rate, kill_rate):
    rows, cols = initial.shape[1:]
    groups = devices // GROUP
    steps = (interval_time / STEPS_DEV, interval_time, interval_time * GROUP)
    tables = []
    for step in steps:
        tables += [jnp.asarray(table) for table in solve_tables(rows, cols, step)]
    state = (rows, 2 * cols)
    block = (1,) + initial.shape
    dma = pltpu.SemaphoreType.DMA
    whole = pl.BlockSpec(memory_space=pltpu.VMEM)
    remain = pl.BlockSpec(memory_space=pltpu.HBM)
    inputs = (initial, coarse_guess, feed_rate, kill_rate, *tables)
    buffer = pltpu.VMEM(state, jnp.float32)
    packed = pl.pallas_call(
        functools.partial(kernel, devices, (rows, cols)),
        out_shape=jax.ShapeDtypeStruct((PIECES,) + state, jnp.float32),
        in_specs=[remain] * INPUTS,
        out_specs=whole,
        scratch_shapes=[pltpu.VMEM(each.shape, each.dtype) for each in inputs]
        + [
            pltpu.VMEM((9,) + state, jnp.float32),
            pltpu.VMEM((GROUP,) + state, jnp.float32),
            buffer,
            buffer,
            buffer,
            pltpu.VMEM((groups,) + state, jnp.float32),
            pltpu.VMEM((GROUP + 1,) + state, jnp.float32),
        ]
        + [buffer] * 6
        + [pltpu.VMEM((2,) + state, jnp.float32), buffer, pltpu.VMEM((2,) + state, jnp.float32)]
        + [dma((LEADERS + 1,)), dma((GROUP,)), dma, dma]
        + [dma(((LEADERS + 1) * groups,)), dma((groups,)), dma((6,)), dma((3,))]
        + [dma] * 7
        + [dma((INPUTS,)), dma((GROUP - 1,)), dma],
        compiler_params=pltpu.CompilerParams(
            collective_id=0, has_side_effects=True, vmem_limit_bytes=VMEM_GRANT
        ),
    )(*[pltpu.with_memory_space_constraint(each, pltpu.HBM) for each in inputs])
    return pl.pallas_call(
        unpack,
        out_shape=[
            jax.ShapeDtypeStruct((STEPS_DEV,) + initial.shape, jnp.float32),
            jax.ShapeDtypeStruct(block, jnp.float32),
            jax.ShapeDtypeStruct(block, jnp.float32),
            jax.ShapeDtypeStruct(block, jnp.float32),
        ],
        in_specs=[whole],
        out_specs=[whole] * 4,
        compiler_params=pltpu.CompilerParams(vmem_limit_bytes=VMEM_GRANT),
    )(pltpu.with_memory_space_constraint(packed, pltpu.VMEM))


def solution(mesh):
    spread = P("tm", None, None, None)
    return jax.shard_map(
        functools.partial(shards, mesh.shape["tm"]),
        mesh=mesh,
        in_specs=(P(), spread, P(), P()),
        out_specs=(spread, spread, spread, spread),
        check_vma=False,
    )
```

```python
import functools

import jax
import jax.numpy as jnp
import ml_dtypes
import numpy as np
from jax import lax
from jax.experimental import pallas as pl
from jax.experimental.pallas import tpu as pltpu
from jax.sharding import PartitionSpec as P

STEPS_DEV = 4
GROUP = 16
INPUTS = 10
LEADERS = 4
PIECES = STEPS_DEV + 3
VMEM_GRANT = 16 * 2**20

diffusion = (0.2, 0.1)
interval_time = 0.03125
MESH = pl.DeviceIdType.MESH
single = np.float32


def cosine_basis(length):
    positions = np.arange(length, dtype=single)
    angles = single(np.pi) * (positions[:, None] + single(0.5)) * positions[None, :] / single(length)
    weight = np.where(positions == 0, np.sqrt(single(1.0 / length)), np.sqrt(single(2.0 / length)))
    return (np.cos(angles) * weight[None, :].astype(single)).astype(single)


def eigen_values(length):
    positions = np.arange(length, dtype=single)
    waves = np.sin(single(np.pi) * positions / single(2.0 * length))
    return (single(-4.0) * waves * waves).astype(single)


def halves(matrix):
    high = matrix.astype(ml_dtypes.bfloat16)
    low = (matrix - high.astype(np.float64)).astype(ml_dtypes.bfloat16)
    return high, low


def factors(rows, cols, time_step, rate, rank):
    basis_rows = cosine_basis(rows).astype(np.float64)
    basis_cols = cosine_basis(cols).astype(np.float64)
    spectrum = eigen_values(rows).astype(np.float64)[:, None] + eigen_values(cols).astype(np.float64)[None, :]
    factor = 1.0 / (1.0 - time_step * rate * spectrum)
    left, sizes, right = np.linalg.svd(factor)
    if rank is None:
        rank = 1
        while np.abs(factor - (left[:, :rank] * sizes[:rank]) @ right[:rank]).max() > 2.0**-26:
            rank += 1
        return rank
    left = left[:, :rank] * np.sqrt(sizes[:rank])
    right = right[:rank].T * np.sqrt(sizes[:rank])
    scale = left[0, 0]
    left[:, 0] /= scale
    right[:, 0] *= scale
    firsts = [basis_rows @ np.diag(left[:, k]) @ basis_rows.T for k in range(rank)]
    seconds = [basis_cols @ np.diag(right[:, k]) @ basis_cols.T for k in range(rank)]
    firsts[0] = firsts[0] - np.eye(rows)
    seconds[0] = seconds[0] - np.eye(cols)
    return firsts, seconds


@functools.lru_cache(maxsize=None)
def solve_tables(rows, cols, time_step):
    rank = max(factors(rows, cols, time_step, rate, None) for rate in diffusion)
    rank = max(rank, 2)
    species = [factors(rows, cols, time_step, rate, rank) for rate in diffusion]
    short = rank == 2
    rights, lefts = [], []
    for firsts, seconds in species:
        highs, lows = [], []
        for second in seconds:
            high, low = halves(second)
            highs += [high] * 2
            lows += [low] * 2
        high = np.concatenate(highs, 1)
        low = np.concatenate(lows, 1)
        rights.append(np.concatenate([high, high, low], 0))
        pairs = [halves(first) for first in firsts]
        highs = [high for high, low in pairs]
        lows = [low for high, low in pairs]
        if short:
            lefts.append(np.concatenate(highs + highs[:1] + lows[:1], 1))
        else:
            lefts.append(np.concatenate(highs + highs + lows, 1))
    return np.stack(rights), np.stack(lefts)


def kernel(devices, sizes, *refs):
    sources = refs[:INPUTS]
    packed_ref = refs[INPUTS]
    held = refs[INPUTS + 1 : 2 * INPUTS + 1]
    (initial_ref, guess_ref, feed_ref, kill_ref) = held[:4]
    table_refs = (held[4:6], held[6:8], held[8:10])
    (rates, b_buf, s_buf, r_buf, p_buf, e_buf, u_buf, prior_buf, end_buf, mine_buf, b_out, r_out, p_out, zero_buf, own_buf, tail_buf) = refs[
        2 * INPUTS + 1 : 2 * INPUTS + 17
    ]
    (
        send_b, recv_b, send_s, recv_s, send_e, recv_e, send_u, send_w,
        recv_u, recv_v, recv_w, send_r, recv_r, send_p, recv_p, load, send_own, recv_own,
    ) = refs[2 * INPUTS + 17 :]
    rows, cols = sizes
    groups = devices // GROUP
    half = GROUP // 2
    me = lax.axis_index("tm")
    group = me // GROUP
    member = me % GROUP
    base = group * GROUP
    slot = (member + 2) % GROUP
    opens = group == 0
    wraps = member >= GROUP - 2
    forwards = jnp.logical_and(wraps, group < groups - 1)
    leads = jnp.logical_and(member >= half, member % 2 == 1)
    relaxes = member == jnp.where(opens, 0, half - 1)
    corrects = jnp.logical_and(relaxes, group > 0)
    serves = jnp.logical_and(leads, jnp.logical_or(opens, member < GROUP - 1))
    listeners = (LEADERS + 1) * (groups - 1 - group)

    loads = [pltpu.make_async_copy(source, target, load.at[i]) for i, (source, target) in enumerate(zip(sources, held))]
    for i in (4, 5, 1, 2, 3, 0, 6, 7, 8, 9):
        loads[i].start()

    def leader(i):
        return GROUP - 1 - 2 * i

    barrier = pltpu.get_barrier_semaphore()

    def greet(other):
        pl.semaphore_signal(barrier, inc=1, device_id=(other,), device_id_type=MESH)

    def greet_peer(i, carry):
        greet(base + (member + 1 + i) % GROUP)
        return carry

    def relaxer(other):
        return other * GROUP + jnp.where(other == 0, 0, half - 1)

    def greet_relaxer(other, carry):
        greet(relaxer(other))
        return carry

    @pl.when(jnp.logical_or(leads, relaxes))
    def _():
        lax.fori_loop(0, group, greet_relaxer, 0)

    @pl.when(jnp.logical_and(jnp.logical_or(leads, relaxes), group > 0))
    def _():
        greet(base - 2)
        greet(base - 1)

    @pl.when(jnp.logical_and(group > 0, member <= 1))
    def _():
        greet(me - 2)

    @pl.when(jnp.logical_and(group > 0, member == 0))
    def _():
        greet(me - 1)

    lax.fori_loop(0, GROUP - 1, greet_peer, 0)

    def await_barrier():
        crossing = jnp.where(forwards, LEADERS + member - (GROUP - 4), 0)
        pl.semaphore_wait(barrier, GROUP - 1 + crossing + jnp.where(relaxes, listeners, 0))

    def remote(source, target, send, recv, other):
        return pltpu.make_async_remote_copy(
            src_ref=source, dst_ref=target, send_sem=send, recv_sem=recv,
            device_id=(other,), device_id_type=MESH,
        )

    left_half = lax.broadcasted_iota(jnp.int32, (rows, 2 * cols), 1) < cols
    fine_step = interval_time / STEPS_DEV
    steps = (fine_step, interval_time, interval_time * GROUP)
    for copy in loads[:6]:
        copy.wait()
    feed = jnp.concatenate([feed_ref[...]] * 2, axis=1)
    kill = jnp.concatenate([kill_ref[...]] * 2, axis=1)
    for level, step in enumerate(steps):
        rates[3 * level] = 1.0 - step * feed
        rates[3 * level + 1] = step * feed
        rates[3 * level + 2] = 1.0 - step * (feed + kill)

    def double(value):
        return jnp.concatenate([value, value], axis=1)

    def join(state):
        return jnp.where(left_half, state[0], state[1])

    def spread(value):
        turned = pltpu.roll(value, cols, 1)
        return jnp.where(left_half, value, turned), jnp.where(left_half, turned, value)

    def plus(state, other):
        return state[0] + other[0], state[1] + other[1]

    def minus(state, other):
        return state[0] - other[0], state[1] - other[1]

    def split(value):
        high = value.astype(jnp.bfloat16)
        low = (value - high.astype(jnp.float32)).astype(jnp.bfloat16)
        return high, low

    def dot(first, second):
        return jnp.dot(first, second, preferred_element_type=jnp.float32)

    def stacked_rows(values):
        return jnp.concatenate(values, 0) if len(values) > 1 else values[0]

    def spectral(level, kind, main):
        count = main.shape[0] // rows
        high = main.astype(jnp.bfloat16)
        wide = high.astype(jnp.float32)
        mixed = jnp.where(stacked_rows([left_half] * count), wide, main - wide).astype(jnp.bfloat16)
        return dot(jnp.concatenate([mixed, high[:, :cols]], 1), table_refs[level][0][kind])

    def gather_terms(main, product):
        count = main.shape[0] // rows
        terms = product.shape[1] // (2 * cols)
        parts = [product[:, 2 * cols * k : 2 * cols * (k + 1)] for k in range(terms)]
        first = main + parts[0]
        parts[0] = first
        columns = []
        for n in range(count):
            pieces = [part[rows * n : rows * (n + 1)] for part in parts]
            if terms == 2:
                first_high, first_low = split(pieces[0])
                stack = [first_high, pieces[1].astype(jnp.bfloat16), first_low, first_high]
            else:
                pairs = [split(piece) for piece in pieces]
                stack = [a for a, b in pairs] + [b for a, b in pairs] + [a for a, b in pairs]
            columns.append(jnp.concatenate(stack, 0))
        return first, jnp.concatenate(columns, 1) if count > 1 else columns[0]

    def react(level, states):
        step = steps[level]
        reacted = ([], [])
        for substrate, catalyst in states:
            uptake = step * (substrate * (catalyst * catalyst))
            reacted[0].append(rates[3 * level] * substrate + rates[3 * level + 1] - uptake)
            reacted[1].append(rates[3 * level + 2] * catalyst + uptake)
        return [stacked_rows(values) for values in reacted]

    def evolve_all(*items):
        mains = [(level, kind, main) for level, states in items for kind, main in enumerate(react(level, states))]
        products = [spectral(level, kind, main) for level, kind, main in mains]
        gathered = [gather_terms(main, product) for (_, _, main), product in zip(mains, products)]
        smalls = [dot(table_refs[level][1][kind], stack) for (level, kind, _), (_, stack) in zip(mains, gathered)]
        solved = [
            [first[rows * n : rows * (n + 1)] + small[:, 2 * cols * n : 2 * cols * (n + 1)] for n in range(first.shape[0] // rows)]
            for (first, stack), small in zip(gathered, smalls)
        ]
        return [list(zip(*solved[2 * i : 2 * i + 2])) for i in range(len(items))]

    def evolve(level, *states):
        return evolve_all((level, states))[0]

    start = double(initial_ref[0]), double(initial_ref[1])
    own = double(guess_ref[0, 0]), double(guess_ref[0, 1])

    def fine_turn(unused, states):
        return tuple(evolve(0, *states))

    def prepare(*states):
        relaxed = lax.fori_loop(0, STEPS_DEV, fine_turn, states, unroll=True)
        r_out[...] = join(relaxed[0])
        for copy in loads[6:]:
            copy.wait()
        arrived, (image,) = evolve_all((0, relaxed), (1, relaxed[:1]))
        arrived = lax.fori_loop(1, STEPS_DEV, fine_turn, tuple(arrived), unroll=True)
        p_out[...] = join(arrived[0])
        b_out[...] = join(minus(arrived[0], image))
        if len(states) > 1:
            zero_buf[0] = join(relaxed[1])
            zero_buf[1] = join(arrived[1])

    pairs = jnp.logical_and(opens, jnp.logical_or(member >= half, member <= 1))

    @pl.when(pairs)
    def _():
        prepare(own, start)

    @pl.when(jnp.logical_not(pairs))
    def _():
        prepare(own)

    r_copy = remote(r_out, r_buf, send_r, recv_r, me + 1)
    p_copy = remote(p_out, p_buf, send_p, recv_p, me + 2)
    reach = base + jnp.where(wraps, GROUP, 0)

    def b_copy(i, other):
        return remote(b_out, b_buf.at[slot], send_b.at[i], recv_b.at[slot], other)

    reached_relaxer = relaxer(group + jnp.where(wraps, 1, 0))
    s_copy = remote(r_out, s_buf, send_s, recv_s, reached_relaxer)

    sends = jnp.logical_or(forwards, jnp.logical_not(wraps))
    defers = jnp.logical_and(opens, jnp.logical_and(member >= half + LEADERS, jnp.logical_not(wraps)))

    def over_relaxer(act):
        @pl.when(jnp.logical_and(forwards, member == GROUP - 2))
        def _():
            act(s_copy)

        @pl.when(jnp.logical_and(sends, me != reached_relaxer))
        def _():
            act(b_copy(LEADERS, reached_relaxer))

    def over_leaders(act, where):
        for i in range(LEADERS):

            @pl.when(jnp.logical_and(jnp.logical_and(sends, where), slot <= leader(i)))
            def _():
                act(b_copy(i, reach + leader(i)))

    await_barrier()

    @pl.when(jnp.logical_not(defers))
    def _():
        over_relaxer(lambda copy: copy.start())

    over_leaders(lambda copy: copy.start(), me >= 0)

    @pl.when(defers)
    def _():
        over_leaders(lambda copy: copy.wait_send(), me >= 0)
        over_relaxer(lambda copy: copy.start())

    @pl.when(me + 2 < devices)
    def _():
        p_copy.start()

    @pl.when(me + 1 < devices)
    def _():
        r_copy.start()

    @pl.when(relaxes)
    def _():
        pltpu.make_async_copy(b_out, b_buf.at[slot], recv_b.at[slot]).start()

    @pl.when(me == 0)
    def _():
        r_buf[...] = zero_buf[0]
        p_buf[...] = zero_buf[0]

    @pl.when(me == 1)
    def _():
        p_buf[...] = zero_buf[1]

    below = member - half - 1
    clients = (below, below + 1, member - 1)

    def u_copy(j):
        return remote(u_buf.at[clients[j]], prior_buf, send_u.at[j], recv_u, base + clients[j])

    def v_copy(j):
        return remote(u_buf.at[clients[j] + 1], end_buf, send_u.at[3 + j], recv_v, base + clients[j])

    def w_copy(j):
        return remote(mine_buf, mine_buf, send_w.at[j], recv_w, base + clients[j])

    def e_copy(i):
        other = (group + 1 + i // (LEADERS + 1)) * GROUP + GROUP - 1 - 2 * (i % (LEADERS + 1))
        return remote(own_buf, e_buf.at[group], send_e.at[i], recv_e.at[group], other)

    def own_copy(i):
        mate = GROUP - 1 - i
        mate = base + mate - jnp.where(mate <= member, 1, 0)
        return remote(own_buf, own_buf, send_own.at[i], recv_own, mate)

    def start_w():
        w_copy(2).start()

        @pl.when(serves)
        def _():
            w_copy(0).start()
            w_copy(1).start()

    def await_b(k):
        remote(b_out, b_buf.at[k], send_b.at[0], recv_b.at[k], me).wait_recv()

    def await_e(other):
        remote(e_buf.at[other], e_buf.at[other], send_e.at[0], recv_e.at[other], me).wait_recv()

    def relax_turn(k, state):
        await_b(k)
        (state,) = evolve(1, state)
        return plus(state, spread(b_buf[k]))

    def coarse_turn(other, before):
        await_e(other)
        (image,) = evolve(2, before)
        return plus(image, spread(e_buf[other]))

    def before_group(first):
        return lax.fori_loop(1, group, coarse_turn, first) if groups > 2 else first

    def serve(reached):
        reached = jnp.where(serves, reached, -1)

        @pl.when(reached == below)
        def _():
            u_copy(0).start()

        @pl.when(reached == below + 1)
        def _():
            u_copy(1).start()
            v_copy(0).start()

        @pl.when(reached == below + 2)
        def _():
            v_copy(1).start()

    def relax_pair(n, state):
        return relax_turn(2 * n + 1, relax_turn(2 * n, state))

    def replay_turn(k, state):
        state = relax_turn(k, state)
        u_buf[k + 1] = join(state)
        return state

    def replay_pair(n, state):
        return replay_turn(2 * n + 1, replay_turn(2 * n, state))

    def serving_turn(k, state):
        state = replay_turn(k, state)
        serve(k + 1)
        return state

    def pick(first, second):
        return tuple(jnp.where(opens, a, b) for a, b in zip(first, second))

    @pl.when(relaxes)
    def _():
        @pl.when(opens)
        def _():
            s_buf[...] = join(start)

        @pl.when(group > 0)
        def _():
            remote(r_out, s_buf, send_s, recv_s, me).wait_recv()

        group_start = spread(s_buf[...])
        (coarse_start,) = evolve(2, group_start)
        opening = pick(spread(zero_buf[1]), group_start)
        closing = lax.fori_loop(jnp.where(opens, 1, 0), 2, relax_pair, opening)
        for n in range(2, GROUP // 2):
            closing = relax_pair(n, closing)
        own_buf[...] = join(minus(closing, coarse_start))

        def start_e(i, carry):
            e_copy(i).start()
            return carry

        def start_own(i, carry):
            own_copy(i).start()
            return carry

        lax.fori_loop(0, listeners, start_e, 0)
        lax.fori_loop(0, GROUP - 1, start_own, 0)

    @pl.when(corrects)
    def _():
        (coarse_initial,) = evolve(2, start)
        await_e(0)
        earlier = before_group(plus(coarse_initial, spread(e_buf[0])))
        (state,), (image,) = evolve_all((1, (earlier,)), (2, (earlier,)))
        state = plus(state, spread(b_buf[0]))
        mine_buf[...] = join(image)
        for k in range(1, half - 1):
            (state,) = evolve(1, state)
            state = plus(state, spread(b_buf[k]))
            if k == half - 3:
                u_buf[half - 2] = join(state)
                u_copy(2).start()
                w_copy(2).start()
        u_buf[half - 1] = join(state)
        v_copy(2).start()
        tail_buf[0], tail_buf[1] = state

    @pl.when(leads)
    def _():
        (coarse_initial,) = evolve(2, start)

        @pl.when(group > 0)
        def _():
            await_b(0)
            await_b(1)
            await_e(0)

        earlier = before_group(pick(start, plus(coarse_initial, spread(e_buf[0]))))
        u_buf[0] = join(earlier)
        @pl.when(jnp.logical_and(serves, below == 0))
        def _():
            u_copy(0).start()


        (state,), (image,) = evolve_all((1, (earlier,)), (2, (earlier,)))
        state = pick(spread(zero_buf[0]), plus(state, spread(b_buf[0])))
        u_buf[1] = join(state)

        @pl.when(jnp.logical_and(serves, below == 0))
        def _():
            u_copy(1).start()
            v_copy(0).start()

        (state,) = evolve(1, state)
        state = pick(spread(zero_buf[1]), plus(state, spread(b_buf[1])))
        u_buf[2] = join(state)

        @pl.when(below <= 2)
        def _():
            serve(2)

        mine_buf[...] = join(image)

        @pl.when(below > 2)
        def _():
            start_w()

        state = lax.fori_loop(1, below // 2, replay_pair, state)

        @pl.when(below > 2)
        def _():
            serve(below)

        state = lax.fori_loop(jnp.maximum(below, 2), below + 2, serving_turn, state)
        @pl.when(below <= 2)
        def _():
            start_w()

        for i in range(GROUP // 4 - 1):
            state = replay_pair(below // 2 + 1 + i, state)
        u_copy(2).start()
        state = replay_turn(member - 1, state)
        tail_buf[0], tail_buf[1] = state
        v_copy(2).start()
        await_b(member)

    chains = jnp.logical_or(leads, corrects)
    follows = jnp.logical_not(chains)

    @pl.when(me >= 1)
    def _():
        remote(r_out, r_buf, send_r, recv_r, me).wait_recv()

    @pl.when(me >= 2)
    def _():
        remote(p_out, p_buf, send_p, recv_p, me).wait_recv()

    packed_ref[STEPS_DEV] = p_buf[...] - r_buf[...]

    @pl.when(follows)
    def _():
        remote(u_buf.at[0], prior_buf, send_u.at[0], recv_u, me).wait_recv()
        tail_buf[0], tail_buf[1] = spread(prior_buf[...])

    prior = tail_buf[0], tail_buf[1]
    (point,), (ending,) = evolve_all((0, (prior,)), (1, (prior,)))
    ending = join(ending) + b_buf[member]
    packed_ref[0] = join(point)
    for i in range(1, STEPS_DEV - 1):
        (point,) = evolve(0, point)
        packed_ref[i] = join(point)

    @pl.when(follows)
    def _():
        remote(u_buf.at[0], end_buf, send_u.at[0], recv_v, me).wait_recv()
        remote(mine_buf, mine_buf, send_w.at[0], recv_w, me).wait_recv()

    @pl.when(jnp.logical_not(relaxes))
    def _():
        remote(own_buf, own_buf, send_own.at[0], recv_own, me).wait_recv()

    @pl.when(chains)
    def _():
        end_buf[...] = ending

    ending = end_buf[...]
    mine = mine_buf[...] + own_buf[...]
    last = member == GROUP - 1
    packed_ref[STEPS_DEV - 1] = jnp.where(last, mine, ending)
    packed_ref[STEPS_DEV + 1] = mine
    packed_ref[STEPS_DEV + 2] = jnp.where(last, ending - mine, 0.0)
    over_relaxer(lambda copy: copy.wait_send())
    over_leaders(lambda copy: copy.wait_send(), jnp.logical_not(defers))

    @pl.when(me + 2 < devices)
    def _():
        p_copy.wait_send()

    @pl.when(me + 1 < devices)
    def _():
        r_copy.wait_send()

    def end_client(j):
        u_copy(j).wait_send()
        v_copy(j).wait_send()
        w_copy(j).wait_send()

    @pl.when(chains)
    def _():
        end_client(2)

    @pl.when(serves)
    def _():
        end_client(0)
        end_client(1)

    @pl.when(relaxes)
    def _():
        def end_e(i, carry):
            e_copy(i).wait_send()
            return carry

        def end_own(i, carry):
            own_copy(i).wait_send()
            return carry

        lax.fori_loop(0, listeners, end_e, 0)
        lax.fori_loop(0, GROUP - 1, end_own, 0)


def unpack(packed_ref, traj_ref, resid_ref, coarse_ref, defect_ref):
    cols = packed_ref.shape[2] // 2
    places = [(traj_ref, i) for i in range(STEPS_DEV)] + [(resid_ref, 0), (coarse_ref, 0), (defect_ref, 0)]
    for i, (ref, index) in enumerate(places):
        ref[index, 0] = packed_ref[i, :, :cols]
        ref[index, 1] = packed_ref[i, :, cols:]


assert 4 * LEADERS == GROUP


def shards(devices, initial, coarse_guess, feed_rate, kill_rate):
    rows, cols = initial.shape[1:]
    groups = devices // GROUP
    steps = (interval_time / STEPS_DEV, interval_time, interval_time * GROUP)
    tables = []
    for step in steps:
        tables += [jnp.asarray(table) for table in solve_tables(rows, cols, step)]
    state = (rows, 2 * cols)
    block = (1,) + initial.shape
    dma = pltpu.SemaphoreType.DMA
    whole = pl.BlockSpec(memory_space=pltpu.VMEM)
    remain = pl.BlockSpec(memory_space=pltpu.HBM)
    inputs = (initial, coarse_guess, feed_rate, kill_rate, *tables)
    buffer = pltpu.VMEM(state, jnp.float32)
    packed = pl.pallas_call(
        functools.partial(kernel, devices, (rows, cols)),
        out_shape=jax.ShapeDtypeStruct((PIECES,) + state, jnp.float32),
        in_specs=[remain] * INPUTS,
        out_specs=whole,
        scratch_shapes=[pltpu.VMEM(each.shape, each.dtype) for each in inputs]
        + [
            pltpu.VMEM((9,) + state, jnp.float32),
            pltpu.VMEM((GROUP,) + state, jnp.float32),
            buffer,
            buffer,
            buffer,
            pltpu.VMEM((groups,) + state, jnp.float32),
            pltpu.VMEM((GROUP + 1,) + state, jnp.float32),
        ]
        + [buffer] * 6
        + [pltpu.VMEM((2,) + state, jnp.float32), buffer, pltpu.VMEM((2,) + state, jnp.float32)]
        + [dma((LEADERS + 1,)), dma((GROUP,)), dma, dma]
        + [dma(((LEADERS + 1) * groups,)), dma((groups,)), dma((6,)), dma((3,))]
        + [dma] * 7
        + [dma((INPUTS,)), dma((GROUP - 1,)), dma],
        compiler_params=pltpu.CompilerParams(
            collective_id=0, has_side_effects=True, vmem_limit_bytes=VMEM_GRANT
        ),
    )(*[pltpu.with_memory_space_constraint(each, pltpu.HBM) for each in inputs])
    return pl.pallas_call(
        unpack,
        out_shape=[
            jax.ShapeDtypeStruct((STEPS_DEV,) + initial.shape, jnp.float32),
            jax.ShapeDtypeStruct(block, jnp.float32),
            jax.ShapeDtypeStruct(block, jnp.float32),
            jax.ShapeDtypeStruct(block, jnp.float32),
        ],
        in_specs=[whole],
        out_specs=[whole] * 4,
        compiler_params=pltpu.CompilerParams(vmem_limit_bytes=VMEM_GRANT),
    )(pltpu.with_memory_space_constraint(packed, pltpu.VMEM))


def solution(mesh):
    spread = P("tm", None, None, None)
    return jax.shard_map(
        functools.partial(shards, mesh.shape["tm"]),
        mesh=mesh,
        in_specs=(P(), spread, P(), P()),
        out_specs=(spread, spread, spread, spread),
        check_vma=False,
    )
```

```python
import functools

import jax
import jax.numpy as jnp
import ml_dtypes
import numpy as np
from jax import lax
from jax.experimental import pallas as pl
from jax.experimental.pallas import tpu as pltpu
from jax.sharding import PartitionSpec as P

STEPS_DEV = 4
GROUP = 16
INPUTS = 10
LEADERS = 4
PIECES = STEPS_DEV + 3
VMEM_GRANT = 16 * 2**20

diffusion = (0.2, 0.1)
interval_time = 0.03125
MESH = pl.DeviceIdType.MESH
single = np.float32


def cosine_basis(length):
    positions = np.arange(length, dtype=single)
    angles = single(np.pi) * (positions[:, None] + single(0.5)) * positions[None, :] / single(length)
    weight = np.where(positions == 0, np.sqrt(single(1.0 / length)), np.sqrt(single(2.0 / length)))
    return (np.cos(angles) * weight[None, :].astype(single)).astype(single)


def eigen_values(length):
    positions = np.arange(length, dtype=single)
    waves = np.sin(single(np.pi) * positions / single(2.0 * length))
    return (single(-4.0) * waves * waves).astype(single)


def halves(matrix):
    high = matrix.astype(ml_dtypes.bfloat16)
    low = (matrix - high.astype(np.float64)).astype(ml_dtypes.bfloat16)
    return high, low


def factors(rows, cols, time_step, rate, rank):
    basis_rows = cosine_basis(rows).astype(np.float64)
    basis_cols = cosine_basis(cols).astype(np.float64)
    spectrum = eigen_values(rows).astype(np.float64)[:, None] + eigen_values(cols).astype(np.float64)[None, :]
    factor = 1.0 / (1.0 - time_step * rate * spectrum)
    left, sizes, right = np.linalg.svd(factor)
    if rank is None:
        rank = 1
        while np.abs(factor - (left[:, :rank] * sizes[:rank]) @ right[:rank]).max() > 2.0**-26:
            rank += 1
        return rank
    left = left[:, :rank] * np.sqrt(sizes[:rank])
    right = right[:rank].T * np.sqrt(sizes[:rank])
    scale = left[0, 0]
    left[:, 0] /= scale
    right[:, 0] *= scale
    firsts = [basis_rows @ np.diag(left[:, k]) @ basis_rows.T for k in range(rank)]
    seconds = [basis_cols @ np.diag(right[:, k]) @ basis_cols.T for k in range(rank)]
    firsts[0] = firsts[0] - np.eye(rows)
    seconds[0] = seconds[0] - np.eye(cols)
    return firsts, seconds


@functools.lru_cache(maxsize=None)
def solve_tables(rows, cols, time_step):
    rank = max(factors(rows, cols, time_step, rate, None) for rate in diffusion)
    rank = max(rank, 2)
    species = [factors(rows, cols, time_step, rate, rank) for rate in diffusion]
    short = rank == 2
    rights, lefts = [], []
    for firsts, seconds in species:
        highs, lows = [], []
        for second in seconds:
            high, low = halves(second)
            highs += [high] * 2
            lows += [low] * 2
        high = np.concatenate(highs, 1)
        low = np.concatenate(lows, 1)
        rights.append(np.concatenate([high, high, low], 0))
        pairs = [halves(first) for first in firsts]
        highs = [high for high, low in pairs]
        lows = [low for high, low in pairs]
        if short:
            lefts.append(np.concatenate(highs[1:] + highs[:1] + lows[:1] + highs[:1], 1))
        else:
            lefts.append(np.concatenate(highs + highs + lows, 1))
    return np.stack(rights), np.stack(lefts)


def kernel(devices, sizes, *refs):
    sources = refs[:INPUTS]
    packed_ref = refs[INPUTS]
    held = refs[INPUTS + 1 : 2 * INPUTS + 1]
    (initial_ref, guess_ref, feed_ref, kill_ref) = held[:4]
    table_refs = (held[4:6], held[6:8], held[8:10])
    (rates, b_buf, s_buf, r_buf, p_buf, e_buf, u_buf, prior_buf, end_buf, mine_buf, b_out, r_out, p_out, zero_buf, own_buf, tail_buf) = refs[
        2 * INPUTS + 1 : 2 * INPUTS + 17
    ]
    (
        send_b, recv_b, send_s, recv_s, send_e, recv_e, send_u, send_w,
        recv_u, recv_v, recv_w, send_r, recv_r, send_p, recv_p, load, send_own, recv_own,
    ) = refs[2 * INPUTS + 17 :]
    rows, cols = sizes
    groups = devices // GROUP
    half = GROUP // 2
    me = lax.axis_index("tm")
    group = me // GROUP
    member = me % GROUP
    base = group * GROUP
    slot = (member + 2) % GROUP
    opens = group == 0
    wraps = member >= GROUP - 2
    forwards = jnp.logical_and(wraps, group < groups - 1)
    leads = jnp.logical_and(member >= half, member % 2 == 1)
    relaxes = member == jnp.where(opens, 0, half - 1)
    corrects = jnp.logical_and(relaxes, group > 0)
    serves = jnp.logical_and(leads, jnp.logical_or(opens, member < GROUP - 1))
    listeners = (LEADERS + 1) * (groups - 1 - group)

    loads = [pltpu.make_async_copy(source, target, load.at[i]) for i, (source, target) in enumerate(zip(sources, held))]
    for i in (4, 5, 1, 2, 3, 0, 6, 7, 8, 9):
        loads[i].start()

    def leader(i):
        return GROUP - 1 - 2 * i

    barrier = pltpu.get_barrier_semaphore()

    def greet(other):
        pl.semaphore_signal(barrier, inc=1, device_id=(other,), device_id_type=MESH)

    def greet_peer(i, carry):
        greet(base + (member + 1 + i) % GROUP)
        return carry

    def relaxer(other):
        return other * GROUP + jnp.where(other == 0, 0, half - 1)

    def greet_relaxer(other, carry):
        greet(relaxer(other))
        return carry

    @pl.when(jnp.logical_or(leads, relaxes))
    def _():
        lax.fori_loop(0, group, greet_relaxer, 0)

    @pl.when(jnp.logical_and(jnp.logical_or(leads, relaxes), group > 0))
    def _():
        greet(base - 2)
        greet(base - 1)

    @pl.when(jnp.logical_and(group > 0, member <= 1))
    def _():
        greet(me - 2)

    @pl.when(jnp.logical_and(group > 0, member == 0))
    def _():
        greet(me - 1)

    lax.fori_loop(0, GROUP - 1, greet_peer, 0)

    def await_barrier():
        crossing = jnp.where(forwards, LEADERS + member - (GROUP - 4), 0)
        pl.semaphore_wait(barrier, GROUP - 1 + crossing + jnp.where(relaxes, listeners, 0))

    def remote(source, target, send, recv, other):
        return pltpu.make_async_remote_copy(
            src_ref=source, dst_ref=target, send_sem=send, recv_sem=recv,
            device_id=(other,), device_id_type=MESH,
        )

    left_half = lax.broadcasted_iota(jnp.int32, (rows, 2 * cols), 1) < cols
    fine_step = interval_time / STEPS_DEV
    steps = (fine_step, interval_time, interval_time * GROUP)
    for copy in loads[:6]:
        copy.wait()
    feed = jnp.concatenate([feed_ref[...]] * 2, axis=1)
    kill = jnp.concatenate([kill_ref[...]] * 2, axis=1)
    for level, step in enumerate(steps):
        rates[3 * level] = 1.0 - step * feed
        rates[3 * level + 1] = step * feed
        rates[3 * level + 2] = 1.0 - step * (feed + kill)

    def double(value):
        return jnp.concatenate([value, value], axis=1)

    def join(state):
        return jnp.where(left_half, state[0], state[1])

    def spread(value):
        turned = pltpu.roll(value, cols, 1)
        return jnp.where(left_half, value, turned), jnp.where(left_half, turned, value)

    def plus(state, other):
        return state[0] + other[0], state[1] + other[1]

    def minus(state, other):
        return state[0] - other[0], state[1] - other[1]

    def split(value):
        high = value.astype(jnp.bfloat16)
        low = (value - high.astype(jnp.float32)).astype(jnp.bfloat16)
        return high, low

    def dot(first, second):
        return jnp.dot(first, second, preferred_element_type=jnp.float32)

    def stacked_rows(values):
        return jnp.concatenate(values, 0) if len(values) > 1 else values[0]

    def spectral(level, kind, main):
        count = main.shape[0] // rows
        high = main.astype(jnp.bfloat16)
        wide = high.astype(jnp.float32)
        mixed = jnp.where(stacked_rows([left_half] * count), wide, main - wide).astype(jnp.bfloat16)
        return dot(jnp.concatenate([mixed, high[:, :cols]], 1), table_refs[level][0][kind])

    def gather_terms(main, product):
        count = main.shape[0] // rows
        terms = product.shape[1] // (2 * cols)
        parts = [product[:, 2 * cols * k : 2 * cols * (k + 1)] for k in range(terms)]
        first = main + parts[0]
        parts[0] = first
        columns = []
        for n in range(count):
            pieces = [part[rows * n : rows * (n + 1)] for part in parts]
            if terms == 2:
                first_high, first_low = split(pieces[0])
                stack = [pieces[1].astype(jnp.bfloat16), first_high, first_high, first_low]
            else:
                pairs = [split(piece) for piece in pieces]
                stack = [a for a, b in pairs] + [b for a, b in pairs] + [a for a, b in pairs]
            columns.append(jnp.concatenate(stack, 0))
        return first, jnp.concatenate(columns, 1) if count > 1 else columns[0]

    def react(level, states):
        step = steps[level]
        reacted = ([], [])
        for substrate, catalyst in states:
            uptake = step * (substrate * (catalyst * catalyst))
            reacted[0].append(rates[3 * level] * substrate + rates[3 * level + 1] - uptake)
            reacted[1].append(rates[3 * level + 2] * catalyst + uptake)
        return [stacked_rows(values) for values in reacted]

    def evolve_all(*items):
        mains = [(level, kind, main) for level, states in items for kind, main in enumerate(react(level, states))]
        products = [spectral(level, kind, main) for level, kind, main in mains]
        gathered = [gather_terms(main, product) for (_, _, main), product in zip(mains, products)]
        smalls = [dot(table_refs[level][1][kind], stack) for (level, kind, _), (_, stack) in zip(mains, gathered)]
        solved = [
            [first[rows * n : rows * (n + 1)] + small[:, 2 * cols * n : 2 * cols * (n + 1)] for n in range(first.shape[0] // rows)]
            for (first, stack), small in zip(gathered, smalls)
        ]
        return [list(zip(*solved[2 * i : 2 * i + 2])) for i in range(len(items))]

    def evolve(level, *states):
        return evolve_all((level, states))[0]

    start = double(initial_ref[0]), double(initial_ref[1])
    own = double(guess_ref[0, 0]), double(guess_ref[0, 1])

    def fine_turn(unused, states):
        return tuple(evolve(0, *states))

    def prepare(*states):
        relaxed = lax.fori_loop(0, STEPS_DEV, fine_turn, states, unroll=True)
        r_out[...] = join(relaxed[0])
        for copy in loads[6:]:
            copy.wait()
        arrived, (image,) = evolve_all((0, relaxed), (1, relaxed[:1]))
        arrived = lax.fori_loop(1, STEPS_DEV, fine_turn, tuple(arrived), unroll=True)
        p_out[...] = join(arrived[0])
        b_out[...] = join(minus(arrived[0], image))
        if len(states) > 1:
            zero_buf[0] = join(relaxed[1])
            zero_buf[1] = join(arrived[1])

    pairs = jnp.logical_and(opens, jnp.logical_or(member >= half, member <= 1))

    @pl.when(pairs)
    def _():
        prepare(own, start)

    @pl.when(jnp.logical_not(pairs))
    def _():
        prepare(own)

    r_copy = remote(r_out, r_buf, send_r, recv_r, me + 1)
    p_copy = remote(p_out, p_buf, send_p, recv_p, me + 2)
    reach = base + jnp.where(wraps, GROUP, 0)

    def b_copy(i, other):
        return remote(b_out, b_buf.at[slot], send_b.at[i], recv_b.at[slot], other)

    reached_relaxer = relaxer(group + jnp.where(wraps, 1, 0))
    s_copy = remote(r_out, s_buf, send_s, recv_s, reached_relaxer)

    sends = jnp.logical_or(forwards, jnp.logical_not(wraps))
    defers = jnp.logical_and(opens, jnp.logical_and(member >= half + LEADERS, jnp.logical_not(wraps)))

    def over_relaxer(act):
        @pl.when(jnp.logical_and(forwards, member == GROUP - 2))
        def _():
            act(s_copy)

        @pl.when(jnp.logical_and(sends, me != reached_relaxer))
        def _():
            act(b_copy(LEADERS, reached_relaxer))

    def over_leaders(act, where):
        for i in range(LEADERS):

            @pl.when(jnp.logical_and(jnp.logical_and(sends, where), slot <= leader(i)))
            def _():
                act(b_copy(i, reach + leader(i)))

    await_barrier()

    @pl.when(jnp.logical_not(defers))
    def _():
        over_relaxer(lambda copy: copy.start())

    over_leaders(lambda copy: copy.start(), me >= 0)

    @pl.when(defers)
    def _():
        over_leaders(lambda copy: copy.wait_send(), me >= 0)
        over_relaxer(lambda copy: copy.start())

    @pl.when(me + 2 < devices)
    def _():
        p_copy.start()

    @pl.when(me + 1 < devices)
    def _():
        r_copy.start()

    @pl.when(relaxes)
    def _():
        pltpu.make_async_copy(b_out, b_buf.at[slot], recv_b.at[slot]).start()

    @pl.when(me == 0)
    def _():
        r_buf[...] = zero_buf[0]
        p_buf[...] = zero_buf[0]

    @pl.when(me == 1)
    def _():
        p_buf[...] = zero_buf[1]

    below = member - half - 1
    clients = (below, below + 1, member - 1)

    def u_copy(j):
        return remote(u_buf.at[clients[j]], prior_buf, send_u.at[j], recv_u, base + clients[j])

    def v_copy(j):
        return remote(u_buf.at[clients[j] + 1], end_buf, send_u.at[3 + j], recv_v, base + clients[j])

    def w_copy(j):
        return remote(mine_buf, mine_buf, send_w.at[j], recv_w, base + clients[j])

    def e_copy(i):
        other = (group + 1 + i // (LEADERS + 1)) * GROUP + GROUP - 1 - 2 * (i % (LEADERS + 1))
        return remote(own_buf, e_buf.at[group], send_e.at[i], recv_e.at[group], other)

    def own_copy(i):
        mate = GROUP - 1 - i
        mate = base + mate - jnp.where(mate <= member, 1, 0)
        return remote(own_buf, own_buf, send_own.at[i], recv_own, mate)

    def start_w():
        w_copy(2).start()

        @pl.when(serves)
        def _():
            w_copy(0).start()
            w_copy(1).start()

    def await_b(k):
        remote(b_out, b_buf.at[k], send_b.at[0], recv_b.at[k], me).wait_recv()

    def await_e(other):
        remote(e_buf.at[other], e_buf.at[other], send_e.at[0], recv_e.at[other], me).wait_recv()

    def relax_turn(k, state):
        await_b(k)
        (state,) = evolve(1, state)
        return plus(state, spread(b_buf[k]))

    def coarse_turn(other, before):
        await_e(other)
        (image,) = evolve(2, before)
        return plus(image, spread(e_buf[other]))

    def before_group(first):
        return lax.fori_loop(1, group, coarse_turn, first) if groups > 2 else first

    def serve(reached):
        reached = jnp.where(serves, reached, -1)

        @pl.when(reached == below)
        def _():
            u_copy(0).start()

        @pl.when(reached == below + 1)
        def _():
            u_copy(1).start()
            v_copy(0).start()

        @pl.when(reached == below + 2)
        def _():
            v_copy(1).start()

    def relax_pair(n, state):
        return relax_turn(2 * n + 1, relax_turn(2 * n, state))

    def replay_turn(k, state):
        state = relax_turn(k, state)
        u_buf[k + 1] = join(state)
        return state

    def replay_pair(n, state):
        return replay_turn(2 * n + 1, replay_turn(2 * n, state))

    def serving_turn(k, state):
        state = replay_turn(k, state)
        serve(k + 1)
        return state

    def pick(first, second):
        return tuple(jnp.where(opens, a, b) for a, b in zip(first, second))

    @pl.when(relaxes)
    def _():
        @pl.when(opens)
        def _():
            s_buf[...] = join(start)

        @pl.when(group > 0)
        def _():
            remote(r_out, s_buf, send_s, recv_s, me).wait_recv()

        group_start = spread(s_buf[...])
        (coarse_start,) = evolve(2, group_start)
        opening = pick(spread(zero_buf[1]), group_start)
        closing = lax.fori_loop(jnp.where(opens, 1, 0), 2, relax_pair, opening)
        for n in range(2, GROUP // 2):
            closing = relax_pair(n, closing)
        own_buf[...] = join(minus(closing, coarse_start))

        def start_e(i, carry):
            e_copy(i).start()
            return carry

        def start_own(i, carry):
            own_copy(i).start()
            return carry

        lax.fori_loop(0, listeners, start_e, 0)
        lax.fori_loop(0, GROUP - 1, start_own, 0)

    @pl.when(corrects)
    def _():
        (coarse_initial,) = evolve(2, start)
        await_e(0)
        earlier = before_group(plus(coarse_initial, spread(e_buf[0])))
        (state,), (image,) = evolve_all((1, (earlier,)), (2, (earlier,)))
        state = plus(state, spread(b_buf[0]))
        mine_buf[...] = join(image)
        for k in range(1, half - 1):
            (state,) = evolve(1, state)
            state = plus(state, spread(b_buf[k]))
            if k == half - 3:
                u_buf[half - 2] = join(state)
                u_copy(2).start()
                w_copy(2).start()
        u_buf[half - 1] = join(state)
        v_copy(2).start()
        tail_buf[0], tail_buf[1] = state

    @pl.when(leads)
    def _():
        (coarse_initial,) = evolve(2, start)

        @pl.when(group > 0)
        def _():
            await_b(0)
            await_b(1)
            await_e(0)

        earlier = before_group(pick(start, plus(coarse_initial, spread(e_buf[0]))))
        u_buf[0] = join(earlier)
        @pl.when(jnp.logical_and(serves, below == 0))
        def _():
            u_copy(0).start()


        (state,), (image,) = evolve_all((1, (earlier,)), (2, (earlier,)))
        state = pick(spread(zero_buf[0]), plus(state, spread(b_buf[0])))
        u_buf[1] = join(state)

        @pl.when(jnp.logical_and(serves, below == 0))
        def _():
            u_copy(1).start()
            v_copy(0).start()

        (state,) = evolve(1, state)
        state = pick(spread(zero_buf[1]), plus(state, spread(b_buf[1])))
        u_buf[2] = join(state)

        @pl.when(below <= 2)
        def _():
            serve(2)

        mine_buf[...] = join(image)

        @pl.when(below > 2)
        def _():
            start_w()

        state = lax.fori_loop(1, below // 2, replay_pair, state)

        @pl.when(below > 2)
        def _():
            serve(below)

        state = lax.fori_loop(jnp.maximum(below, 2), below + 2, serving_turn, state)
        @pl.when(below <= 2)
        def _():
            start_w()

        for i in range(GROUP // 4 - 1):
            state = replay_pair(below // 2 + 1 + i, state)
        u_copy(2).start()
        state = replay_turn(member - 1, state)
        tail_buf[0], tail_buf[1] = state
        v_copy(2).start()
        await_b(member)

    chains = jnp.logical_or(leads, corrects)
    follows = jnp.logical_not(chains)

    @pl.when(me >= 1)
    def _():
        remote(r_out, r_buf, send_r, recv_r, me).wait_recv()

    @pl.when(me >= 2)
    def _():
        remote(p_out, p_buf, send_p, recv_p, me).wait_recv()

    packed_ref[STEPS_DEV] = p_buf[...] - r_buf[...]

    @pl.when(follows)
    def _():
        remote(u_buf.at[0], prior_buf, send_u.at[0], recv_u, me).wait_recv()
        tail_buf[0], tail_buf[1] = spread(prior_buf[...])

    prior = tail_buf[0], tail_buf[1]
    (point,), (ending,) = evolve_all((0, (prior,)), (1, (prior,)))
    ending = join(ending) + b_buf[member]
    packed_ref[0] = join(point)
    for i in range(1, STEPS_DEV - 1):
        (point,) = evolve(0, point)
        packed_ref[i] = join(point)

    @pl.when(follows)
    def _():
        remote(u_buf.at[0], end_buf, send_u.at[0], recv_v, me).wait_recv()
        remote(mine_buf, mine_buf, send_w.at[0], recv_w, me).wait_recv()

    @pl.when(jnp.logical_not(relaxes))
    def _():
        remote(own_buf, own_buf, send_own.at[0], recv_own, me).wait_recv()

    @pl.when(chains)
    def _():
        end_buf[...] = ending

    ending = end_buf[...]
    mine = mine_buf[...] + own_buf[...]
    last = member == GROUP - 1
    packed_ref[STEPS_DEV - 1] = jnp.where(last, mine, ending)
    packed_ref[STEPS_DEV + 1] = mine
    packed_ref[STEPS_DEV + 2] = jnp.where(last, ending - mine, 0.0)
    over_relaxer(lambda copy: copy.wait_send())
    over_leaders(lambda copy: copy.wait_send(), jnp.logical_not(defers))

    @pl.when(me + 2 < devices)
    def _():
        p_copy.wait_send()

    @pl.when(me + 1 < devices)
    def _():
        r_copy.wait_send()

    def end_client(j):
        u_copy(j).wait_send()
        v_copy(j).wait_send()
        w_copy(j).wait_send()

    @pl.when(chains)
    def _():
        end_client(2)

    @pl.when(serves)
    def _():
        end_client(0)
        end_client(1)

    @pl.when(relaxes)
    def _():
        def end_e(i, carry):
            e_copy(i).wait_send()
            return carry

        def end_own(i, carry):
            own_copy(i).wait_send()
            return carry

        lax.fori_loop(0, listeners, end_e, 0)
        lax.fori_loop(0, GROUP - 1, end_own, 0)


def unpack(packed_ref, traj_ref, resid_ref, coarse_ref, defect_ref):
    cols = packed_ref.shape[2] // 2
    places = [(traj_ref, i) for i in range(STEPS_DEV)] + [(resid_ref, 0), (coarse_ref, 0), (defect_ref, 0)]
    for i, (ref, index) in enumerate(places):
        ref[index, 0] = packed_ref[i, :, :cols]
        ref[index, 1] = packed_ref[i, :, cols:]


assert 4 * LEADERS == GROUP


def shards(devices, initial, coarse_guess, feed_rate, kill_rate):
    rows, cols = initial.shape[1:]
    groups = devices // GROUP
    steps = (interval_time / STEPS_DEV, interval_time, interval_time * GROUP)
    tables = []
    for step in steps:
        tables += [jnp.asarray(table) for table in solve_tables(rows, cols, step)]
    state = (rows, 2 * cols)
    block = (1,) + initial.shape
    dma = pltpu.SemaphoreType.DMA
    whole = pl.BlockSpec(memory_space=pltpu.VMEM)
    remain = pl.BlockSpec(memory_space=pltpu.HBM)
    inputs = (initial, coarse_guess, feed_rate, kill_rate, *tables)
    buffer = pltpu.VMEM(state, jnp.float32)
    packed = pl.pallas_call(
        functools.partial(kernel, devices, (rows, cols)),
        out_shape=jax.ShapeDtypeStruct((PIECES,) + state, jnp.float32),
        in_specs=[remain] * INPUTS,
        out_specs=whole,
        scratch_shapes=[pltpu.VMEM(each.shape, each.dtype) for each in inputs]
        + [
            pltpu.VMEM((9,) + state, jnp.float32),
            pltpu.VMEM((GROUP,) + state, jnp.float32),
            buffer,
            buffer,
            buffer,
            pltpu.VMEM((groups,) + state, jnp.float32),
            pltpu.VMEM((GROUP + 1,) + state, jnp.float32),
        ]
        + [buffer] * 6
        + [pltpu.VMEM((2,) + state, jnp.float32), buffer, pltpu.VMEM((2,) + state, jnp.float32)]
        + [dma((LEADERS + 1,)), dma((GROUP,)), dma, dma]
        + [dma(((LEADERS + 1) * groups,)), dma((groups,)), dma((6,)), dma((3,))]
        + [dma] * 7
        + [dma((INPUTS,)), dma((GROUP - 1,)), dma],
        compiler_params=pltpu.CompilerParams(
            collective_id=0, has_side_effects=True, vmem_limit_bytes=VMEM_GRANT
        ),
    )(*[pltpu.with_memory_space_constraint(each, pltpu.HBM) for each in inputs])
    return pl.pallas_call(
        unpack,
        out_shape=[
            jax.ShapeDtypeStruct((STEPS_DEV,) + initial.shape, jnp.float32),
            jax.ShapeDtypeStruct(block, jnp.float32),
            jax.ShapeDtypeStruct(block, jnp.float32),
            jax.ShapeDtypeStruct(block, jnp.float32),
        ],
        in_specs=[whole],
        out_specs=[whole] * 4,
        compiler_params=pltpu.CompilerParams(vmem_limit_bytes=VMEM_GRANT),
    )(pltpu.with_memory_space_constraint(packed, pltpu.VMEM))


def solution(mesh):
    spread = P("tm", None, None, None)
    return jax.shard_map(
        functools.partial(shards, mesh.shape["tm"]),
        mesh=mesh,
        in_specs=(P(), spread, P(), P()),
        out_specs=(spread, spread, spread, spread),
        check_vma=False,
    )
```
